128 devices in a mesh: row: 8 (over x_hi, z), col: 16 (over y, x_lo, core).
Axes of the slice: x: 4 (x_hi: 2, x_lo: 2; x = x_hi * 2 + x_lo), y: 4, z: 4, core: 2. Of those that a mesh axis runs over, the one named last changes fastest.
Arguments:
- tiles: float32 [2, 4608, 9216], P(None, 'row', 'col'), may hold values from -5 to 5
- pupils: float32 [2, 1024, 2048], P(None, 'row', 'col'), may hold values from -5 to 5
- intensity: float32 [16, 1024, 2048], P(None, 'row', 'col'), may hold values from 0.2 to 3
- offsets: int32 [8, 16, 2, 16], P('row', 'col'), may hold values from 0 to 448
Outputs:
- refocused: float32 [2, 4096, 8192], P(None, 'row', 'col')
The draws below stay inside these ranges and needn't reach their ends.
Inputs may be any that keep to these rules, and one draw needn't show every extreme that they name: `offsets`: each window lies inside the tile's spectrum.
All inputs are finite; a program needn't handle non-finite values.
Results may differ from the reference program's by a relative error of at most 0.00017.
Values sent between devices are 32-bit elements; how exact they have to be, the bound alone decides.
A program may use at most 128 MiB of HBM per device.

```python
import math
import jax
import jax.numpy as jnp
from jax import lax

TILE = 576
OVL = 64
M = 128
K = 16
STRIDE = 512
NX = 4096
NY = 8192
FRESNEL = 2048
N_ROW = 8
N_COL = 16


def set_ends(drawn, rng, low, largest):
    index_at = [jax.random.randint(jax.random.fold_in(rng, axis), (), 0, length) for axis, length in enumerate(drawn.shape)]
    longest = drawn.shape.index(max(drawn.shape))
    next_to = index_at[:longest] + [(index_at[longest] + 1) % drawn.shape[longest]] + index_at[longest + 1:]
    return drawn.at[tuple(index_at)].set(low).at[tuple(next_to)].set(largest)


def level_of(stream_key, dims, cuts, least, top_value):
    gain, own = 1.0, jax.random.fold_in(stream_key, 6)
    for dim, parts in cuts:
        heights = jnp.exp(jax.random.uniform(jax.random.fold_in(own, dim), (parts,), jnp.float32, least / len(cuts), top_value / len(cuts)))
        gain = gain * jnp.repeat(heights, dims[dim] // parts).reshape([-1 if axis == dim else 1 for axis in range(len(dims))])
    return gain


def scatter_about(key, dims, spread, reach, shards=(), held_as=jnp.bfloat16):
    loudness = level_of(key, dims, shards, -0.22, 0.18) if shards else 1.0
    entries = jax.random.normal(key, dims, jnp.float32) * spread * loudness
    return jnp.minimum(jnp.maximum(entries, -reach), reach).astype(held_as)


def setup_inputs(seed: int = 0) -> dict:
    splits = jax.random.split(jax.random.key(seed), 5)
    return {
        "tiles": scatter_about(splits[0], (2, N_ROW * TILE, N_COL * TILE), 0.7, 5.0, ((1, 8), (2, 16)), jnp.float32),
        "pupils": scatter_about(splits[1], (2, N_ROW * M, N_COL * M), 0.7, 5.0, ((1, 8), (2, 16)), jnp.float32),
        "intensity": jnp.clip(jnp.exp(math.log(3.0) - 2.7080502 * jax.random.uniform(splits[2], (K, N_ROW * M, N_COL * M), jnp.float32) ** level_of(splits[2], (K, N_ROW * M, N_COL * M), ((1, 8), (2, 16)), -0.2, 0.2)), 0.2, 3.0),
        "offsets": set_ends(jax.random.randint(splits[3], (N_ROW, N_COL, 2, K), 0, TILE - M + 1), jax.random.fold_in(splits[3], 1), 0, TILE - M).astype(jnp.int32),
    }


STEP_SIZE = 0.05
TWO_PI = 2.0 * math.pi


def propagator(rows, cols, total_rows, total_cols):
    signed_rows = jnp.where(rows < total_rows // 2, rows, rows - total_rows)
    signed_cols = jnp.where(cols < total_cols // 2, cols, cols - total_cols)
    square_rows = (signed_rows * signed_rows).astype(jnp.float32)
    square_cols = (signed_cols * signed_cols).astype(jnp.float32)
    turns_rows = square_rows * (FRESNEL / (total_rows * total_rows))
    turns_rows = turns_rows - jnp.floor(turns_rows)
    turns_cols = square_cols * (FRESNEL / (total_cols * total_cols))
    turns_cols = turns_cols - jnp.floor(turns_cols)
    angle = (-TWO_PI) * (turns_rows[:, None] + turns_cols[None, :])
    decay = jnp.exp(-2.0 * (square_rows[:, None] / (total_rows * total_rows) + square_cols[None, :] / (total_cols * total_cols)))
    return decay * jnp.cos(angle), decay * jnp.sin(angle)


def refine(item):
    estimate, lens, measured, starts = item
    spectrum = jnp.fft.fft2(estimate, norm="ortho")

    def cut(row_start, col_start):
        return lax.dynamic_slice(spectrum, (row_start, col_start), (M, M))

    crops = jax.vmap(cut)(starts[0], starts[1])
    wave = jnp.fft.ifft2(lens * crops, norm="ortho")
    excess = wave.real * wave.real + wave.imag * wave.imag - measured
    update = jnp.conj(lens) * jnp.fft.fft2(wave * excess, norm="ortho")

    def place(led, total):
        corner = (starts[0, led], starts[1, led])
        current = lax.dynamic_slice(total, corner, (M, M))
        return lax.dynamic_update_slice(total, current + update[led], corner)

    total = lax.fori_loop(0, K, place, jnp.zeros_like(spectrum))
    return jnp.fft.ifft2(spectrum - STEP_SIZE * total, norm="ortho")


def reference(tiles, pupils, intensity, offsets):
    objects = (tiles[0] + 1j * tiles[1]).reshape(N_ROW, TILE, N_COL, TILE).transpose(0, 2, 1, 3).reshape(N_ROW * N_COL, TILE, TILE)
    lenses = (pupils[0] + 1j * pupils[1]).reshape(N_ROW, M, N_COL, M).transpose(0, 2, 1, 3).reshape(N_ROW * N_COL, M, M)
    measured = intensity.reshape(K, N_ROW, M, N_COL, M).transpose(1, 3, 0, 2, 4).reshape(N_ROW * N_COL, K, M, M)
    starts = offsets.reshape(N_ROW * N_COL, 2, K)
    refined = lax.map(refine, (objects, lenses, measured, starts))
    refined = refined.reshape(N_ROW, N_COL, TILE, TILE)
    ramp = (jnp.arange(OVL, dtype=jnp.float32) + 0.5) / OVL
    prior = jnp.roll(refined, 1, axis=0)
    top = ramp[:, None] * refined[:, :, :OVL, :] + (1.0 - ramp)[:, None] * prior[:, :, STRIDE:, :]
    rowed = jnp.concatenate([top, refined[:, :, OVL:STRIDE, :]], axis=2)
    prior = jnp.roll(rowed, 1, axis=1)
    front = ramp * rowed[:, :, :, :OVL] + (1.0 - ramp) * prior[:, :, :, STRIDE:]
    stitched = jnp.concatenate([front, rowed[:, :, :, OVL:STRIDE]], axis=3)
    stitched = stitched.transpose(0, 2, 1, 3).reshape(NX, NY)
    prop_real, prop_imag = propagator(jnp.arange(NX, dtype=jnp.int32), jnp.arange(NY, dtype=jnp.int32), NX, NY)
    result = jnp.fft.ifft2(jnp.fft.fft2(stitched) * (prop_real + 1j * prop_imag))
    return jnp.stack([result.real, result.imag]).astype(jnp.float32)
```

```python
import math

import numpy as np
import ml_dtypes
import jax
import jax.numpy as jnp
from jax import lax
from jax.experimental import pallas as pl
from jax.experimental.pallas import tpu as pltpu
from jax.sharding import PartitionSpec as P

TILE = 576
PAD = 640
OVL = 64
WIN = 128
LEDS = 16
STRIDE = 512
ROWS = 4096
COLS = 8192
FRESNEL = 2048
STEP_SIZE = 0.05
RADIX = 6
SUB = TILE // RADIX
BF = jnp.bfloat16
F32 = jnp.float32
GROUP = 4


def split_np(table):
    table = np.asarray(table, np.float64)
    high = table.astype(np.float32).astype(ml_dtypes.bfloat16)
    low = (table - high.astype(np.float64)).astype(np.float32).astype(ml_dtypes.bfloat16)
    return high, low


def unit(turns):
    turns = np.asarray(turns, np.float64)
    return np.exp(2j * np.pi * (turns - np.floor(turns)))


def right_block(table):
    return np.block([[table.real, table.imag], [-table.imag, table.real]])


def left_block(table):
    return np.block([[table.real, -table.imag], [table.imag, table.real]])


def dft_np(length, sign):
    index = np.arange(length)
    return unit(sign * (index[:, None] * index[None, :] % length) / length)


def axis_filter(length):
    freq = np.arange(length)
    signed = np.where(freq < length // 2, freq, freq - length).astype(np.float64)
    turns = signed * signed * (FRESNEL / (length * length))
    return np.exp(-2.0 * signed * signed / (length * length)) * unit(-turns) / length


def split(value):
    high = value.astype(BF)
    low = (value - high.astype(F32)).astype(BF)
    return high, low


def mm(left, right):
    return jnp.dot(left, right, preferred_element_type=F32)


def mm3(left, right):
    return mm(left[0], right[0]) + (mm(left[1], right[0]) + mm(left[0], right[1]))


def mm_nt(left, right):
    return lax.dot_general(left, right, (((1,), (1,)), ((), ())), preferred_element_type=F32)


def cmul(ar, ai, br, bi):
    return ar * br - ai * bi, ar * bi + ai * br


def cscale(value, factor):
    re, im = value
    fr, fi = float(factor.real), float(factor.imag)
    near = 1e-12
    if abs(fi) < near:
        if abs(fr - 1) < near:
            return re, im
        if abs(fr + 1) < near:
            return -re, -im
    if abs(fr) < near:
        if abs(fi - 1) < near:
            return -im, re
        if abs(fi + 1) < near:
            return im, -re
    if abs(abs(fr) - abs(fi)) < near:
        size = abs(fr)
        sr, si = math.copysign(1, fr), math.copysign(1, fi)
        left = re if sr > 0 else -re
        low = im if sr > 0 else -im
        new_re = left - im if si > 0 else left + im
        new_im = low + re if si > 0 else low - re
        return new_re * size, new_im * size
    return re * fr - im * fi, re * fi + im * fr


def fft_list(items, sign):
    count = len(items)
    if count == 1:
        return items
    if count == 3:
        (ar, ai), (br, bi), (cr, ci) = items
        sr, si, dr, di = br + cr, bi + ci, br - cr, bi - ci
        mr, mi = ar - 0.5 * sr, ai - 0.5 * si
        root = sign * math.sqrt(0.75)
        tr, ti = -root * di, root * dr
        return [(ar + sr, ai + si), (mr + tr, mi + ti), (mr - tr, mi - ti)]
    even = fft_list(items[0::2], sign)
    odd = fft_list(items[1::2], sign)
    half = count // 2
    first, second = [], []
    for index in range(half):
        turned = cscale(odd[index], unit(sign * index / count))
        er, ei = even[index]
        first.append((er + turned[0], ei + turned[1]))
        second.append((er - turned[0], ei - turned[1]))
    return first + second


def tile_tables():
    index = np.arange(TILE)
    low = unit(-(np.arange(24)[:, None] * index[None, :] % TILE) / TILE) / math.sqrt(TILE)
    high = unit(-(24 * np.arange(24)[:, None] * index[None, :] % TILE) / TILE)
    seeds = np.zeros((4, 24, PAD), np.float32)
    seeds[0, :, :TILE], seeds[1, :, :TILE] = low.real, low.imag
    seeds[2, :, :TILE], seeds[3, :, :TILE] = high.real, high.imag
    small = np.arange(SUB)
    forward, inverse = [], []
    for part in range(RADIX):
        turned = unit(-(part * small[:, None] + RADIX * small[:, None] * small[None, :]) / TILE)
        turned = turned / math.sqrt(TILE)
        forward.append(left_block(turned))
        inverse.append(left_block(np.conj(turned.T)))
    forward = np.stack(split_np(np.stack(forward)))
    inverse = np.stack(split_np(np.stack(inverse)))
    window = dft_np(WIN, -1) / math.sqrt(WIN)
    lanes = np.stack(
        [*split_np(right_block(np.conj(window))), *split_np(right_block(window))]
    )
    sides = np.stack(
        [*split_np(left_block(np.conj(window))), *split_np(left_block(window))]
    )
    return seeds, forward, inverse, lanes, sides


def cut(ref, part, row, first, back):
    base = pl.multiple_of((row // 8) * 8, 8)
    down = row - base
    wide = ref[part, pl.ds(base, WIN + 8), pl.ds(first, 256)]
    wide = pltpu.roll(wide, back, 1)[:, :WIN].reshape(WIN // 8 + 1, 8, WIN)
    wide = pltpu.roll(wide, lax.rem(8 - down, 8), 1)
    lane = lax.broadcasted_iota(jnp.int32, (WIN // 8, 8, WIN), 1)
    return jnp.where(lane < 8 - down, wide[:-1], wide[1:]).reshape(WIN, WIN)


def add(ref, part, row, first, shift, value):
    base = pl.multiple_of((row // 8) * 8, 8)
    down = row - base
    turned = pltpu.roll(value.reshape(WIN // 8, 8, WIN), down, 1)
    zero = jnp.zeros((1, 8, WIN), F32)
    lane = lax.broadcasted_iota(jnp.int32, (WIN // 8 + 1, 8, WIN), 1)
    upper = jnp.concatenate([zero, turned], axis=0)
    lower = jnp.concatenate([turned, zero], axis=0)
    tall = jnp.where(lane < down, upper, lower).reshape(WIN + 8, WIN)
    wide = jnp.concatenate([tall, jnp.zeros((WIN + 8, 128), F32)], axis=1)
    here = (part, pl.ds(base, WIN + 8), pl.ds(first, 256))
    ref[here] = ref[here] + pltpu.roll(wide, shift, 1)


def tile_body(
    offs, tiles, pupils, intensity, seeds, fwd, inv, lanes, sides, out,
    base, t_hi, t_lo, l_hi, l_lo, x_hi, x_lo, y, sub, spec, new, v_hi, v_lo, win_a, win_b,
):
    low_r, low_i = seeds[0], seeds[1]

    @pl.loop(0, 24)
    def _(a):
        hr = seeds[2, pl.ds(a, 1), :]
        hi = seeds[3, pl.ds(a, 1), :]
        tr, ti = cmul(low_r, low_i, hr, hi)
        start = pl.multiple_of(a * 24, 8)
        base[0, pl.ds(start, 24), :] = tr
        base[1, pl.ds(start, 24), :] = ti

    zero_tail = jnp.zeros((PAD - TILE, 2 * PAD), BF)
    t_hi[TILE:PAD, :] = zero_tail
    t_lo[TILE:PAD, :] = zero_tail
    t_hi[PAD + TILE :, :] = zero_tail
    t_lo[PAD + TILE :, :] = zero_tail

    @pl.loop(0, TILE // 96)
    def _(a):
        start = pl.multiple_of(a * 96, 16)
        ch, cl = split(base[0, pl.ds(start, 96), :])
        sh, sl = split(base[1, pl.ds(start, 96), :])
        t_hi[pl.ds(start, 96), :PAD] = ch
        t_lo[pl.ds(start, 96), :PAD] = cl
        t_hi[pl.ds(start, 96), PAD:] = sh
        t_lo[pl.ds(start, 96), PAD:] = sl
        t_hi[pl.ds(start + PAD, 96), :PAD] = -sh
        t_lo[pl.ds(start + PAD, 96), :PAD] = -sl
        t_hi[pl.ds(start + PAD, 96), PAD:] = ch
        t_lo[pl.ds(start + PAD, 96), PAD:] = cl

    x_hi[...] = jnp.zeros_like(x_hi)
    x_lo[...] = jnp.zeros_like(x_lo)

    @pl.loop(0, TILE // 96)
    def _(a):
        start = pl.multiple_of(a * 96, 16)
        for part in range(2):
            high, low = split(tiles[part, pl.ds(start, 96), :])
            x_hi[pl.ds(start, 96), part * PAD : part * PAD + TILE] = high
            x_lo[pl.ds(start, 96), part * PAD : part * PAD + TILE] = low

    @pl.loop(0, 2 * PAD // 256)
    def _(n):
        at = pl.ds(pl.multiple_of(n * 256, 256), 256)
        both = mm3((x_hi[...], x_lo[...]), (t_hi[:, at], t_lo[:, at]))
        y[2 * n] = both[:, :128]
        y[2 * n + 1] = both[:, 128:]

    @pl.loop(0, RADIX)
    def _(b):
        rows = pl.ds(b, SUB, stride=RADIX)
        parts = [
            jnp.concatenate([y[n, rows, :] for n in range(5 * part, 5 * part + 5)], axis=1)
            for part in range(2)
        ]
        sub[b] = mm3((fwd[0, b], fwd[1, b]), split(jnp.concatenate(parts, axis=0)))

    @pl.loop(0, PAD // 128)
    def _(n):
        at = pl.ds(pl.multiple_of(n * 128, 128), 128)
        for row in range(0, SUB, 8):
            items = [
                (sub[b, row : row + 8, at], sub[b, SUB + row : SUB + row + 8, at])
                for b in range(RADIX)
            ]
            done = fft_list(items, -1)
            for k in range(RADIX):
                here = slice(k * SUB + row, k * SUB + row + 8)
                spec[0, here, at] = done[k][0]
                spec[1, here, at] = done[k][1]
                new[0, here, at] = done[k][0]
                new[1, here, at] = done[k][1]

    for ref in (spec, new):
        for part in range(2):
            ref[part, TILE:, :] = jnp.zeros((8, PAD), F32)
    pr, pi = pupils[0], pupils[1]
    inv_lanes = (lanes[0], lanes[1])
    fwd_lanes = (lanes[2], lanes[3])
    inv_sides = (sides[0], sides[1])
    fwd_sides = (sides[2], sides[3])

    @pl.loop(0, LEDS // GROUP)
    def _(step):
        for j in range(GROUP):
            led = step * GROUP + j
            row, col = offs[0, led], offs[1, led]
            first = pl.multiple_of((col // 128) * 128, 128)
            shift = col - first
            back = lax.rem(256 - shift, 256)
            cr = cut(spec, 0, row, first, back)
            ci = cut(spec, 1, row, first, back)
            wr, wi = cmul(pr, pi, cr, ci)
            win_a[:WIN, j * WIN : (j + 1) * WIN] = wr
            win_a[WIN:, j * WIN : (j + 1) * WIN] = wi
        side = mm3(inv_sides, split(win_a[...]))
        for j in range(GROUP):
            win_b[j * WIN : (j + 1) * WIN, :WIN] = side[:WIN, j * WIN : (j + 1) * WIN]
            win_b[j * WIN : (j + 1) * WIN, WIN:] = side[WIN:, j * WIN : (j + 1) * WIN]
        wave = mm3(split(win_b[...]), inv_lanes)
        for j in range(GROUP):
            wr = wave[j * WIN : (j + 1) * WIN, :WIN]
            wi = wave[j * WIN : (j + 1) * WIN, WIN:]
            excess = wr * wr + wi * wi - intensity[step * GROUP + j]
            win_b[j * WIN : (j + 1) * WIN, :WIN] = wr * excess
            win_b[j * WIN : (j + 1) * WIN, WIN:] = wi * excess
        grad = mm3(split(win_b[...]), fwd_lanes)
        for j in range(GROUP):
            win_a[:WIN, j * WIN : (j + 1) * WIN] = grad[j * WIN : (j + 1) * WIN, :WIN]
            win_a[WIN:, j * WIN : (j + 1) * WIN] = grad[j * WIN : (j + 1) * WIN, WIN:]
        win_a[...] = mm3(fwd_sides, split(win_a[...]))
        for j in range(GROUP):
            led = step * GROUP + j
            row, col = offs[0, led], offs[1, led]
            first = pl.multiple_of((col // 128) * 128, 128)
            shift = col - first
            gr = win_a[:WIN, j * WIN : (j + 1) * WIN] * -STEP_SIZE
            gi = win_a[WIN:, j * WIN : (j + 1) * WIN] * -STEP_SIZE
            ur, ui = cmul(pr, -pi, gr, gi)
            add(new, 0, row, first, shift, ur)
            add(new, 1, row, first, shift, ui)

    @pl.loop(0, PAD // 128)
    def _(n):
        at = pl.ds(pl.multiple_of(n * 128, 128), 128)
        for row in range(0, SUB, 8):
            items = []
            for k in range(RADIX):
                here = slice(k * SUB + row, k * SUB + row + 8)
                items.append((new[0, here, at], new[1, here, at]))
            done = fft_list(items, 1)
            for b in range(RADIX):
                sub[b, row : row + 8, at] = done[b][0]
                sub[b, SUB + row : SUB + row + 8, at] = done[b][1]

    @pl.loop(0, RADIX)
    def _(b):
        mixed = mm3((inv[0, b], inv[1, b]), split(sub[b]))
        rows = pl.ds(b, SUB, stride=RADIX)
        for n in range(5):
            y[n, rows, :] = mixed[:SUB, 128 * n : 128 * n + 128]
            y[5 + n, rows, :] = mixed[SUB:, 128 * n : 128 * n + 128]

    def put(start, count, real_at, imag_at):
        for n in range(5):
            rh, rl = split(y[n, start : start + count, :])
            ih, il = split(y[5 + n, start : start + count, :])
            left, right = slice(128 * n, 128 * n + 128), slice(PAD + 128 * n, PAD + 128 * n + 128)
            a = slice(real_at, real_at + count)
            v_hi[a, left], v_hi[a, right] = rh, ih
            v_lo[a, left], v_lo[a, right] = rl, il
            b = slice(imag_at, imag_at + count)
            v_hi[b, left], v_hi[b, right] = ih, -rh
            v_lo[b, left], v_lo[b, right] = il, -rl

    put(0, STRIDE, 0, STRIDE)
    put(STRIDE, OVL, 2 * STRIDE, 2 * STRIDE + OVL)

    for at, width in ((0, 256), (256, 256), (512, 256), (768, 256), (1024, 128)):
        right = (v_hi[at : at + width, :], v_lo[at : at + width, :])
        left = (t_hi[:TILE, :], t_lo[:TILE, :])
        out[:, at : at + width] = (
            mm_nt(left[0], right[0]) + (mm_nt(left[1], right[0]) + mm_nt(left[0], right[1]))
        )


def vmem():
    return pl.BlockSpec(memory_space=pltpu.VMEM)


def tile_step(tiles, pupils, intensity, offsets):
    seeds, fwd, inv, lanes, sides = tile_tables()
    return pl.pallas_call(
        tile_body,
        out_shape=jax.ShapeDtypeStruct((TILE, 2 * TILE), F32),
        in_specs=[pl.BlockSpec(memory_space=pltpu.SMEM)] + [vmem()] * 8,
        out_specs=vmem(),
        scratch_shapes=[
            pltpu.VMEM((2, TILE, PAD), F32),
            pltpu.VMEM((2 * PAD, 2 * PAD), BF),
            pltpu.VMEM((2 * PAD, 2 * PAD), BF),
            pltpu.VMEM((16, 128), BF),
            pltpu.VMEM((16, 128), BF),
            pltpu.VMEM((TILE, 2 * PAD), BF),
            pltpu.VMEM((TILE, 2 * PAD), BF),
            pltpu.VMEM((2 * PAD // 128, TILE, 128), F32),
            pltpu.VMEM((RADIX, 2 * SUB, PAD), F32),
            pltpu.VMEM((2, TILE + 8, PAD), F32),
            pltpu.VMEM((2, TILE + 8, PAD), F32),
            pltpu.VMEM((2 * TILE, 2 * PAD), BF),
            pltpu.VMEM((2 * TILE, 2 * PAD), BF),
            pltpu.VMEM((2 * WIN, GROUP * WIN), F32),
            pltpu.VMEM((GROUP * WIN, 2 * WIN), F32),
        ],
        compiler_params=pltpu.CompilerParams(vmem_limit_bytes=60 << 20),
        name="tile_step",
    )(offsets, tiles, pupils, intensity, seeds, fwd, inv, lanes, sides)


def row_tables():
    lane = np.arange(128)
    k1 = np.arange(32)
    turn = unit(-(k1[:, None] * lane[None, :]) / ROWS)
    keep = axis_filter(ROWS)[k1[:, None] + 32 * lane[None, :]]
    rows = np.stack([turn.real, turn.imag, keep.real, keep.imag]).astype(np.float32)
    full = dft_np(128, -1)
    mats = np.stack([*split_np(right_block(full)), *split_np(right_block(np.conj(full)))])
    return rows, mats


def row_body(got, rows, mats, out, work, mid):
    lane = lax.broadcasted_iota(jnp.int32, (8, 128), 1)
    ramp = jnp.where(lane < OVL, (lane.astype(F32) + 0.5) / OVL, 1.0)
    rest = jnp.where(lane < OVL, 1.0 - ramp, 0.0)

    @pl.loop(0, 8)
    def _(g):
        at = pl.ds(pl.multiple_of(g * 8, 8), 8)
        for a in range(4):
            items = []
            for p in range(8):
                re = got[p, at, 128 * a : 128 * a + 128]
                im = got[p, at, STRIDE + 128 * a : STRIDE + 128 * a + 128]
                if a == 0:
                    tail = got[(p - 1) % 8, at, 2 * STRIDE :]
                    re = ramp * re + rest * tail
                    im = ramp * im + rest * pltpu.roll(tail, 64, 1)
                items.append((re, im))
            done = fft_list(items, -1)
            for k in range(8):
                re, im = cscale(done[k], unit(-a * k / 32))
                mid[4 * k + a, 0, at, :] = re
                mid[4 * k + a, 1, at, :] = im

        @pl.loop(0, 8)
        def _(k):
            items = [(mid[4 * k + a, 0, at, :], mid[4 * k + a, 1, at, :]) for a in range(4)]
            done = fft_list(items, -1)
            for q in range(4):
                index = k + 8 * q
                tr = rows[0, pl.ds(index, 1), :]
                ti = rows[1, pl.ds(index, 1), :]
                re, im = cmul(*done[q], tr, ti)
                start = pl.ds(pl.multiple_of(index * 64 + g * 8, 8), 8)
                work[start, :128] = re
                work[start, 128:] = im

    @pl.loop(0, 4)
    def _(n):
        at = pl.ds(pl.multiple_of(n * 512, 512), 512)
        full = mm3(split(work[at, :]), (mats[0], mats[1]))
        full = full.reshape(8, 64, 256)
        keep = pl.ds(pl.multiple_of(n * 8, 8), 8)
        kr, ki = rows[2, keep, :][:, None, :], rows[3, keep, :][:, None, :]
        re, im = cmul(full[:, :, :128], full[:, :, 128:], kr, ki)
        both = jnp.concatenate([re, im], axis=2).reshape(512, 256)
        work[at, :] = mm3(split(both), (mats[2], mats[3]))

    @pl.loop(0, 8)
    def _(g):
        at = pl.ds(pl.multiple_of(g * 8, 8), 8)

        @pl.loop(0, 8)
        def _(k):
            items = []
            for q in range(4):
                index = k + 8 * q
                tr = rows[0, pl.ds(index, 1), :]
                ti = rows[1, pl.ds(index, 1), :]
                start = pl.ds(pl.multiple_of(index * 64 + g * 8, 8), 8)
                items.append(cmul(work[start, :128], work[start, 128:], tr, -ti))
            done = fft_list(items, 1)
            for a in range(4):
                mid[4 * k + a, 0, at, :] = done[a][0]
                mid[4 * k + a, 1, at, :] = done[a][1]

        for a in range(4):
            items = [
                cscale((mid[4 * k + a, 0, at, :], mid[4 * k + a, 1, at, :]), unit(a * k / 32))
                for k in range(8)
            ]
            done = fft_list(items, 1)
            for p in range(8):
                mid[4 * p + a, 0, at, :] = done[p][0]
                mid[4 * p + a, 1, at, :] = done[p][1]

    @pl.loop(0, 32)
    def _(a):
        out[a] = jnp.transpose(mid[a].reshape(128, 128))


def row_step(got):
    rows, mats = row_tables()
    return pl.pallas_call(
        row_body,
        out_shape=jax.ShapeDtypeStruct((32, 128, 128), F32),
        in_specs=[vmem()] * 3,
        out_specs=vmem(),
        scratch_shapes=[
            pltpu.VMEM((2048, 256), F32),
            pltpu.VMEM((32, 2, 64, 128), F32),
        ],
        compiler_params=pltpu.CompilerParams(vmem_limit_bytes=40 << 20),
        name="row_step",
    )(got, rows, mats)


def col_tables():
    lane = np.arange(64)
    kc = np.arange(16)
    kr = np.arange(8)
    low = kc[None, :] + 16 * kr[:, None]
    turn = unit(-(low[:, :, None] * lane) / COLS)
    keep = axis_filter(COLS)[low[:, :, None] + 128 * lane]
    rows = np.stack([turn.real, turn.imag, keep.real, keep.imag]).reshape(4, 128, 64)
    rows = np.concatenate([rows, rows], axis=2).astype(np.float32)
    inner = unit(-(np.arange(8)[:, None] * kc[None, :]) / 128)
    full = np.kron(np.eye(2), dft_np(64, -1))
    mats = np.stack([*split_np(right_block(full)), *split_np(right_block(np.conj(full)))])
    return rows, mats, inner


def col_body(got, rows, mats, out, work, mid):
    left = lax.broadcasted_iota(jnp.int32, (8, 128), 1) < 64
    inner = col_tables()[2]

    for half in range(2):
        at = slice(8 * half, 8 * half + 8)
        for r in range(8):
            items = []
            for c in range(16):
                a = got[16 * r + c, 8 * half : 8 * half + 8, :]
                b = got[16 * r + c, 16 + 8 * half : 24 + 8 * half, :]
                re = jnp.where(left, a, pltpu.roll(b, 64, 1))
                im = jnp.where(left, pltpu.roll(a, 64, 1), b)
                items.append((re, im))
            done = fft_list(items, -1)
            for k in range(16):
                re, im = cscale(done[k], inner[r, k])
                mid[16 * r + k, 0, at, :] = re
                mid[16 * r + k, 1, at, :] = im

    @pl.loop(0, 16)
    def _(k):
        for half in range(2):
            at = slice(8 * half, 8 * half + 8)
            items = [(mid[16 * r + k, 0, at, :], mid[16 * r + k, 1, at, :]) for r in range(8)]
            done = fft_list(items, -1)
            for q in range(8):
                index = 16 * q + k
                tr = rows[0, pl.ds(index, 1), :]
                ti = rows[1, pl.ds(index, 1), :]
                re, im = cmul(*done[q], tr, ti)
                work[index, at, :128] = re
                work[index, at, 128:] = im

    @pl.loop(0, 4)
    def _(n):
        keep = pl.ds(pl.multiple_of(n * 32, 32), 32)
        full = mm3(split(work[keep].reshape(512, 256)), (mats[0], mats[1]))
        full = full.reshape(32, 16, 256)
        kr, ki = rows[2, keep, :][:, None, :], rows[3, keep, :][:, None, :]
        re, im = cmul(full[:, :, :128], full[:, :, 128:], kr, ki)
        both = jnp.concatenate([re, im], axis=2).reshape(512, 256)
        work[keep] = mm3(split(both), (mats[2], mats[3])).reshape(32, 16, 256)

    @pl.loop(0, 16)
    def _(k):
        for half in range(2):
            at = slice(8 * half, 8 * half + 8)
            items = []
            for q in range(8):
                index = 16 * q + k
                tr = rows[0, pl.ds(index, 1), :]
                ti = rows[1, pl.ds(index, 1), :]
                items.append(cmul(work[index, at, :128], work[index, at, 128:], tr, -ti))
            done = fft_list(items, 1)
            for r in range(8):
                mid[16 * r + k, 0, at, :] = done[r][0]
                mid[16 * r + k, 1, at, :] = done[r][1]

    for half in range(2):
        at = slice(8 * half, 8 * half + 8)
        for r in range(8):
            items = [
                cscale((mid[16 * r + k, 0, at, :], mid[16 * r + k, 1, at, :]), np.conj(inner[r, k]))
                for k in range(16)
            ]
            done = fft_list(items, 1)
            for c in range(16):
                mid[16 * r + c, 0, at, :] = done[c][0]
                mid[16 * r + c, 1, at, :] = done[c][1]

    @pl.loop(0, 16)
    def _(c):
        for part in range(2):
            for half in range(2):
                at = slice(8 * half, 8 * half + 8)
                for pair in range(4):
                    a = mid[32 * pair + c, part, at, :]
                    b = mid[32 * pair + 16 + c, part, at, :]
                    lanes = slice(128 * pair, 128 * pair + 128)
                    top = pl.ds(pl.multiple_of(c * 32 + 8 * half, 8), 8)
                    low = pl.ds(pl.multiple_of(c * 32 + 16 + 8 * half, 8), 8)
                    out[part, top, lanes] = jnp.where(left, a, pltpu.roll(b, 64, 1))
                    out[part, low, lanes] = jnp.where(left, pltpu.roll(a, 64, 1), b)


def col_step(got):
    rows, mats, _ = col_tables()
    return pl.pallas_call(
        col_body,
        out_shape=jax.ShapeDtypeStruct((2, 512, 512), F32),
        in_specs=[vmem()] * 3,
        out_specs=vmem(),
        scratch_shapes=[
            pltpu.VMEM((128, 16, 256), F32),
            pltpu.VMEM((128, 2, 16, 128), F32),
        ],
        compiler_params=pltpu.CompilerParams(vmem_limit_bytes=40 << 20),
        name="col_step",
    )(got, rows, mats)


def local(tiles, pupils, intensity, offsets):
    refined = tile_step(tiles, pupils, intensity, offsets[0, 0])
    pairs = [(source, (source + 1) % 16) for source in range(16)]
    behind = lax.ppermute(refined[STRIDE:], "col", pairs)
    ramp = ((jnp.arange(OVL, dtype=F32) + 0.5) / OVL)[:, None]
    front = ramp * refined[:OVL] + (1.0 - ramp) * behind
    field = lax.dynamic_update_slice(refined[:STRIDE], front, (0, 0))
    field = field.reshape(8, 64, 2 * TILE)
    field = lax.all_to_all(field, "row", split_axis=0, concat_axis=0, tiled=True)
    field = row_step(field).reshape(128, 32, 128)
    field = lax.all_to_all(field, ("row", "col"), split_axis=0, concat_axis=0, tiled=True)
    field = col_step(field)
    return lax.all_to_all(field, "col", split_axis=1, concat_axis=1, tiled=True)


def solution(mesh):
    placed = (
        P(None, "row", "col"),
        P(None, "row", "col"),
        P(None, "row", "col"),
        P("row", "col", None, None),
    )
    return jax.shard_map(
        local, mesh=mesh, in_specs=placed, out_specs=P(None, "row", "col"), check_vma=False
    )
```

```python
import math

import numpy as np
import ml_dtypes
import jax
import jax.numpy as jnp
from jax import lax
from jax.experimental import pallas as pl
from jax.experimental.pallas import tpu as pltpu
from jax.sharding import PartitionSpec as P

TILE = 576
PAD = 640
OVL = 64
WIN = 128
LEDS = 16
STRIDE = 512
ROWS = 4096
COLS = 8192
FRESNEL = 2048
STEP_SIZE = 0.05
RADIX = 6
SUB = TILE // RADIX
BF = jnp.bfloat16
F32 = jnp.float32
GROUP = 4


def split_np(table):
    table = np.asarray(table, np.float64)
    high = table.astype(np.float32).astype(ml_dtypes.bfloat16)
    low = (table - high.astype(np.float64)).astype(np.float32).astype(ml_dtypes.bfloat16)
    return high, low


def unit(turns):
    turns = np.asarray(turns, np.float64)
    return np.exp(2j * np.pi * (turns - np.floor(turns)))


def right_block(table):
    return np.block([[table.real, table.imag], [-table.imag, table.real]])


def left_block(table):
    return np.block([[table.real, -table.imag], [table.imag, table.real]])


def dft_np(length, sign):
    index = np.arange(length)
    return unit(sign * (index[:, None] * index[None, :] % length) / length)


def axis_filter(length):
    freq = np.arange(length)
    signed = np.where(freq < length // 2, freq, freq - length).astype(np.float64)
    turns = signed * signed * (FRESNEL / (length * length))
    return np.exp(-2.0 * signed * signed / (length * length)) * unit(-turns) / length


def split(value):
    high = value.astype(BF)
    low = (value - high.astype(F32)).astype(BF)
    return high, low


def mm(left, right):
    return jnp.dot(left, right, preferred_element_type=F32)


def mm3(left, right):
    return mm(left[0], right[0]) + (mm(left[1], right[0]) + mm(left[0], right[1]))


def mm_nt(left, right):
    return lax.dot_general(left, right, (((1,), (1,)), ((), ())), preferred_element_type=F32)


def cmul(ar, ai, br, bi):
    return ar * br - ai * bi, ar * bi + ai * br


def cscale(value, factor):
    re, im = value
    fr, fi = float(factor.real), float(factor.imag)
    near = 1e-12
    if abs(fi) < near:
        if abs(fr - 1) < near:
            return re, im
        if abs(fr + 1) < near:
            return -re, -im
    if abs(fr) < near:
        if abs(fi - 1) < near:
            return -im, re
        if abs(fi + 1) < near:
            return im, -re
    if abs(abs(fr) - abs(fi)) < near:
        size = abs(fr)
        sr, si = math.copysign(1, fr), math.copysign(1, fi)
        left = re if sr > 0 else -re
        low = im if sr > 0 else -im
        new_re = left - im if si > 0 else left + im
        new_im = low + re if si > 0 else low - re
        return new_re * size, new_im * size
    return re * fr - im * fi, re * fi + im * fr


def fft_list(items, sign):
    count = len(items)
    if count == 1:
        return items
    if count == 3:
        (ar, ai), (br, bi), (cr, ci) = items
        sr, si, dr, di = br + cr, bi + ci, br - cr, bi - ci
        mr, mi = ar - 0.5 * sr, ai - 0.5 * si
        root = sign * math.sqrt(0.75)
        tr, ti = -root * di, root * dr
        return [(ar + sr, ai + si), (mr + tr, mi + ti), (mr - tr, mi - ti)]
    even = fft_list(items[0::2], sign)
    odd = fft_list(items[1::2], sign)
    half = count // 2
    first, second = [], []
    for index in range(half):
        turned = cscale(odd[index], unit(sign * index / count))
        er, ei = even[index]
        first.append((er + turned[0], ei + turned[1]))
        second.append((er - turned[0], ei - turned[1]))
    return first + second


def tile_tables():
    index = np.arange(TILE)
    low = unit(-(np.arange(24)[:, None] * index[None, :] % TILE) / TILE) / math.sqrt(TILE)
    high = unit(-(24 * np.arange(24)[:, None] * index[None, :] % TILE) / TILE)
    seeds = np.zeros((4, 24, PAD), np.float32)
    seeds[0, :, :TILE], seeds[1, :, :TILE] = low.real, low.imag
    seeds[2, :, :TILE], seeds[3, :, :TILE] = high.real, high.imag
    small = np.arange(SUB)
    forward, inverse = [], []
    for part in range(RADIX):
        turned = unit(-(part * small[:, None] + RADIX * small[:, None] * small[None, :]) / TILE)
        turned = turned / math.sqrt(TILE)
        forward.append(left_block(turned))
        inverse.append(left_block(np.conj(turned.T)))
    forward = np.stack(split_np(np.stack(forward)))
    inverse = np.stack(split_np(np.stack(inverse)))
    window = dft_np(WIN, -1) / math.sqrt(WIN)
    lanes = np.stack(
        [*split_np(right_block(np.conj(window))), *split_np(right_block(window))]
    )
    sides = np.stack(
        [*split_np(left_block(np.conj(window))), *split_np(left_block(window))]
    )
    return seeds, forward, inverse, lanes, sides


def cut(ref, part, row, first, back):
    base = pl.multiple_of((row // 8) * 8, 8)
    down = row - base
    wide = ref[part, pl.ds(base, WIN + 8), pl.ds(first, 256)]
    wide = pltpu.roll(wide, back, 1)[:, :WIN].reshape(WIN // 8 + 1, 8, WIN)
    wide = pltpu.roll(wide, lax.rem(8 - down, 8), 1)
    lane = lax.broadcasted_iota(jnp.int32, (WIN // 8, 8, WIN), 1)
    return jnp.where(lane < 8 - down, wide[:-1], wide[1:]).reshape(WIN, WIN)


def add(ref, part, row, first, shift, value):
    base = pl.multiple_of((row // 8) * 8, 8)
    down = row - base
    turned = pltpu.roll(value.reshape(WIN // 8, 8, WIN), down, 1)
    zero = jnp.zeros((1, 8, WIN), F32)
    lane = lax.broadcasted_iota(jnp.int32, (WIN // 8 + 1, 8, WIN), 1)
    upper = jnp.concatenate([zero, turned], axis=0)
    lower = jnp.concatenate([turned, zero], axis=0)
    tall = jnp.where(lane < down, upper, lower).reshape(WIN + 8, WIN)
    wide = jnp.concatenate([tall, jnp.zeros((WIN + 8, 128), F32)], axis=1)
    here = (part, pl.ds(base, WIN + 8), pl.ds(first, 256))
    ref[here] = ref[here] + pltpu.roll(wide, shift, 1)


def tile_body(
    offs, tiles, pupils, intensity, seeds, fwd, inv, lanes, sides, out,
    base, t_hi, t_lo, l_hi, l_lo, x_hi, x_lo, y, sub, spec, new, v_hi, v_lo, win_a, win_b,
):
    low_r, low_i = seeds[0], seeds[1]

    @pl.loop(0, 24)
    def _(a):
        hr = seeds[2, pl.ds(a, 1), :]
        hi = seeds[3, pl.ds(a, 1), :]
        tr, ti = cmul(low_r, low_i, hr, hi)
        start = pl.multiple_of(a * 24, 8)
        base[0, pl.ds(start, 24), :] = tr
        base[1, pl.ds(start, 24), :] = ti

    zero_tail = jnp.zeros((PAD - TILE, 2 * PAD), BF)
    t_hi[TILE:PAD, :] = zero_tail
    t_lo[TILE:PAD, :] = zero_tail
    t_hi[PAD + TILE :, :] = zero_tail
    t_lo[PAD + TILE :, :] = zero_tail

    @pl.loop(0, TILE // 96)
    def _(a):
        start = pl.multiple_of(a * 96, 16)
        ch, cl = split(base[0, pl.ds(start, 96), :])
        sh, sl = split(base[1, pl.ds(start, 96), :])
        t_hi[pl.ds(start, 96), :PAD] = ch
        t_lo[pl.ds(start, 96), :PAD] = cl
        t_hi[pl.ds(start, 96), PAD:] = sh
        t_lo[pl.ds(start, 96), PAD:] = sl
        t_hi[pl.ds(start + PAD, 96), :PAD] = -sh
        t_lo[pl.ds(start + PAD, 96), :PAD] = -sl
        t_hi[pl.ds(start + PAD, 96), PAD:] = ch
        t_lo[pl.ds(start + PAD, 96), PAD:] = cl

    x_hi[...] = jnp.zeros_like(x_hi)
    x_lo[...] = jnp.zeros_like(x_lo)

    @pl.loop(0, TILE // 96)
    def _(a):
        start = pl.multiple_of(a * 96, 16)
        for part in range(2):
            high, low = split(tiles[part, pl.ds(start, 96), :])
            x_hi[pl.ds(start, 96), part * PAD : part * PAD + TILE] = high
            x_lo[pl.ds(start, 96), part * PAD : part * PAD + TILE] = low

    @pl.loop(0, 2 * PAD // 256)
    def _(n):
        at = pl.ds(pl.multiple_of(n * 256, 256), 256)
        both = mm3((x_hi[...], x_lo[...]), (t_hi[:, at], t_lo[:, at]))
        y[2 * n] = both[:, :128]
        y[2 * n + 1] = both[:, 128:]

    @pl.loop(0, RADIX)
    def _(b):
        rows = pl.ds(b, SUB, stride=RADIX)
        parts = [
            jnp.concatenate([y[n, rows, :] for n in range(5 * part, 5 * part + 5)], axis=1)
            for part in range(2)
        ]
        sub[b] = mm3((fwd[0, b], fwd[1, b]), split(jnp.concatenate(parts, axis=0)))

    @pl.loop(0, PAD // 128)
    def _(n):
        at = pl.ds(pl.multiple_of(n * 128, 128), 128)
        for row in range(0, SUB, 8):
            items = [
                (sub[b, row : row + 8, at], sub[b, SUB + row : SUB + row + 8, at])
                for b in range(RADIX)
            ]
            done = fft_list(items, -1)
            for k in range(RADIX):
                here = slice(k * SUB + row, k * SUB + row + 8)
                spec[0, here, at] = done[k][0]
                spec[1, here, at] = done[k][1]
                new[0, here, at] = done[k][0]
                new[1, here, at] = done[k][1]

    for ref in (spec, new):
        for part in range(2):
            ref[part, TILE:, :] = jnp.zeros((8, PAD), F32)
    pr, pi = pupils[0], pupils[1]
    inv_lanes = (lanes[0], lanes[1])
    fwd_lanes = (lanes[2], lanes[3])
    inv_sides = (sides[0], sides[1])
    fwd_sides = (sides[2], sides[3])

    @pl.loop(0, LEDS // GROUP)
    def _(step):
        for j in range(GROUP):
            led = step * GROUP + j
            row, col = offs[0, led], offs[1, led]
            first = pl.multiple_of((col // 128) * 128, 128)
            shift = col - first
            back = lax.rem(256 - shift, 256)
            cr = cut(spec, 0, row, first, back)
            ci = cut(spec, 1, row, first, back)
            wr, wi = cmul(pr, pi, cr, ci)
            win_a[:WIN, j * WIN : (j + 1) * WIN] = wr
            win_a[WIN:, j * WIN : (j + 1) * WIN] = wi
        side = mm3(inv_sides, split(win_a[...]))
        for j in range(GROUP):
            win_b[j * WIN : (j + 1) * WIN, :WIN] = side[:WIN, j * WIN : (j + 1) * WIN]
            win_b[j * WIN : (j + 1) * WIN, WIN:] = side[WIN:, j * WIN : (j + 1) * WIN]
        wave = mm3(split(win_b[...]), inv_lanes)
        for j in range(GROUP):
            wr = wave[j * WIN : (j + 1) * WIN, :WIN]
            wi = wave[j * WIN : (j + 1) * WIN, WIN:]
            excess = wr * wr + wi * wi - intensity[step * GROUP + j]
            win_b[j * WIN : (j + 1) * WIN, :WIN] = wr * excess
            win_b[j * WIN : (j + 1) * WIN, WIN:] = wi * excess
        grad = mm3(split(win_b[...]), fwd_lanes)
        for j in range(GROUP):
            win_a[:WIN, j * WIN : (j + 1) * WIN] = grad[j * WIN : (j + 1) * WIN, :WIN]
            win_a[WIN:, j * WIN : (j + 1) * WIN] = grad[j * WIN : (j + 1) * WIN, WIN:]
        win_a[...] = mm3(fwd_sides, split(win_a[...]))
        for j in range(GROUP):
            led = step * GROUP + j
            row, col = offs[0, led], offs[1, led]
            first = pl.multiple_of((col // 128) * 128, 128)
            shift = col - first
            gr = win_a[:WIN, j * WIN : (j + 1) * WIN] * -STEP_SIZE
            gi = win_a[WIN:, j * WIN : (j + 1) * WIN] * -STEP_SIZE
            ur, ui = cmul(pr, -pi, gr, gi)
            add(new, 0, row, first, shift, ur)
            add(new, 1, row, first, shift, ui)

    @pl.loop(0, PAD // 128)
    def _(n):
        at = pl.ds(pl.multiple_of(n * 128, 128), 128)
        for row in range(0, SUB, 8):
            items = []
            for k in range(RADIX):
                here = slice(k * SUB + row, k * SUB + row + 8)
                items.append((new[0, here, at], new[1, here, at]))
            done = fft_list(items, 1)
            for b in range(RADIX):
                sub[b, row : row + 8, at] = done[b][0]
                sub[b, SUB + row : SUB + row + 8, at] = done[b][1]

    @pl.loop(0, RADIX)
    def _(b):
        mixed = mm3((inv[0, b], inv[1, b]), split(sub[b]))
        rows = pl.ds(b, SUB, stride=RADIX)
        for n in range(5):
            y[n, rows, :] = mixed[:SUB, 128 * n : 128 * n + 128]
            y[5 + n, rows, :] = mixed[SUB:, 128 * n : 128 * n + 128]

    def put(start, count, real_at, imag_at):
        for n in range(5):
            rh, rl = split(y[n, start : start + count, :])
            ih, il = split(y[5 + n, start : start + count, :])
            left, right = slice(128 * n, 128 * n + 128), slice(PAD + 128 * n, PAD + 128 * n + 128)
            a = slice(real_at, real_at + count)
            v_hi[a, left], v_hi[a, right] = rh, ih
            v_lo[a, left], v_lo[a, right] = rl, il
            b = slice(imag_at, imag_at + count)
            v_hi[b, left], v_hi[b, right] = ih, -rh
            v_lo[b, left], v_lo[b, right] = il, -rl

    put(0, STRIDE, 0, STRIDE)
    put(STRIDE, OVL, 2 * STRIDE, 2 * STRIDE + OVL)

    for at, width in ((0, 256), (256, 256), (512, 256), (768, 256), (1024, 128)):
        right = (v_hi[at : at + width, :], v_lo[at : at + width, :])
        left = (t_hi[:TILE, :], t_lo[:TILE, :])
        out[:, at : at + width] = (
            mm_nt(left[0], right[0]) + (mm_nt(left[1], right[0]) + mm_nt(left[0], right[1]))
        )


def vmem():
    return pl.BlockSpec(memory_space=pltpu.VMEM)


def tile_step(tiles, pupils, intensity, offsets):
    seeds, fwd, inv, lanes, sides = tile_tables()
    return pl.pallas_call(
        tile_body,
        out_shape=jax.ShapeDtypeStruct((TILE, 2 * TILE), F32),
        in_specs=[pl.BlockSpec(memory_space=pltpu.SMEM)] + [vmem()] * 8,
        out_specs=vmem(),
        scratch_shapes=[
            pltpu.VMEM((2, TILE, PAD), F32),
            pltpu.VMEM((2 * PAD, 2 * PAD), BF),
            pltpu.VMEM((2 * PAD, 2 * PAD), BF),
            pltpu.VMEM((16, 128), BF),
            pltpu.VMEM((16, 128), BF),
            pltpu.VMEM((TILE, 2 * PAD), BF),
            pltpu.VMEM((TILE, 2 * PAD), BF),
            pltpu.VMEM((2 * PAD // 128, TILE, 128), F32),
            pltpu.VMEM((RADIX, 2 * SUB, PAD), F32),
            pltpu.VMEM((2, TILE + 8, PAD), F32),
            pltpu.VMEM((2, TILE + 8, PAD), F32),
            pltpu.VMEM((2 * TILE, 2 * PAD), BF),
            pltpu.VMEM((2 * TILE, 2 * PAD), BF),
            pltpu.VMEM((2 * WIN, GROUP * WIN), F32),
            pltpu.VMEM((GROUP * WIN, 2 * WIN), F32),
        ],
        compiler_params=pltpu.CompilerParams(vmem_limit_bytes=60 << 20),
        name="tile_step",
    )(offsets, tiles, pupils, intensity, seeds, fwd, inv, lanes, sides)


def row_tables():
    lane = np.arange(128)
    k1 = np.arange(32)
    turn = unit(-(k1[:, None] * lane[None, :]) / ROWS)
    keep = axis_filter(ROWS)[k1[:, None] + 32 * lane[None, :]]
    rows = np.stack([turn.real, turn.imag, keep.real, keep.imag]).astype(np.float32)
    full = dft_np(128, -1)
    mats = np.stack([*split_np(right_block(full)), *split_np(right_block(np.conj(full)))])
    return rows, mats


def col_tables():
    lane = np.arange(64)
    kc = np.arange(16)
    kr = np.arange(8)
    low = kc[None, :] + 16 * kr[:, None]
    turn = unit(-(low[:, :, None] * lane) / COLS)
    keep = axis_filter(COLS)[low[:, :, None] + 128 * lane]
    rows = np.stack([turn.real, turn.imag, keep.real, keep.imag]).reshape(4, 128, 64)
    rows = np.concatenate([rows, rows], axis=2).astype(np.float32)
    inner = unit(-(np.arange(8)[:, None] * kc[None, :]) / 128)
    full = np.kron(np.eye(2), dft_np(64, -1))
    mats = np.stack([*split_np(right_block(full)), *split_np(right_block(np.conj(full)))])
    return rows, mats, inner


MESH = pl.DeviceIdType.MESH
FAR_ROWS = ((1, 2), (1, 1), (1, 3), (0, 2), (1, 0), (0, 1), (0, 3))
FAR_COLS = sorted(
    ((y, x, k) for y in range(4) for x in range(2) for k in range(2) if y or x or k),
    key=lambda step: -(min(step[0], 4 - step[0]) + step[1]),
)
QUARTER = 16


def settle(ref, sem):
    pltpu.make_async_copy(ref, ref, sem).wait()


def field_body(
    refined, r_rows, r_mats, c_rows, c_mats, out,
    halo, front, got, work, mid, give, have, send,
    halo_sem, send_sem, recv_row, own_row, recv_all, own_all, recv_col, own_sem,
):
    row, col = lax.axis_index("row"), lax.axis_index("col")
    xh, z = row // 4, lax.rem(row, 4)
    y, xl, core = col // 4, lax.rem(col // 2, 2), lax.rem(col, 2)
    rows_at = [lax.rem(row + step, 8) for step in range(8)]
    cols_at = [lax.rem(col + step, 16) for step in range(16)]

    barrier = pltpu.get_barrier_semaphore()
    for i in range(8):
        for j in range(16):
            if i or j:
                pl.semaphore_signal(
                    barrier, inc=1, device_id=(rows_at[i], cols_at[j]), device_id_type=MESH
                )
    pl.semaphore_wait(barrier, 127)

    edge = pltpu.make_async_remote_copy(
        refined.at[STRIDE:], halo, halo_sem.at[0], halo_sem.at[1],
        device_id=(row, cols_at[1]), device_id_type=MESH,
    )
    edge.start()

    chunks = [lax.rem(xh + i, 2) * 4 + lax.rem(z + j, 4) for i, j in FAR_ROWS]

    def give_row(target, quarter, source):
        pltpu.make_async_remote_copy(
            source, got.at[row, quarter * QUARTER : (quarter + 1) * QUARTER],
            send_sem.at[0], recv_row.at[quarter], device_id=(target, col), device_id_type=MESH,
        ).start()

    def plain(target, quarter):
        start = pl.multiple_of(target * 64 + quarter * QUARTER, QUARTER)
        return refined.at[pl.ds(start, QUARTER)]

    def blended(quarter):
        return front.at[quarter * QUARTER : (quarter + 1) * QUARTER]

    for target in chunks:
        @pl.when(target != 0)
        def _():
            give_row(target, 0, plain(target, 0))

    edge.wait()
    place = lax.broadcasted_iota(jnp.int32, (OVL, 2 * TILE), 0).astype(F32)
    ramp = (place + 0.5) / OVL
    front[...] = ramp * refined[:OVL] + (1.0 - ramp) * halo[...]

    for target in chunks:
        @pl.when(target == 0)
        def _():
            give_row(target, 0, blended(0))

    for quarter in range(1, 4):
        for target in chunks:
            @pl.when(target != 0)
            def _():
                give_row(target, quarter, plain(target, quarter))

            @pl.when(target == 0)
            def _():
                give_row(target, quarter, blended(quarter))

    @pl.when(row == 0)
    def _():
        pltpu.make_async_copy(front, got.at[0], own_row).start()

    @pl.when(row != 0)
    def _():
        start = pl.multiple_of(row * 64, 64)
        pltpu.make_async_copy(refined.at[pl.ds(start, 64)], got.at[row], own_row).start()

    settle(front, own_row)

    lane = lax.broadcasted_iota(jnp.int32, (8, 128), 1)
    slope = jnp.where(lane < OVL, (lane.astype(F32) + 0.5) / OVL, 1.0)
    rest = jnp.where(lane < OVL, 1.0 - slope, 0.0)

    @pl.loop(0, 4)
    def _(quarter):
        columns = pl.ds(pl.multiple_of(quarter * QUARTER, QUARTER), QUARTER)
        settle(got.at[:7, columns], recv_row.at[quarter])

        @pl.loop(0, 2)
        def _(half):
            at = pl.ds(pl.multiple_of(quarter * QUARTER + half * 8, 8), 8)
            for a in range(4):
                items = []
                for p in range(8):
                    re = got[p, at, 128 * a : 128 * a + 128]
                    im = got[p, at, STRIDE + 128 * a : STRIDE + 128 * a + 128]
                    if a == 0:
                        tail = got[(p - 1) % 8, at, 2 * STRIDE :]
                        re = slope * re + rest * tail
                        im = slope * im + rest * pltpu.roll(tail, 64, 1)
                    items.append((re, im))
                done = fft_list(items, -1)
                for k in range(8):
                    re, im = cscale(done[k], unit(-a * k / 32))
                    mid[4 * k + a, 0, at, :] = re
                    mid[4 * k + a, 1, at, :] = im

            @pl.loop(0, 8)
            def _(k):
                items = [(mid[4 * k + a, 0, at, :], mid[4 * k + a, 1, at, :]) for a in range(4)]
                done = fft_list(items, -1)
                for q in range(4):
                    index = k + 8 * q
                    tr = r_rows[0, pl.ds(index, 1), :]
                    ti = r_rows[1, pl.ds(index, 1), :]
                    re, im = cmul(*done[q], tr, ti)
                    start = pl.ds(pl.multiple_of(index * QUARTER + half * 8, 8), 8)
                    work[start, :128] = re
                    work[start, 128:] = im

        full = mm3(split(work[:512]), (r_mats[0], r_mats[1]))
        full = full.reshape(32, QUARTER, 256)
        kr, ki = r_rows[2][:, None, :], r_rows[3][:, None, :]
        re, im = cmul(full[:, :, :128], full[:, :, 128:], kr, ki)
        both = jnp.concatenate([re, im], axis=2).reshape(512, 256)
        work[:512] = mm3(split(both), (r_mats[2], r_mats[3]))

        @pl.loop(0, 2)
        def _(half):
            at = pl.ds(pl.multiple_of(quarter * QUARTER + half * 8, 8), 8)

            @pl.loop(0, 8)
            def _(k):
                items = []
                for q in range(4):
                    index = k + 8 * q
                    tr = r_rows[0, pl.ds(index, 1), :]
                    ti = r_rows[1, pl.ds(index, 1), :]
                    start = pl.ds(pl.multiple_of(index * QUARTER + half * 8, 8), 8)
                    items.append(cmul(work[start, :128], work[start, 128:], tr, -ti))
                done = fft_list(items, 1)
                for a in range(4):
                    mid[4 * k + a, 0, at, :] = done[a][0]
                    mid[4 * k + a, 1, at, :] = done[a][1]

            for a in range(4):
                items = [
                    cscale((mid[4 * k + a, 0, at, :], mid[4 * k + a, 1, at, :]), unit(a * k / 32))
                    for k in range(8)
                ]
                done = fft_list(items, 1)
                for p in range(8):
                    mid[4 * p + a, 0, at, :] = done[p][0]
                    mid[4 * p + a, 1, at, :] = done[p][1]

    me = row * 16 + col

    def peers(step):
        tr = lax.rem(xh + 1 + step // 16, 2) * 4 + lax.rem(z + 2 + (step // 4) % 4, 4)
        ty = lax.rem(y + 2 + step % 4, 4)
        ends = []
        for i in range(2):
            for j in range(2):
                ends.append((tr, ty * 4 + lax.rem(xl + i, 2) * 2 + lax.rem(core + j, 2)))
        return tr * 4 + ty, ends

    own_step = 26

    def give_all(step, ends, part):
        lines = slice(part * 16, part * 16 + 16)
        for index, (tr, tc) in enumerate(ends):
            def go(tr=tr, tc=tc):
                pltpu.make_async_remote_copy(
                    give.at[tr * 16 + tc, lines], have.at[me, lines],
                    send_sem.at[1], recv_all.at[part], device_id=(tr, tc), device_id_type=MESH,
                ).start()

            if index:
                go()
            else:
                pl.when(step != own_step)(go)

    @pl.loop(0, 32)
    def _(step):
        block, ends = peers(step)
        flat = jnp.transpose(mid[block].reshape(128, 128))
        for i in range(4):
            give[block * 4 + i] = flat[32 * i : 32 * i + 32]
        give_all(step, ends, 0)

    own = pltpu.make_async_copy(give.at[me], have.at[me], own_all)
    own.start()

    @pl.loop(0, 32)
    def _(step):
        give_all(step, peers(step)[1], 1)

    own.wait()

    left = lane < 64
    inner = col_tables()[2]

    @pl.loop(0, 2)
    def _(part):
        lines = pl.ds(pl.multiple_of(part * 16, 16), 16)
        top = pl.ds(pl.multiple_of(part * 16, 8), 8)
        low = pl.ds(pl.multiple_of(part * 16 + 8, 8), 8)
        settle(have.at[:127, lines], recv_all.at[part])

        for r in range(8):
            items = []
            for c in range(16):
                a = have[16 * r + c, top, :]
                b = have[16 * r + c, low, :]
                re = jnp.where(left, a, pltpu.roll(b, 64, 1))
                im = jnp.where(left, pltpu.roll(a, 64, 1), b)
                items.append((re, im))
            done = fft_list(items, -1)
            for k in range(16):
                flat = 8 * (16 * r + k)
                re, im = cscale(done[k], inner[r, k])
                work[flat : flat + 8, :128] = re
                work[flat : flat + 8, 128:] = im

        @pl.loop(0, 16)
        def _(k):
            places = [pl.ds(pl.multiple_of(8 * (16 * r + k), 8), 8) for r in range(8)]
            items = [(work[at, :128], work[at, 128:]) for at in places]
            done = fft_list(items, -1)
            for q in range(8):
                tr = c_rows[0, pl.ds(16 * q + k, 1), :]
                ti = c_rows[1, pl.ds(16 * q + k, 1), :]
                re, im = cmul(*done[q], tr, ti)
                work[places[q], :128] = re
                work[places[q], 128:] = im

        @pl.loop(0, 2)
        def _(n):
            at = pl.ds(pl.multiple_of(n * 512, 512), 512)
            keep = pl.ds(pl.multiple_of(n * 64, 64), 64)
            full = mm3(split(work[at, :]), (c_mats[0], c_mats[1]))
            full = full.reshape(64, 8, 256)
            kr, ki = c_rows[2, keep, :][:, None, :], c_rows[3, keep, :][:, None, :]
            re, im = cmul(full[:, :, :128], full[:, :, 128:], kr, ki)
            both = jnp.concatenate([re, im], axis=2).reshape(512, 256)
            work[at, :] = mm3(split(both), (c_mats[2], c_mats[3]))

        @pl.loop(0, 16)
        def _(k):
            places = [pl.ds(pl.multiple_of(8 * (16 * r + k), 8), 8) for r in range(8)]
            items = []
            for q in range(8):
                tr = c_rows[0, pl.ds(16 * q + k, 1), :]
                ti = c_rows[1, pl.ds(16 * q + k, 1), :]
                items.append(cmul(work[places[q], :128], work[places[q], 128:], tr, -ti))
            done = fft_list(items, 1)
            for r in range(8):
                work[places[r], :128] = done[r][0]
                work[places[r], 128:] = done[r][1]

        for r in range(8):
            items = []
            for k in range(16):
                flat = 8 * (16 * r + k)
                value = (work[flat : flat + 8, :128], work[flat : flat + 8, 128:])
                items.append(cscale(value, np.conj(inner[r, k])))
            done = fft_list(items, 1)
            for c in range(16):
                flat = 8 * (16 * r + c)
                work[flat : flat + 8, :128] = done[c][0]
                work[flat : flat + 8, 128:] = done[c][1]

        @pl.loop(0, 16)
        def _(c):
            for piece in range(2):
                lanes = slice(128 * piece, 128 * piece + 128)
                for pair in range(4):
                    first = pl.ds(pl.multiple_of(8 * (32 * pair + c), 8), 8)
                    second = pl.ds(pl.multiple_of(8 * (32 * pair + 16 + c), 8), 8)
                    a = work[first, lanes]
                    b = work[second, lanes]
                    to = slice(128 * pair, 128 * pair + 128)
                    send[c, piece, top, to] = jnp.where(left, a, pltpu.roll(b, 64, 1))
                    send[c, piece, low, to] = jnp.where(left, pltpu.roll(a, 64, 1), b)

        mine = pl.ds(pl.multiple_of(col * 32 + part * 16, 16), 16)
        for i, j, k in FAR_COLS:
            tc = lax.rem(y + i, 4) * 4 + lax.rem(xl + j, 2) * 2 + lax.rem(core + k, 2)
            pltpu.make_async_remote_copy(
                send.at[tc, :, lines], out.at[:, mine],
                send_sem.at[2], recv_col.at[part], device_id=(row, tc), device_id_type=MESH,
            ).start()
        pltpu.make_async_copy(send.at[col, :, lines], out.at[:, mine], own_sem.at[part]).start()

    for part in range(2):
        settle(send.at[:15, :, :16], recv_col.at[part])
        settle(send.at[0, :, :16], own_sem.at[part])
    settle(got.at[:7], send_sem.at[0])
    settle(have.at[:127], send_sem.at[1])
    settle(send.at[:15], send_sem.at[2])


def field_step(refined):
    r_rows, r_mats = row_tables()
    c_rows, c_mats, _ = col_tables()
    return pl.pallas_call(
        field_body,
        out_shape=jax.ShapeDtypeStruct((2, STRIDE, STRIDE), F32),
        in_specs=[vmem()] * 5,
        out_specs=vmem(),
        scratch_shapes=[
            pltpu.VMEM((OVL, 2 * TILE), F32),
            pltpu.VMEM((OVL, 2 * TILE), F32),
            pltpu.VMEM((8, 64, 2 * TILE), F32),
            pltpu.VMEM((1024, 256), F32),
            pltpu.VMEM((32, 2, 64, 128), F32),
            pltpu.VMEM((128, 32, 128), F32),
            pltpu.VMEM((128, 32, 128), F32),
            pltpu.VMEM((16, 2, 32, STRIDE), F32),
            pltpu.SemaphoreType.DMA((2,)),
            pltpu.SemaphoreType.DMA((3,)),
            pltpu.SemaphoreType.DMA((4,)),
            pltpu.SemaphoreType.DMA(()),
            pltpu.SemaphoreType.DMA((2,)),
            pltpu.SemaphoreType.DMA(()),
            pltpu.SemaphoreType.DMA((2,)),
            pltpu.SemaphoreType.DMA((2,)),
        ],
        compiler_params=pltpu.CompilerParams(
            vmem_limit_bytes=60 << 20, collective_id=0, has_side_effects=True
        ),
        name="field_step",
    )(refined, r_rows, r_mats, c_rows, c_mats)


def local(tiles, pupils, intensity, offsets):
    return field_step(tile_step(tiles, pupils, intensity, offsets[0, 0]))


def solution(mesh):
    placed = (
        P(None, "row", "col"),
        P(None, "row", "col"),
        P(None, "row", "col"),
        P("row", "col", None, None),
    )
    return jax.shard_map(
        local, mesh=mesh, in_specs=placed, out_specs=P(None, "row", "col"), check_vma=False
    )
```

```python
import math

import numpy as np
import ml_dtypes
import jax
import jax.numpy as jnp
from jax import lax
from jax.experimental import pallas as pl
from jax.experimental.pallas import tpu as pltpu
from jax.sharding import PartitionSpec as P

TILE = 576
PAD = 640
OVL = 64
WIN = 128
LEDS = 16
STRIDE = 512
ROWS = 4096
COLS = 8192
FRESNEL = 2048
STEP_SIZE = 0.05
RADIX = 6
SUB = TILE // RADIX
BF = jnp.bfloat16
F32 = jnp.float32
GROUP = 4
A_LIMIT = 38
B_LIMIT = 24


def split_np(table):
    table = np.asarray(table, np.float64)
    high = table.astype(np.float32).astype(ml_dtypes.bfloat16)
    low = (table - high.astype(np.float64)).astype(np.float32).astype(ml_dtypes.bfloat16)
    return high, low


def unit(turns):
    turns = np.asarray(turns, np.float64)
    return np.exp(2j * np.pi * (turns - np.floor(turns)))


def right_block(table):
    return np.block([[table.real, table.imag], [-table.imag, table.real]])


def left_block(table):
    return np.block([[table.real, -table.imag], [table.imag, table.real]])


def dft_np(length, sign):
    index = np.arange(length)
    return unit(sign * (index[:, None] * index[None, :] % length) / length)


def axis_filter(length):
    freq = np.arange(length)
    signed = np.where(freq < length // 2, freq, freq - length).astype(np.float64)
    turns = signed * signed * (FRESNEL / (length * length))
    return np.exp(-2.0 * signed * signed / (length * length)) * unit(-turns) / length


def split(value):
    high = value.astype(BF)
    low = (value - high.astype(F32)).astype(BF)
    return high, low


def mm(left, right):
    return jnp.dot(left, right, preferred_element_type=F32)


def mm3(left, right):
    return mm(left[0], right[0]) + (mm(left[1], right[0]) + mm(left[0], right[1]))


def mm_nt(left, right):
    return lax.dot_general(left, right, (((1,), (1,)), ((), ())), preferred_element_type=F32)


def cmul(ar, ai, br, bi):
    return ar * br - ai * bi, ar * bi + ai * br


def cscale(value, factor):
    re, im = value
    fr, fi = float(factor.real), float(factor.imag)
    near = 1e-12
    if abs(fi) < near:
        if abs(fr - 1) < near:
            return re, im
        if abs(fr + 1) < near:
            return -re, -im
    if abs(fr) < near:
        if abs(fi - 1) < near:
            return -im, re
        if abs(fi + 1) < near:
            return im, -re
    if abs(abs(fr) - abs(fi)) < near:
        size = abs(fr)
        sr, si = math.copysign(1, fr), math.copysign(1, fi)
        left = re if sr > 0 else -re
        low = im if sr > 0 else -im
        new_re = left - im if si > 0 else left + im
        new_im = low + re if si > 0 else low - re
        return new_re * size, new_im * size
    return re * fr - im * fi, re * fi + im * fr


def fft_list(items, sign):
    count = len(items)
    if count == 1:
        return items
    if count == 3:
        (ar, ai), (br, bi), (cr, ci) = items
        sr, si, dr, di = br + cr, bi + ci, br - cr, bi - ci
        mr, mi = ar - 0.5 * sr, ai - 0.5 * si
        root = sign * math.sqrt(0.75)
        tr, ti = -root * di, root * dr
        return [(ar + sr, ai + si), (mr + tr, mi + ti), (mr - tr, mi - ti)]
    even = fft_list(items[0::2], sign)
    odd = fft_list(items[1::2], sign)
    half = count // 2
    first, second = [], []
    for index in range(half):
        turned = cscale(odd[index], unit(sign * index / count))
        er, ei = even[index]
        first.append((er + turned[0], ei + turned[1]))
        second.append((er - turned[0], ei - turned[1]))
    return first + second


def tile_tables():
    index = np.arange(TILE)
    low = unit(-(np.arange(24)[:, None] * index[None, :] % TILE) / TILE) / math.sqrt(TILE)
    high = unit(-(24 * np.arange(24)[:, None] * index[None, :] % TILE) / TILE)
    seeds = np.zeros((4, 24, PAD), np.float32)
    seeds[0, :, :TILE], seeds[1, :, :TILE] = low.real, low.imag
    seeds[2, :, :TILE], seeds[3, :, :TILE] = high.real, high.imag
    small = np.arange(SUB)
    forward, inverse = [], []
    for part in range(RADIX):
        turned = unit(-(part * small[:, None] + RADIX * small[:, None] * small[None, :]) / TILE)
        turned = turned / math.sqrt(TILE)
        forward.append(left_block(turned))
        inverse.append(left_block(np.conj(turned.T)))
    forward = np.stack(split_np(np.stack(forward)))
    inverse = np.stack(split_np(np.stack(inverse)))
    window = dft_np(WIN, -1) / math.sqrt(WIN)
    lanes = np.stack(
        [*split_np(right_block(np.conj(window))), *split_np(right_block(window))]
    )
    sides = np.stack(
        [*split_np(left_block(np.conj(window))), *split_np(left_block(window))]
    )
    return seeds, forward, inverse, lanes, sides


def cut(ref, part, row, first, back):
    base = pl.multiple_of((row // 8) * 8, 8)
    down = row - base
    wide = ref[part, pl.ds(base, WIN + 8), pl.ds(first, 256)]
    wide = pltpu.roll(wide, back, 1)[:, :WIN].reshape(WIN // 8 + 1, 8, WIN)
    wide = pltpu.roll(wide, lax.rem(8 - down, 8), 1)
    lane = lax.broadcasted_iota(jnp.int32, (WIN // 8, 8, WIN), 1)
    return jnp.where(lane < 8 - down, wide[:-1], wide[1:]).reshape(WIN, WIN)


def add(ref, part, row, first, shift, value):
    base = pl.multiple_of((row // 8) * 8, 8)
    down = row - base
    turned = pltpu.roll(value.reshape(WIN // 8, 8, WIN), down, 1)
    zero = jnp.zeros((1, 8, WIN), F32)
    lane = lax.broadcasted_iota(jnp.int32, (WIN // 8 + 1, 8, WIN), 1)
    upper = jnp.concatenate([zero, turned], axis=0)
    lower = jnp.concatenate([turned, zero], axis=0)
    tall = jnp.where(lane < down, upper, lower).reshape(WIN + 8, WIN)
    wide = jnp.concatenate([tall, jnp.zeros((WIN + 8, 128), F32)], axis=1)
    here = (part, pl.ds(base, WIN + 8), pl.ds(first, 256))
    ref[here] = ref[here] + pltpu.roll(wide, shift, 1)


def tile_body(
    offs, tiles_in, pupils_in, intensity_in, seeds_in, fwd_in, inv_in, lanes_in, sides_in, l_hi, l_lo, v_hi, v_lo,
    base, t_hi, t_lo, x_hi, x_lo, y, sub, spec, new, win_a, win_b,
    tiles, pupils, intensity, seeds, fwd, inv, lanes, sides, sems,
):
    sources = (seeds_in, tiles_in, fwd_in, pupils_in, intensity_in, lanes_in, sides_in, inv_in)
    targets = (seeds, tiles, fwd, pupils, intensity, lanes, sides, inv)
    loads = [
        pltpu.make_async_copy(source, target, sems.at[index])
        for index, (source, target) in enumerate(zip(sources, targets))
    ]
    for load in loads:
        load.start()
    loads[0].wait()

    low_r, low_i = seeds[0], seeds[1]

    @pl.loop(0, 24)
    def _(a):
        hr = seeds[2, pl.ds(a, 1), :]
        hi = seeds[3, pl.ds(a, 1), :]
        tr, ti = cmul(low_r, low_i, hr, hi)
        start = pl.multiple_of(a * 24, 8)
        base[0, pl.ds(start, 24), :] = tr
        base[1, pl.ds(start, 24), :] = ti

    zero_tail = jnp.zeros((PAD - TILE, 2 * PAD), BF)
    t_hi[TILE:PAD, :] = zero_tail
    t_lo[TILE:PAD, :] = zero_tail
    t_hi[PAD + TILE :, :] = zero_tail
    t_lo[PAD + TILE :, :] = zero_tail

    @pl.loop(0, TILE // 96)
    def _(a):
        start = pl.multiple_of(a * 96, 16)
        ch, cl = split(base[0, pl.ds(start, 96), :])
        sh, sl = split(base[1, pl.ds(start, 96), :])
        t_hi[pl.ds(start, 96), :PAD] = ch
        t_lo[pl.ds(start, 96), :PAD] = cl
        t_hi[pl.ds(start, 96), PAD:] = sh
        t_lo[pl.ds(start, 96), PAD:] = sl
        l_hi[pl.ds(start, 96), :PAD] = ch
        l_lo[pl.ds(start, 96), :PAD] = cl
        l_hi[pl.ds(start, 96), PAD:] = sh
        l_lo[pl.ds(start, 96), PAD:] = sl
        t_hi[pl.ds(start + PAD, 96), :PAD] = -sh
        t_lo[pl.ds(start + PAD, 96), :PAD] = -sl
        t_hi[pl.ds(start + PAD, 96), PAD:] = ch
        t_lo[pl.ds(start + PAD, 96), PAD:] = cl

    loads[1].wait()
    x_hi[...] = jnp.zeros_like(x_hi)
    x_lo[...] = jnp.zeros_like(x_lo)

    @pl.loop(0, TILE // 96)
    def _(a):
        start = pl.multiple_of(a * 96, 16)
        for part in range(2):
            high, low = split(tiles[part, pl.ds(start, 96), :])
            x_hi[pl.ds(start, 96), part * PAD : part * PAD + TILE] = high
            x_lo[pl.ds(start, 96), part * PAD : part * PAD + TILE] = low

    @pl.loop(0, 2 * PAD // 256)
    def _(n):
        at = pl.ds(pl.multiple_of(n * 256, 256), 256)
        both = mm3((x_hi[...], x_lo[...]), (t_hi[:, at], t_lo[:, at]))
        y[2 * n] = both[:, :128]
        y[2 * n + 1] = both[:, 128:]

    loads[2].wait()

    @pl.loop(0, RADIX)
    def _(b):
        rows = pl.ds(b, SUB, stride=RADIX)
        parts = [
            jnp.concatenate([y[n, rows, :] for n in range(5 * part, 5 * part + 5)], axis=1)
            for part in range(2)
        ]
        sub[b] = mm3((fwd[0, b], fwd[1, b]), split(jnp.concatenate(parts, axis=0)))

    @pl.loop(0, PAD // 128)
    def _(n):
        at = pl.ds(pl.multiple_of(n * 128, 128), 128)
        for row in range(0, SUB, 8):
            items = [
                (sub[b, row : row + 8, at], sub[b, SUB + row : SUB + row + 8, at])
                for b in range(RADIX)
            ]
            done = fft_list(items, -1)
            for k in range(RADIX):
                here = slice(k * SUB + row, k * SUB + row + 8)
                spec[0, here, at] = done[k][0]
                spec[1, here, at] = done[k][1]
                new[0, here, at] = done[k][0]
                new[1, here, at] = done[k][1]

    for ref in (spec, new):
        for part in range(2):
            ref[part, TILE:, :] = jnp.zeros((8, PAD), F32)
    for load in loads[3:]:
        load.wait()
    pr, pi = pupils[0], pupils[1]
    inv_lanes = (lanes[0], lanes[1])
    fwd_lanes = (lanes[2], lanes[3])
    inv_sides = (sides[0], sides[1])
    fwd_sides = (sides[2], sides[3])

    @pl.loop(0, LEDS // GROUP)
    def _(step):
        for j in range(GROUP):
            led = step * GROUP + j
            row, col = offs[0, led], offs[1, led]
            first = pl.multiple_of((col // 128) * 128, 128)
            shift = col - first
            back = lax.rem(256 - shift, 256)
            cr = cut(spec, 0, row, first, back)
            ci = cut(spec, 1, row, first, back)
            wr, wi = cmul(pr, pi, cr, ci)
            win_a[:WIN, j * WIN : (j + 1) * WIN] = wr
            win_a[WIN:, j * WIN : (j + 1) * WIN] = wi
        side = mm3(inv_sides, split(win_a[...]))
        for j in range(GROUP):
            win_b[j * WIN : (j + 1) * WIN, :WIN] = side[:WIN, j * WIN : (j + 1) * WIN]
            win_b[j * WIN : (j + 1) * WIN, WIN:] = side[WIN:, j * WIN : (j + 1) * WIN]
        wave = mm3(split(win_b[...]), inv_lanes)
        for j in range(GROUP):
            wr = wave[j * WIN : (j + 1) * WIN, :WIN]
            wi = wave[j * WIN : (j + 1) * WIN, WIN:]
            excess = wr * wr + wi * wi - intensity[step * GROUP + j]
            win_b[j * WIN : (j + 1) * WIN, :WIN] = wr * excess
            win_b[j * WIN : (j + 1) * WIN, WIN:] = wi * excess
        grad = mm3(split(win_b[...]), fwd_lanes)
        for j in range(GROUP):
            win_a[:WIN, j * WIN : (j + 1) * WIN] = grad[j * WIN : (j + 1) * WIN, :WIN]
            win_a[WIN:, j * WIN : (j + 1) * WIN] = grad[j * WIN : (j + 1) * WIN, WIN:]
        win_a[...] = mm3(fwd_sides, split(win_a[...]))
        for j in range(GROUP):
            led = step * GROUP + j
            row, col = offs[0, led], offs[1, led]
            first = pl.multiple_of((col // 128) * 128, 128)
            shift = col - first
            gr = win_a[:WIN, j * WIN : (j + 1) * WIN] * -STEP_SIZE
            gi = win_a[WIN:, j * WIN : (j + 1) * WIN] * -STEP_SIZE
            ur, ui = cmul(pr, -pi, gr, gi)
            add(new, 0, row, first, shift, ur)
            add(new, 1, row, first, shift, ui)

    @pl.loop(0, PAD // 128)
    def _(n):
        at = pl.ds(pl.multiple_of(n * 128, 128), 128)
        for row in range(0, SUB, 8):
            items = []
            for k in range(RADIX):
                here = slice(k * SUB + row, k * SUB + row + 8)
                items.append((new[0, here, at], new[1, here, at]))
            done = fft_list(items, 1)
            for b in range(RADIX):
                sub[b, row : row + 8, at] = done[b][0]
                sub[b, SUB + row : SUB + row + 8, at] = done[b][1]

    @pl.loop(0, RADIX)
    def _(b):
        mixed = mm3((inv[0, b], inv[1, b]), split(sub[b]))
        rows = pl.ds(b, SUB, stride=RADIX)
        for n in range(5):
            y[n, rows, :] = mixed[:SUB, 128 * n : 128 * n + 128]
            y[5 + n, rows, :] = mixed[SUB:, 128 * n : 128 * n + 128]

    def put(start, count, real_at, imag_at):
        for n in range(5):
            rh, rl = split(y[n, start : start + count, :])
            ih, il = split(y[5 + n, start : start + count, :])
            left, right = slice(128 * n, 128 * n + 128), slice(PAD + 128 * n, PAD + 128 * n + 128)
            a = slice(real_at, real_at + count)
            v_hi[a, left], v_hi[a, right] = rh, ih
            v_lo[a, left], v_lo[a, right] = rl, il
            b = slice(imag_at, imag_at + count)
            v_hi[b, left], v_hi[b, right] = ih, -rh
            v_lo[b, left], v_lo[b, right] = il, -rl

    put(0, STRIDE, 0, STRIDE)
    put(STRIDE, OVL, 2 * STRIDE, 2 * STRIDE + OVL)


def vmem():
    return pl.BlockSpec(memory_space=pltpu.VMEM)


def tile_step(tiles, pupils, intensity, offsets):
    seeds, fwd, inv, lanes, sides = tile_tables()
    return pl.pallas_call(
        tile_body,
        out_shape=[
            jax.ShapeDtypeStruct((TILE, 2 * PAD), BF),
            jax.ShapeDtypeStruct((TILE, 2 * PAD), BF),
            jax.ShapeDtypeStruct((2 * TILE, 2 * PAD), BF),
            jax.ShapeDtypeStruct((2 * TILE, 2 * PAD), BF),
        ],
        in_specs=[pl.BlockSpec(memory_space=pltpu.SMEM)]
        + [pl.BlockSpec(memory_space=pltpu.HBM)] * 8,
        out_specs=[vmem()] * 4,
        scratch_shapes=[
            pltpu.VMEM((2, TILE, PAD), F32),
            pltpu.VMEM((2 * PAD, 2 * PAD), BF),
            pltpu.VMEM((2 * PAD, 2 * PAD), BF),
            pltpu.VMEM((TILE, 2 * PAD), BF),
            pltpu.VMEM((TILE, 2 * PAD), BF),
            pltpu.VMEM((2 * PAD // 128, TILE, 128), F32),
            pltpu.VMEM((RADIX, 2 * SUB, PAD), F32),
            pltpu.VMEM((2, TILE + 8, PAD), F32),
            pltpu.VMEM((2, TILE + 8, PAD), F32),
            pltpu.VMEM((2 * WIN, GROUP * WIN), F32),
            pltpu.VMEM((GROUP * WIN, 2 * WIN), F32),
            *[
                pltpu.VMEM(value.shape, value.dtype)
                for value in (tiles, pupils, intensity, seeds, fwd, inv, lanes, sides)
            ],
            pltpu.SemaphoreType.DMA((8,)),
        ],
        compiler_params=pltpu.CompilerParams(vmem_limit_bytes=A_LIMIT << 20),
        name="tile_step",
    )(
        offsets,
        *[
            pltpu.with_memory_space_constraint(jnp.asarray(value), pltpu.HBM)
            for value in (tiles, pupils, intensity, seeds, fwd, inv, lanes, sides)
        ],
    )


def row_tables():
    lane = np.arange(128)
    k1 = np.arange(32)
    turn = unit(-(k1[:, None] * lane[None, :]) / ROWS)
    keep = axis_filter(ROWS)[k1[:, None] + 32 * lane[None, :]]
    rows = np.stack([turn.real, turn.imag, keep.real, keep.imag]).astype(np.float32)
    full = dft_np(128, -1)
    mats = np.stack([*split_np(right_block(full)), *split_np(right_block(np.conj(full)))])
    return rows, mats


def col_tables():
    lane = np.arange(64)
    kc = np.arange(16)
    kr = np.arange(8)
    low = kc[None, :] + 16 * kr[:, None]
    turn = unit(-(low[:, :, None] * lane) / COLS)
    keep = axis_filter(COLS)[low[:, :, None] + 128 * lane]
    rows = np.stack([turn.real, turn.imag, keep.real, keep.imag]).reshape(4, 128, 64)
    rows = np.concatenate([rows, rows], axis=2).astype(np.float32)
    inner = unit(-(np.arange(8)[:, None] * kc[None, :]) / 128)
    full = np.kron(np.eye(2), dft_np(64, -1))
    mats = np.stack([*split_np(right_block(full)), *split_np(right_block(np.conj(full)))])
    return rows, mats, inner


MESH = pl.DeviceIdType.MESH
FAR_ROWS = ((1, 2), (1, 1), (1, 3), (0, 2), (1, 0), (0, 1), (0, 3))
FAR_COLS = sorted(
    ((y, x, k) for y in range(4) for x in range(2) for k in range(2) if y or x or k),
    key=lambda step: -(min(step[0], 4 - step[0]) + step[1]),
)
QUARTER = 16


def settle(ref, sem):
    pltpu.make_async_copy(ref, ref, sem).wait()


def field_body(
    l_hi, l_lo, v_hi, v_lo, r_rows, r_mats, c_rows, c_mats, out,
    refined, halo, front, got, work, mid, give, have, send,
    halo_sem, send_sem, recv_row, own_row, recv_all, own_all, recv_col, own_sem,
):
    row, col = lax.axis_index("row"), lax.axis_index("col")
    xh, z = row // 4, lax.rem(row, 4)
    y, xl, core = col // 4, lax.rem(col // 2, 2), lax.rem(col, 2)
    rows_at = [lax.rem(row + step, 8) for step in range(8)]
    cols_at = [lax.rem(col + step, 16) for step in range(16)]

    barrier = pltpu.get_barrier_semaphore()
    for i in range(8):
        for j in range(16):
            if i or j:
                pl.semaphore_signal(
                    barrier, inc=1, device_id=(rows_at[i], cols_at[j]), device_id_type=MESH
                )

    chunks = [lax.rem(xh + i, 2) * 4 + lax.rem(z + j, 4) for i, j in FAR_ROWS]

    def columns_of(blocks):
        places = [pl.ds(pl.multiple_of(block * 64, 64), 64) for block in blocks]

        def fill(at):
            high = jnp.concatenate([l_hi[place, :] for place in places], axis=0)
            low = jnp.concatenate([l_lo[place, :] for place in places], axis=0)
            righl_high, righl_low = v_hi[at, :], v_lo[at, :]
            value = mm_nt(high, righl_high) + (mm_nt(low, righl_high) + mm_nt(high, righl_low))
            for index, place in enumerate(places):
                refined[place, at] = value[64 * index : 64 * index + 64]

        @pl.loop(0, 4)
        def _(n):
            fill(pl.ds(pl.multiple_of(n * 256, 256), 256))

        fill(slice(1024, 1152))

    columns_of([8, *chunks[:2]])
    pl.semaphore_wait(barrier, 127)

    edge = pltpu.make_async_remote_copy(
        refined.at[STRIDE:], halo, halo_sem.at[0], halo_sem.at[1],
        device_id=(row, cols_at[1]), device_id_type=MESH,
    )
    edge.start()

    def give_row(target, quarter, source):
        pltpu.make_async_remote_copy(
            source, got.at[row, quarter * QUARTER : (quarter + 1) * QUARTER],
            send_sem.at[0], recv_row.at[quarter], device_id=(target, col), device_id_type=MESH,
        ).start()

    def plain(target, quarter):
        start = pl.multiple_of(target * 64 + quarter * QUARTER, QUARTER)
        return refined.at[pl.ds(start, QUARTER)]

    def blended(quarter):
        return front.at[quarter * QUARTER : (quarter + 1) * QUARTER]

    def give_plain(targets):
        for target in targets:
            @pl.when(target != 0)
            def _():
                give_row(target, 0, plain(target, 0))

    give_plain(chunks[:2])
    columns_of(chunks[2:5])
    give_plain(chunks[2:5])
    columns_of([*chunks[5:], row])
    give_plain(chunks[5:])

    edge.wait()
    place = lax.broadcasted_iota(jnp.int32, (OVL, 2 * TILE), 0).astype(F32)
    ramp = (place + 0.5) / OVL
    front[...] = ramp * refined[:OVL] + (1.0 - ramp) * halo[...]

    for target in chunks:
        @pl.when(target == 0)
        def _():
            give_row(target, 0, blended(0))

    for quarter in range(1, 4):
        for target in chunks:
            @pl.when(target != 0)
            def _():
                give_row(target, quarter, plain(target, quarter))

            @pl.when(target == 0)
            def _():
                give_row(target, quarter, blended(quarter))

    @pl.when(row == 0)
    def _():
        pltpu.make_async_copy(front, got.at[0], own_row).start()

    @pl.when(row != 0)
    def _():
        start = pl.multiple_of(row * 64, 64)
        pltpu.make_async_copy(refined.at[pl.ds(start, 64)], got.at[row], own_row).start()

    settle(front, own_row)

    lane = lax.broadcasted_iota(jnp.int32, (8, 128), 1)
    slope = jnp.where(lane < OVL, (lane.astype(F32) + 0.5) / OVL, 1.0)
    rest = jnp.where(lane < OVL, 1.0 - slope, 0.0)

    @pl.loop(0, 4)
    def _(quarter):
        columns = pl.ds(pl.multiple_of(quarter * QUARTER, QUARTER), QUARTER)
        settle(got.at[:7, columns], recv_row.at[quarter])

        @pl.loop(0, 2)
        def _(half):
            at = pl.ds(pl.multiple_of(quarter * QUARTER + half * 8, 8), 8)
            for a in range(4):
                items = []
                for p in range(8):
                    re = got[p, at, 128 * a : 128 * a + 128]
                    im = got[p, at, STRIDE + 128 * a : STRIDE + 128 * a + 128]
                    if a == 0:
                        tail = got[(p - 1) % 8, at, 2 * STRIDE :]
                        re = slope * re + rest * tail
                        im = slope * im + rest * pltpu.roll(tail, 64, 1)
                    items.append((re, im))
                done = fft_list(items, -1)
                for k in range(8):
                    re, im = cscale(done[k], unit(-a * k / 32))
                    mid[4 * k + a, 0, at, :] = re
                    mid[4 * k + a, 1, at, :] = im

            @pl.loop(0, 8)
            def _(k):
                items = [(mid[4 * k + a, 0, at, :], mid[4 * k + a, 1, at, :]) for a in range(4)]
                done = fft_list(items, -1)
                for q in range(4):
                    index = k + 8 * q
                    tr = r_rows[0, pl.ds(index, 1), :]
                    ti = r_rows[1, pl.ds(index, 1), :]
                    re, im = cmul(*done[q], tr, ti)
                    start = pl.ds(pl.multiple_of(index * QUARTER + half * 8, 8), 8)
                    work[start, :128] = re
                    work[start, 128:] = im

        full = mm3(split(work[:512]), (r_mats[0], r_mats[1]))
        full = full.reshape(32, QUARTER, 256)
        kr, ki = r_rows[2][:, None, :], r_rows[3][:, None, :]
        re, im = cmul(full[:, :, :128], full[:, :, 128:], kr, ki)
        both = jnp.concatenate([re, im], axis=2).reshape(512, 256)
        work[:512] = mm3(split(both), (r_mats[2], r_mats[3]))

        @pl.loop(0, 2)
        def _(half):
            at = pl.ds(pl.multiple_of(quarter * QUARTER + half * 8, 8), 8)

            @pl.loop(0, 8)
            def _(k):
                items = []
                for q in range(4):
                    index = k + 8 * q
                    tr = r_rows[0, pl.ds(index, 1), :]
                    ti = r_rows[1, pl.ds(index, 1), :]
                    start = pl.ds(pl.multiple_of(index * QUARTER + half * 8, 8), 8)
                    items.append(cmul(work[start, :128], work[start, 128:], tr, -ti))
                done = fft_list(items, 1)
                for a in range(4):
                    mid[4 * k + a, 0, at, :] = done[a][0]
                    mid[4 * k + a, 1, at, :] = done[a][1]

            for a in range(4):
                items = [
                    cscale((mid[4 * k + a, 0, at, :], mid[4 * k + a, 1, at, :]), unit(a * k / 32))
                    for k in range(8)
                ]
                done = fft_list(items, 1)
                for p in range(8):
                    mid[4 * p + a, 0, at, :] = done[p][0]
                    mid[4 * p + a, 1, at, :] = done[p][1]

    me = row * 16 + col

    def peers(step):
        tr = lax.rem(xh + 1 + step // 16, 2) * 4 + lax.rem(z + 2 + (step // 4) % 4, 4)
        ty = lax.rem(y + 2 + step % 4, 4)
        ends = []
        for i in range(2):
            for j in range(2):
                ends.append((tr, ty * 4 + lax.rem(xl + i, 2) * 2 + lax.rem(core + j, 2)))
        return tr * 4 + ty, ends

    own_step = 26

    def give_all(step, ends, part):
        lines = slice(part * 16, part * 16 + 16)
        for index, (tr, tc) in enumerate(ends):
            def go(tr=tr, tc=tc):
                pltpu.make_async_remote_copy(
                    give.at[tr * 16 + tc, lines], have.at[me, lines],
                    send_sem.at[1], recv_all.at[part], device_id=(tr, tc), device_id_type=MESH,
                ).start()

            if index:
                go()
            else:
                pl.when(step != own_step)(go)

    @pl.loop(0, 32)
    def _(step):
        block, ends = peers(step)
        flat = jnp.transpose(mid[block].reshape(128, 128))
        for i in range(4):
            give[block * 4 + i] = flat[32 * i : 32 * i + 32]
        give_all(step, ends, 0)

    own = pltpu.make_async_copy(give.at[me], have.at[me], own_all)
    own.start()

    @pl.loop(0, 32)
    def _(step):
        give_all(step, peers(step)[1], 1)

    own.wait()

    left = lane < 64
    inner = col_tables()[2]

    @pl.loop(0, 2)
    def _(part):
        lines = pl.ds(pl.multiple_of(part * 16, 16), 16)
        top = pl.ds(pl.multiple_of(part * 16, 8), 8)
        low = pl.ds(pl.multiple_of(part * 16 + 8, 8), 8)
        settle(have.at[:127, lines], recv_all.at[part])

        for r in range(8):
            items = []
            for c in range(16):
                a = have[16 * r + c, top, :]
                b = have[16 * r + c, low, :]
                re = jnp.where(left, a, pltpu.roll(b, 64, 1))
                im = jnp.where(left, pltpu.roll(a, 64, 1), b)
                items.append((re, im))
            done = fft_list(items, -1)
            for k in range(16):
                flat = 8 * (16 * r + k)
                re, im = cscale(done[k], inner[r, k])
                work[flat : flat + 8, :128] = re
                work[flat : flat + 8, 128:] = im

        @pl.loop(0, 16)
        def _(k):
            places = [pl.ds(pl.multiple_of(8 * (16 * r + k), 8), 8) for r in range(8)]
            items = [(work[at, :128], work[at, 128:]) for at in places]
            done = fft_list(items, -1)
            for q in range(8):
                tr = c_rows[0, pl.ds(16 * q + k, 1), :]
                ti = c_rows[1, pl.ds(16 * q + k, 1), :]
                re, im = cmul(*done[q], tr, ti)
                work[places[q], :128] = re
                work[places[q], 128:] = im

        @pl.loop(0, 2)
        def _(n):
            at = pl.ds(pl.multiple_of(n * 512, 512), 512)
            keep = pl.ds(pl.multiple_of(n * 64, 64), 64)
            full = mm3(split(work[at, :]), (c_mats[0], c_mats[1]))
            full = full.reshape(64, 8, 256)
            kr, ki = c_rows[2, keep, :][:, None, :], c_rows[3, keep, :][:, None, :]
            re, im = cmul(full[:, :, :128], full[:, :, 128:], kr, ki)
            both = jnp.concatenate([re, im], axis=2).reshape(512, 256)
            work[at, :] = mm3(split(both), (c_mats[2], c_mats[3]))

        @pl.loop(0, 16)
        def _(k):
            places = [pl.ds(pl.multiple_of(8 * (16 * r + k), 8), 8) for r in range(8)]
            items = []
            for q in range(8):
                tr = c_rows[0, pl.ds(16 * q + k, 1), :]
                ti = c_rows[1, pl.ds(16 * q + k, 1), :]
                items.append(cmul(work[places[q], :128], work[places[q], 128:], tr, -ti))
            done = fft_list(items, 1)
            for r in range(8):
                work[places[r], :128] = done[r][0]
                work[places[r], 128:] = done[r][1]

        for r in range(8):
            items = []
            for k in range(16):
                flat = 8 * (16 * r + k)
                value = (work[flat : flat + 8, :128], work[flat : flat + 8, 128:])
                items.append(cscale(value, np.conj(inner[r, k])))
            done = fft_list(items, 1)
            for c in range(16):
                flat = 8 * (16 * r + c)
                work[flat : flat + 8, :128] = done[c][0]
                work[flat : flat + 8, 128:] = done[c][1]

        @pl.loop(0, 16)
        def _(c):
            for piece in range(2):
                lanes = slice(128 * piece, 128 * piece + 128)
                for pair in range(4):
                    first = pl.ds(pl.multiple_of(8 * (32 * pair + c), 8), 8)
                    second = pl.ds(pl.multiple_of(8 * (32 * pair + 16 + c), 8), 8)
                    a = work[first, lanes]
                    b = work[second, lanes]
                    to = slice(128 * pair, 128 * pair + 128)
                    send[c, piece, top, to] = jnp.where(left, a, pltpu.roll(b, 64, 1))
                    send[c, piece, low, to] = jnp.where(left, pltpu.roll(a, 64, 1), b)

        mine = pl.ds(pl.multiple_of(col * 32 + part * 16, 16), 16)
        for i, j, k in FAR_COLS:
            tc = lax.rem(y + i, 4) * 4 + lax.rem(xl + j, 2) * 2 + lax.rem(core + k, 2)
            pltpu.make_async_remote_copy(
                send.at[tc, :, lines], out.at[:, mine],
                send_sem.at[2], recv_col.at[part], device_id=(row, tc), device_id_type=MESH,
            ).start()
        pltpu.make_async_copy(send.at[col, :, lines], out.at[:, mine], own_sem.at[part]).start()

    for part in range(2):
        settle(send.at[:15, :, :16], recv_col.at[part])
        settle(send.at[0, :, :16], own_sem.at[part])
    settle(got.at[:7], send_sem.at[0])
    settle(have.at[:127], send_sem.at[1])
    settle(send.at[:15], send_sem.at[2])


def field_step(l_hi, l_lo, v_hi, v_lo):
    r_rows, r_mats = row_tables()
    c_rows, c_mats, _ = col_tables()
    return pl.pallas_call(
        field_body,
        out_shape=jax.ShapeDtypeStruct((2, STRIDE, STRIDE), F32),
        in_specs=[vmem()] * 8,
        out_specs=vmem(),
        scratch_shapes=[
            pltpu.VMEM((TILE, 2 * TILE), F32),
            pltpu.VMEM((OVL, 2 * TILE), F32),
            pltpu.VMEM((OVL, 2 * TILE), F32),
            pltpu.VMEM((8, 64, 2 * TILE), F32),
            pltpu.VMEM((1024, 256), F32),
            pltpu.VMEM((32, 2, 64, 128), F32),
            pltpu.VMEM((128, 32, 128), F32),
            pltpu.VMEM((128, 32, 128), F32),
            pltpu.VMEM((16, 2, 32, STRIDE), F32),
            pltpu.SemaphoreType.DMA((2,)),
            pltpu.SemaphoreType.DMA((3,)),
            pltpu.SemaphoreType.DMA((4,)),
            pltpu.SemaphoreType.DMA(()),
            pltpu.SemaphoreType.DMA((2,)),
            pltpu.SemaphoreType.DMA(()),
            pltpu.SemaphoreType.DMA((2,)),
            pltpu.SemaphoreType.DMA((2,)),
        ],
        compiler_params=pltpu.CompilerParams(
            vmem_limit_bytes=B_LIMIT << 20, collective_id=0, has_side_effects=True
        ),
        name="field_step",
    )(l_hi, l_lo, v_hi, v_lo, r_rows, r_mats, c_rows, c_mats)


def local(tiles, pupils, intensity, offsets):
    return field_step(*tile_step(tiles, pupils, intensity, offsets[0, 0]))


def solution(mesh):
    placed = (
        P(None, "row", "col"),
        P(None, "row", "col"),
        P(None, "row", "col"),
        P("row", "col", None, None),
    )
    return jax.shard_map(
        local, mesh=mesh, in_specs=placed, out_specs=P(None, "row", "col"), check_vma=False
    )
```

```python
import math

import numpy as np
import ml_dtypes
import jax
import jax.numpy as jnp
from jax import lax
from jax.experimental import pallas as pl
from jax.experimental.pallas import tpu as pltpu
from jax.sharding import PartitionSpec as P

TILE = 576
PAD = 640
OVL = 64
WIN = 128
LEDS = 16
STRIDE = 512
ROWS = 4096
COLS = 8192
FRESNEL = 2048
STEP_SIZE = 0.05
RADIX = 6
SUB = TILE // RADIX
BF = jnp.bfloat16
F32 = jnp.float32
GROUP = 4
A_LIMIT = 38
B_LIMIT = 24


def split_np(table):
    table = np.asarray(table, np.float64)
    high = table.astype(np.float32).astype(ml_dtypes.bfloat16)
    low = (table - high.astype(np.float64)).astype(np.float32).astype(ml_dtypes.bfloat16)
    return high, low


def unit(turns):
    turns = np.asarray(turns, np.float64)
    return np.exp(2j * np.pi * (turns - np.floor(turns)))


def right_block(table):
    return np.block([[table.real, table.imag], [-table.imag, table.real]])


def left_block(table):
    return np.block([[table.real, -table.imag], [table.imag, table.real]])


def dft_np(length, sign):
    index = np.arange(length)
    return unit(sign * (index[:, None] * index[None, :] % length) / length)


def axis_filter(length):
    freq = np.arange(length)
    signed = np.where(freq < length // 2, freq, freq - length).astype(np.float64)
    turns = signed * signed * (FRESNEL / (length * length))
    return np.exp(-2.0 * signed * signed / (length * length)) * unit(-turns) / length


def split(value):
    high = value.astype(BF)
    low = (value - high.astype(F32)).astype(BF)
    return high, low


def mm(left, right):
    return jnp.dot(left, right, preferred_element_type=F32)


def mm3(left, right):
    return mm(left[0], right[0]) + (mm(left[1], right[0]) + mm(left[0], right[1]))


def mm_nt(left, right):
    return lax.dot_general(left, right, (((1,), (1,)), ((), ())), preferred_element_type=F32)


def cmul(ar, ai, br, bi):
    return ar * br - ai * bi, ar * bi + ai * br


def cscale(value, factor):
    re, im = value
    fr, fi = float(factor.real), float(factor.imag)
    near = 1e-12
    if abs(fi) < near:
        if abs(fr - 1) < near:
            return re, im
        if abs(fr + 1) < near:
            return -re, -im
    if abs(fr) < near:
        if abs(fi - 1) < near:
            return -im, re
        if abs(fi + 1) < near:
            return im, -re
    if abs(abs(fr) - abs(fi)) < near:
        size = abs(fr)
        sr, si = math.copysign(1, fr), math.copysign(1, fi)
        left = re if sr > 0 else -re
        low = im if sr > 0 else -im
        new_re = left - im if si > 0 else left + im
        new_im = low + re if si > 0 else low - re
        return new_re * size, new_im * size
    return re * fr - im * fi, re * fi + im * fr


def fft_list(items, sign):
    count = len(items)
    if count == 1:
        return items
    if count == 3:
        (ar, ai), (br, bi), (cr, ci) = items
        sr, si, dr, di = br + cr, bi + ci, br - cr, bi - ci
        mr, mi = ar - 0.5 * sr, ai - 0.5 * si
        root = sign * math.sqrt(0.75)
        tr, ti = -root * di, root * dr
        return [(ar + sr, ai + si), (mr + tr, mi + ti), (mr - tr, mi - ti)]
    even = fft_list(items[0::2], sign)
    odd = fft_list(items[1::2], sign)
    half = count // 2
    first, second = [], []
    for index in range(half):
        turned = cscale(odd[index], unit(sign * index / count))
        er, ei = even[index]
        first.append((er + turned[0], ei + turned[1]))
        second.append((er - turned[0], ei - turned[1]))
    return first + second


def tile_tables():
    index = np.arange(TILE)
    low = unit(-(np.arange(24)[:, None] * index[None, :] % TILE) / TILE) / math.sqrt(TILE)
    high = unit(-(24 * np.arange(24)[:, None] * index[None, :] % TILE) / TILE)
    seeds = np.zeros((4, 24, PAD), np.float32)
    seeds[0, :, :TILE], seeds[1, :, :TILE] = low.real, low.imag
    seeds[2, :, :TILE], seeds[3, :, :TILE] = high.real, high.imag
    small = np.arange(SUB)
    forward, inverse = [], []
    for part in range(RADIX):
        turned = unit(-(part * small[:, None] + RADIX * small[:, None] * small[None, :]) / TILE)
        turned = turned / math.sqrt(TILE)
        forward.append(left_block(turned))
        inverse.append(left_block(np.conj(turned.T)))
    forward = np.stack(split_np(np.stack(forward)))
    inverse = np.stack(split_np(np.stack(inverse)))
    window = dft_np(WIN, -1) / math.sqrt(WIN)
    lanes = np.stack(split_np(right_block(np.conj(window))))
    sides = np.stack(
        [*split_np(left_block(np.conj(window))), *split_np(left_block(window))]
    )
    return seeds, forward, inverse, lanes, sides


def cut(ref, part, row, first, back):
    base = pl.multiple_of((row // 8) * 8, 8)
    down = row - base
    wide = ref[part, pl.ds(base, WIN + 8), pl.ds(first, 256)]
    wide = pltpu.roll(wide, back, 1)[:, :WIN].reshape(WIN // 8 + 1, 8, WIN)
    wide = pltpu.roll(wide, lax.rem(8 - down, 8), 1)
    lane = lax.broadcasted_iota(jnp.int32, (WIN // 8, 8, WIN), 1)
    return jnp.where(lane < 8 - down, wide[:-1], wide[1:]).reshape(WIN, WIN)


def add(ref, part, row, first, shift, value):
    base = pl.multiple_of((row // 8) * 8, 8)
    down = row - base
    turned = pltpu.roll(value.reshape(WIN // 8, 8, WIN), down, 1)
    zero = jnp.zeros((1, 8, WIN), F32)
    lane = lax.broadcasted_iota(jnp.int32, (WIN // 8 + 1, 8, WIN), 1)
    upper = jnp.concatenate([zero, turned], axis=0)
    lower = jnp.concatenate([turned, zero], axis=0)
    tall = jnp.where(lane < down, upper, lower).reshape(WIN + 8, WIN)
    wide = jnp.concatenate([tall, jnp.zeros((WIN + 8, 128), F32)], axis=1)
    here = (part, pl.ds(base, WIN + 8), pl.ds(first, 256))
    ref[here] = ref[here] + pltpu.roll(wide, shift, 1)


def tile_body(
    offs, tiles_in, pupils_in, intensity_in, seeds_in, fwd_in, inv_in, lanes_in, sides_in,
    z_hi, z_lo, r_hi, r_lo,
    base, y, sub, spec, new, win_a, win_b, turned,
    tiles, raw, pupils, intensity, seeds, fwd, inv, lanes, sides, sems,
):
    pairs = [(seeds_in, seeds), (tiles_in, raw), (fwd_in, fwd)]
    pairs += [(pupils_in, pupils), (intensity_in, intensity)]
    pairs += [(lanes_in, lanes), (sides_in, sides), (inv_in, inv)]
    loads = [
        pltpu.make_async_copy(source, target, sems.at[index])
        for index, (source, target) in enumerate(pairs)
    ]
    for load in loads:
        load.start()
    loads[0].wait()

    low_r, low_i = seeds[0], seeds[1]

    @pl.loop(0, 24)
    def _(a):
        hr = seeds[2, pl.ds(a, 1), :]
        hi = seeds[3, pl.ds(a, 1), :]
        tr, ti = cmul(low_r, low_i, hr, hi)
        start = pl.multiple_of(a * 24, 8)
        base[0, pl.ds(start, 24), :] = tr
        base[1, pl.ds(start, 24), :] = ti

    for ref in (r_hi, r_lo):
        zero_tail = jnp.zeros((PAD - TILE, 2 * TILE), BF)
        ref[TILE:PAD, :] = zero_tail
        ref[PAD + TILE :, :] = zero_tail

    @pl.loop(0, TILE // 96)
    def _(a):
        start = pl.multiple_of(a * 96, 16)
        re, im = base[0, pl.ds(start, 96), :], base[1, pl.ds(start, 96), :]
        for offset, left, right in ((0, re, -im), (PAD, im, re)):
            at = pl.ds(start + offset, 96)
            ends = left[:, STRIDE:] + pltpu.roll(right[:, STRIDE:], 64, 1)
            for where, value in (
                (slice(0, STRIDE), left[:, :STRIDE]),
                (slice(STRIDE, 2 * STRIDE), right[:, :STRIDE]),
                (slice(2 * STRIDE, 2 * TILE), ends),
            ):
                high, low = split(value)
                r_hi[at, where] = high
                r_lo[at, where] = low

    def forward(targets):
        @pl.loop(0, RADIX)
        def _(b):
            rows = pl.ds(b, SUB, stride=RADIX)
            parts = [
                jnp.concatenate([tiles[part, n, rows, :] for n in range(5)], axis=1)
                for part in range(2)
            ]
            sub[b] = mm3((fwd[0, b], fwd[1, b]), split(jnp.concatenate(parts, axis=0)))

        @pl.loop(0, PAD // 128)
        def _(n):
            at = pl.ds(pl.multiple_of(n * 128, 128), 128)
            for row in range(0, SUB, 8):
                items = [
                    (sub[b, row : row + 8, at], sub[b, SUB + row : SUB + row + 8, at])
                    for b in range(RADIX)
                ]
                done = fft_list(items, -1)
                for k in range(RADIX):
                    here = slice(k * SUB + row, k * SUB + row + 8)
                    for ref in targets:
                        ref[0, here, at] = done[k][0]
                        ref[1, here, at] = done[k][1]

    loads[1].wait()
    for part in range(2):
        for n in range(5):
            width = min(128, TILE - 128 * n)
            tiles[part, n, :, :width] = raw[part, :, 128 * n : 128 * n + width]
    loads[2].wait()
    forward((spec,))

    def flip(part, at, count, to):
        for i in range(4):
            block = jnp.transpose(spec[part, 128 * i : 128 * i + 128, at])
            tiles[part, i, to, :] = block[:count]
        half = jnp.concatenate([spec[part, STRIDE:TILE, at], jnp.zeros((64, 128), F32)], axis=0)
        tiles[part, 4, to, :] = jnp.transpose(half)[:count]

    for part in range(2):
        @pl.loop(0, 4)
        def _(j):
            at = pl.ds(pl.multiple_of(j * 128, 128), 128)
            flip(part, at, 128, at)

        flip(part, slice(STRIDE, PAD), 64, slice(STRIDE, TILE))

    forward((spec, new))

    for ref in (spec, new):
        for part in range(2):
            ref[part, TILE:, :] = jnp.zeros((8, PAD), F32)
    for load in loads[3:]:
        load.wait()
    for part in range(2):
        turned[part] = jnp.transpose(pupils[part])
    inv_lanes = (lanes[0], lanes[1])
    inv_sides = (sides[0], sides[1])
    fwd_sides = (sides[2], sides[3])

    def sides_nt(table, value):
        high, low = split(value)
        return mm_nt(table[0], high) + (mm_nt(table[1], high) + mm_nt(table[0], low))

    def restack(value):
        for j in range(GROUP):
            win_b[j * WIN : (j + 1) * WIN, :WIN] = value[:WIN, j * WIN : (j + 1) * WIN]
            win_b[j * WIN : (j + 1) * WIN, WIN:] = value[WIN:, j * WIN : (j + 1) * WIN]

    @pl.loop(0, LEDS // GROUP)
    def _(step):
        pr, pi = turned[0], turned[1]
        for j in range(GROUP):
            led = step * GROUP + j
            row, col = offs[1, led], offs[0, led]
            first = pl.multiple_of((col // 128) * 128, 128)
            shift = col - first
            back = lax.rem(256 - shift, 256)
            cr = cut(spec, 0, row, first, back)
            ci = cut(spec, 1, row, first, back)
            wr, wi = cmul(pr, pi, cr, ci)
            win_b[j * WIN : (j + 1) * WIN, :WIN] = wr
            win_b[j * WIN : (j + 1) * WIN, WIN:] = wi
        restack(sides_nt(inv_sides, win_b[...]))
        wave = mm3(split(win_b[...]), inv_lanes)
        for j in range(GROUP):
            wr = wave[j * WIN : (j + 1) * WIN, :WIN]
            wi = wave[j * WIN : (j + 1) * WIN, WIN:]
            excess = wr * wr + wi * wi - intensity[step * GROUP + j]
            win_a[:WIN, j * WIN : (j + 1) * WIN] = wr * excess
            win_a[WIN:, j * WIN : (j + 1) * WIN] = wi * excess
        restack(mm3(fwd_sides, split(win_a[...])))
        win_a[...] = sides_nt(fwd_sides, win_b[...])
        for j in range(GROUP):
            led = step * GROUP + j
            row, col = offs[1, led], offs[0, led]
            first = pl.multiple_of((col // 128) * 128, 128)
            shift = col - first
            gr = win_a[:WIN, j * WIN : (j + 1) * WIN] * -STEP_SIZE
            gi = win_a[WIN:, j * WIN : (j + 1) * WIN] * -STEP_SIZE
            ur, ui = cmul(pr, -pi, gr, gi)
            add(new, 0, row, first, shift, ur)
            add(new, 1, row, first, shift, ui)

    @pl.loop(0, PAD // 128)
    def _(n):
        at = pl.ds(pl.multiple_of(n * 128, 128), 128)
        for row in range(0, SUB, 8):
            items = []
            for k in range(RADIX):
                here = slice(k * SUB + row, k * SUB + row + 8)
                items.append((new[0, here, at], new[1, here, at]))
            done = fft_list(items, 1)
            for b in range(RADIX):
                sub[b, row : row + 8, at] = done[b][0]
                sub[b, SUB + row : SUB + row + 8, at] = done[b][1]

    @pl.loop(0, RADIX)
    def _(b):
        mixed = mm3((inv[0, b], inv[1, b]), split(sub[b]))
        rows = pl.ds(b, SUB, stride=RADIX)
        for n in range(5):
            y[n, rows, :] = mixed[:SUB, 128 * n : 128 * n + 128]
            y[5 + n, rows, :] = mixed[SUB:, 128 * n : 128 * n + 128]

    for n in range(10):
        at = slice(128 * n, 128 * n + 128)
        high, low = split(y[n])
        z_hi[:, at] = high
        z_lo[:, at] = low


def vmem():
    return pl.BlockSpec(memory_space=pltpu.VMEM)


def tile_step(tiles, pupils, intensity, offsets):
    seeds, fwd, inv, lanes, sides = tile_tables()
    held = (pupils, intensity, seeds, fwd, inv, lanes, sides)
    return pl.pallas_call(
        tile_body,
        out_shape=[
            jax.ShapeDtypeStruct((TILE, 2 * PAD), BF),
            jax.ShapeDtypeStruct((TILE, 2 * PAD), BF),
            jax.ShapeDtypeStruct((2 * PAD, 2 * TILE), BF),
            jax.ShapeDtypeStruct((2 * PAD, 2 * TILE), BF),
        ],
        in_specs=[pl.BlockSpec(memory_space=pltpu.SMEM)]
        + [pl.BlockSpec(memory_space=pltpu.HBM)] * 8,
        out_specs=[vmem()] * 4,
        scratch_shapes=[
            pltpu.VMEM((2, TILE, PAD), F32),
            pltpu.VMEM((2 * PAD // 128, TILE, 128), F32),
            pltpu.VMEM((RADIX, 2 * SUB, PAD), F32),
            pltpu.VMEM((2, TILE + 8, PAD), F32),
            pltpu.VMEM((2, TILE + 8, PAD), F32),
            pltpu.VMEM((2 * WIN, GROUP * WIN), F32),
            pltpu.VMEM((GROUP * WIN, 2 * WIN), F32),
            pltpu.VMEM((2, WIN, WIN), F32),
            pltpu.VMEM((2, PAD // 128, TILE, 128), F32),
            pltpu.VMEM((2, TILE, TILE), F32),
            *[pltpu.VMEM(value.shape, value.dtype) for value in held],
            pltpu.SemaphoreType.DMA((8,)),
        ],
        compiler_params=pltpu.CompilerParams(vmem_limit_bytes=A_LIMIT << 20),
        name="tile_step",
    )(
        *[
            pltpu.with_memory_space_constraint(jnp.asarray(value), pltpu.HBM)
            for value in (offsets, tiles, *held)
        ]
    )


def row_tables():
    lane = np.arange(128)
    k1 = np.arange(32)
    turn = unit(-(k1[:, None] * lane[None, :]) / ROWS)
    keep = axis_filter(ROWS)[k1[:, None] + 32 * lane[None, :]]
    rows = np.stack([turn.real, turn.imag, keep.real, keep.imag]).astype(np.float32)
    full = dft_np(128, -1)
    mats = np.stack([*split_np(right_block(full)), *split_np(right_block(np.conj(full)))])
    return rows, mats


def col_tables():
    lane = np.arange(64)
    kc = np.arange(16)
    kr = np.arange(8)
    low = kc[None, :] + 16 * kr[:, None]
    turn = unit(-(low[:, :, None] * lane) / COLS)
    keep = axis_filter(COLS)[low[:, :, None] + 128 * lane]
    rows = np.stack([turn.real, turn.imag, keep.real, keep.imag]).reshape(4, 128, 64)
    rows = np.concatenate([rows, rows], axis=2).astype(np.float32)
    inner = unit(-(np.arange(8)[:, None] * kc[None, :]) / 128)
    full = np.kron(np.eye(2), dft_np(64, -1))
    mats = np.stack([*split_np(right_block(full)), *split_np(right_block(np.conj(full)))])
    return rows, mats, inner


MESH = pl.DeviceIdType.MESH
FAR_ROWS = ((1, 2), (1, 1), (1, 3), (0, 2), (1, 0), (0, 1), (0, 3))
FAR_COLS = sorted(
    ((y, x, k) for y in range(4) for x in range(2) for k in range(2) if y or x or k),
    key=lambda step: -(min(step[0], 4 - step[0]) + step[1]),
)
QUARTER = 16


def settle(ref, sem):
    pltpu.make_async_copy(ref, ref, sem).wait()


def field_body(
    z_hi, z_lo, r_hi, r_lo, r_rows, r_mats, c_rows, c_mats, out,
    refined, halo, front, got, work, mid, give, have, send,
    halo_sem, send_sem, recv_row, own_row, recv_all, own_all, recv_col, own_sem, ready,
):
    row, col = lax.axis_index("row"), lax.axis_index("col")
    xh, z = row // 4, lax.rem(row, 4)
    y, xl, core = col // 4, lax.rem(col // 2, 2), lax.rem(col, 2)
    rows_at = [lax.rem(row + step, 8) for step in range(8)]
    cols_at = [lax.rem(col + step, 16) for step in range(16)]

    barrier = pltpu.get_barrier_semaphore()
    for i in range(1, 8):
        pl.semaphore_signal(barrier, inc=1, device_id=(rows_at[i], col), device_id_type=MESH)
    for j in range(1, 16):
        pl.semaphore_signal(barrier, inc=1, device_id=(row, cols_at[j]), device_id_type=MESH)

    chunks = [lax.rem(xh + i, 2) * 4 + lax.rem(z + j, 4) for i, j in FAR_ROWS]

    def columns_of(blocks):
        places = [pl.ds(pl.multiple_of(block * 64, 64), 64) for block in blocks]

        def fill(at):
            high = jnp.concatenate([z_hi[place, :] for place in places], axis=0)
            low = jnp.concatenate([z_lo[place, :] for place in places], axis=0)
            value = mm3((high, low), (r_hi[:, at], r_lo[:, at]))
            for index, place in enumerate(places):
                refined[place, at] = value[64 * index : 64 * index + 64]

        @pl.loop(0, 4)
        def _(n):
            fill(pl.ds(pl.multiple_of(n * 256, 256), 256))

        fill(slice(1024, 1152))

    columns_of([8, *chunks[:2]])
    pl.semaphore_wait(barrier, 22)
    for j in range(1, 16):
        pl.semaphore_signal(ready, inc=1, device_id=(row, cols_at[j]), device_id_type=MESH)

    edge = pltpu.make_async_remote_copy(
        refined.at[STRIDE:], halo, halo_sem.at[0], halo_sem.at[1],
        device_id=(row, cols_at[1]), device_id_type=MESH,
    )
    edge.start()

    def give_row(target, quarter, source):
        pltpu.make_async_remote_copy(
            source, got.at[row, quarter * QUARTER : (quarter + 1) * QUARTER],
            send_sem.at[0], recv_row.at[quarter], device_id=(target, col), device_id_type=MESH,
        ).start()

    def plain(target, quarter):
        start = pl.multiple_of(target * 64 + quarter * QUARTER, QUARTER)
        return refined.at[pl.ds(start, QUARTER)]

    def blended(quarter):
        return front.at[quarter * QUARTER : (quarter + 1) * QUARTER]

    def give_plain(targets, quarter=0):
        for target in targets:
            @pl.when(target != 0)
            def _():
                give_row(target, quarter, plain(target, quarter))

    def give_blended(quarter):
        for target in chunks:
            @pl.when(target == 0)
            def _():
                give_row(target, quarter, blended(quarter))

    give_plain(chunks[:2])
    columns_of(chunks[2:5])
    give_plain(chunks[2:5])
    columns_of([*chunks[5:], row])
    give_plain(chunks[5:])
    give_plain(chunks, 1)

    edge.wait()
    place = lax.broadcasted_iota(jnp.int32, (OVL, 2 * TILE), 0).astype(F32)
    ramp = (place + 0.5) / OVL
    front[...] = ramp * refined[:OVL] + (1.0 - ramp) * halo[...]

    give_blended(0)
    give_blended(1)
    for quarter in range(2, 4):
        give_plain(chunks, quarter)
        give_blended(quarter)

    @pl.when(row == 0)
    def _():
        pltpu.make_async_copy(front, got.at[0], own_row).start()

    @pl.when(row != 0)
    def _():
        start = pl.multiple_of(row * 64, 64)
        pltpu.make_async_copy(refined.at[pl.ds(start, 64)], got.at[row], own_row).start()

    settle(front, own_row)

    lane = lax.broadcasted_iota(jnp.int32, (8, 128), 1)
    slope = jnp.where(lane < OVL, (lane.astype(F32) + 0.5) / OVL, 1.0)
    rest = jnp.where(lane < OVL, 1.0 - slope, 0.0)

    @pl.loop(0, 4)
    def _(quarter):
        columns = pl.ds(pl.multiple_of(quarter * QUARTER, QUARTER), QUARTER)
        settle(got.at[:7, columns], recv_row.at[quarter])

        @pl.loop(0, 2)
        def _(half):
            at = pl.ds(pl.multiple_of(quarter * QUARTER + half * 8, 8), 8)
            for a in range(4):
                items = []
                for p in range(8):
                    re = got[p, at, 128 * a : 128 * a + 128]
                    im = got[p, at, STRIDE + 128 * a : STRIDE + 128 * a + 128]
                    if a == 0:
                        tail = got[(p - 1) % 8, at, 2 * STRIDE :]
                        re = slope * re + rest * tail
                        im = slope * im + rest * pltpu.roll(tail, 64, 1)
                    items.append((re, im))
                done = fft_list(items, -1)
                for k in range(8):
                    re, im = cscale(done[k], unit(-a * k / 32))
                    mid[4 * k + a, 0, at, :] = re
                    mid[4 * k + a, 1, at, :] = im

            @pl.loop(0, 8)
            def _(k):
                items = [(mid[4 * k + a, 0, at, :], mid[4 * k + a, 1, at, :]) for a in range(4)]
                done = fft_list(items, -1)
                for q in range(4):
                    index = k + 8 * q
                    tr = r_rows[0, pl.ds(index, 1), :]
                    ti = r_rows[1, pl.ds(index, 1), :]
                    re, im = cmul(*done[q], tr, ti)
                    start = pl.ds(pl.multiple_of(index * QUARTER + half * 8, 8), 8)
                    work[start, :128] = re
                    work[start, 128:] = im

        full = mm3(split(work[:512]), (r_mats[0], r_mats[1]))
        full = full.reshape(32, QUARTER, 256)
        kr, ki = r_rows[2][:, None, :], r_rows[3][:, None, :]
        re, im = cmul(full[:, :, :128], full[:, :, 128:], kr, ki)
        both = jnp.concatenate([re, im], axis=2).reshape(512, 256)
        work[:512] = mm3(split(both), (r_mats[2], r_mats[3]))

        @pl.loop(0, 2)
        def _(half):
            at = pl.ds(pl.multiple_of(quarter * QUARTER + half * 8, 8), 8)

            @pl.loop(0, 8)
            def _(k):
                items = []
                for q in range(4):
                    index = k + 8 * q
                    tr = r_rows[0, pl.ds(index, 1), :]
                    ti = r_rows[1, pl.ds(index, 1), :]
                    start = pl.ds(pl.multiple_of(index * QUARTER + half * 8, 8), 8)
                    items.append(cmul(work[start, :128], work[start, 128:], tr, -ti))
                done = fft_list(items, 1)
                for a in range(4):
                    mid[4 * k + a, 0, at, :] = done[a][0]
                    mid[4 * k + a, 1, at, :] = done[a][1]

            for a in range(4):
                items = [
                    cscale((mid[4 * k + a, 0, at, :], mid[4 * k + a, 1, at, :]), unit(a * k / 32))
                    for k in range(8)
                ]
                done = fft_list(items, 1)
                for p in range(8):
                    mid[4 * p + a, 0, at, :] = done[p][0]
                    mid[4 * p + a, 1, at, :] = done[p][1]

    me = row * 16 + col

    def peers(step):
        tr = lax.rem(xh + 1 + step // 16, 2) * 4 + lax.rem(z + 2 + (step // 4) % 4, 4)
        ty = lax.rem(y + 2 + step % 4, 4)
        ends = []
        for i in range(2):
            for j in range(2):
                ends.append((tr, ty * 4 + lax.rem(xl + i, 2) * 2 + lax.rem(core + j, 2)))
        return tr * 4 + ty, ends

    own_step = 26

    def give_all(step, ends, part):
        lines = slice(part * 16, part * 16 + 16)
        for index, (tr, tc) in enumerate(ends):
            def go(tr=tr, tc=tc):
                pltpu.make_async_remote_copy(
                    give.at[tr * 16 + tc, lines], have.at[me, lines],
                    send_sem.at[1], recv_all.at[part], device_id=(tr, tc), device_id_type=MESH,
                ).start()

            if index:
                go()
            else:
                pl.when(step != own_step)(go)

    pl.semaphore_wait(ready, 15)

    @pl.loop(0, 32)
    def _(step):
        block, ends = peers(step)
        flat = jnp.transpose(mid[block].reshape(128, 128))
        for i in range(4):
            give[block * 4 + i] = flat[32 * i : 32 * i + 32]
        give_all(step, ends, 0)

    own = pltpu.make_async_copy(give.at[me], have.at[me], own_all)
    own.start()

    @pl.loop(0, 32)
    def _(step):
        give_all(step, peers(step)[1], 1)

    own.wait()

    left = lane < 64
    inner = col_tables()[2]

    @pl.loop(0, 2)
    def _(part):
        lines = pl.ds(pl.multiple_of(part * 16, 16), 16)
        top = pl.ds(pl.multiple_of(part * 16, 8), 8)
        low = pl.ds(pl.multiple_of(part * 16 + 8, 8), 8)
        settle(have.at[:127, lines], recv_all.at[part])

        for r in range(8):
            items = []
            for c in range(16):
                a = have[16 * r + c, top, :]
                b = have[16 * r + c, low, :]
                re = jnp.where(left, a, pltpu.roll(b, 64, 1))
                im = jnp.where(left, pltpu.roll(a, 64, 1), b)
                items.append((re, im))
            done = fft_list(items, -1)
            for k in range(16):
                flat = 8 * (16 * r + k)
                re, im = cscale(done[k], inner[r, k])
                work[flat : flat + 8, :128] = re
                work[flat : flat + 8, 128:] = im

        @pl.loop(0, 16)
        def _(k):
            places = [pl.ds(pl.multiple_of(8 * (16 * r + k), 8), 8) for r in range(8)]
            items = [(work[at, :128], work[at, 128:]) for at in places]
            done = fft_list(items, -1)
            for q in range(8):
                tr = c_rows[0, pl.ds(16 * q + k, 1), :]
                ti = c_rows[1, pl.ds(16 * q + k, 1), :]
                re, im = cmul(*done[q], tr, ti)
                work[places[q], :128] = re
                work[places[q], 128:] = im

        @pl.loop(0, 2)
        def _(n):
            at = pl.ds(pl.multiple_of(n * 512, 512), 512)
            keep = pl.ds(pl.multiple_of(n * 64, 64), 64)
            full = mm3(split(work[at, :]), (c_mats[0], c_mats[1]))
            full = full.reshape(64, 8, 256)
            kr, ki = c_rows[2, keep, :][:, None, :], c_rows[3, keep, :][:, None, :]
            re, im = cmul(full[:, :, :128], full[:, :, 128:], kr, ki)
            both = jnp.concatenate([re, im], axis=2).reshape(512, 256)
            work[at, :] = mm3(split(both), (c_mats[2], c_mats[3]))

        @pl.loop(0, 16)
        def _(k):
            places = [pl.ds(pl.multiple_of(8 * (16 * r + k), 8), 8) for r in range(8)]
            items = []
            for q in range(8):
                tr = c_rows[0, pl.ds(16 * q + k, 1), :]
                ti = c_rows[1, pl.ds(16 * q + k, 1), :]
                items.append(cmul(work[places[q], :128], work[places[q], 128:], tr, -ti))
            done = fft_list(items, 1)
            for r in range(8):
                work[places[r], :128] = done[r][0]
                work[places[r], 128:] = done[r][1]

        for r in range(8):
            items = []
            for k in range(16):
                flat = 8 * (16 * r + k)
                value = (work[flat : flat + 8, :128], work[flat : flat + 8, 128:])
                items.append(cscale(value, np.conj(inner[r, k])))
            done = fft_list(items, 1)
            for c in range(16):
                flat = 8 * (16 * r + c)
                work[flat : flat + 8, :128] = done[c][0]
                work[flat : flat + 8, 128:] = done[c][1]

        @pl.loop(0, 16)
        def _(c):
            for piece in range(2):
                lanes = slice(128 * piece, 128 * piece + 128)
                for pair in range(4):
                    first = pl.ds(pl.multiple_of(8 * (32 * pair + c), 8), 8)
                    second = pl.ds(pl.multiple_of(8 * (32 * pair + 16 + c), 8), 8)
                    a = work[first, lanes]
                    b = work[second, lanes]
                    to = slice(128 * pair, 128 * pair + 128)
                    send[c, piece, top, to] = jnp.where(left, a, pltpu.roll(b, 64, 1))
                    send[c, piece, low, to] = jnp.where(left, pltpu.roll(a, 64, 1), b)

        mine = pl.ds(pl.multiple_of(col * 32 + part * 16, 16), 16)
        for i, j, k in FAR_COLS:
            tc = lax.rem(y + i, 4) * 4 + lax.rem(xl + j, 2) * 2 + lax.rem(core + k, 2)
            pltpu.make_async_remote_copy(
                send.at[tc, :, lines], out.at[:, mine],
                send_sem.at[2], recv_col.at[part], device_id=(row, tc), device_id_type=MESH,
            ).start()
        pltpu.make_async_copy(send.at[col, :, lines], out.at[:, mine], own_sem.at[part]).start()

    for part in range(2):
        settle(send.at[:15, :, :16], recv_col.at[part])
        settle(send.at[0, :, :16], own_sem.at[part])
    settle(got.at[:7], send_sem.at[0])
    settle(have.at[:127], send_sem.at[1])
    settle(send.at[:15], send_sem.at[2])


def field_step(z_hi, z_lo, r_hi, r_lo):
    r_rows, r_mats = row_tables()
    c_rows, c_mats, _ = col_tables()
    return pl.pallas_call(
        field_body,
        out_shape=jax.ShapeDtypeStruct((2, STRIDE, STRIDE), F32),
        in_specs=[vmem()] * 8,
        out_specs=vmem(),
        scratch_shapes=[
            pltpu.VMEM((TILE, 2 * TILE), F32),
            pltpu.VMEM((OVL, 2 * TILE), F32),
            pltpu.VMEM((OVL, 2 * TILE), F32),
            pltpu.VMEM((8, 64, 2 * TILE), F32),
            pltpu.VMEM((1024, 256), F32),
            pltpu.VMEM((32, 2, 64, 128), F32),
            pltpu.VMEM((128, 32, 128), F32),
            pltpu.VMEM((128, 32, 128), F32),
            pltpu.VMEM((16, 2, 32, STRIDE), F32),
            pltpu.SemaphoreType.DMA((2,)),
            pltpu.SemaphoreType.DMA((3,)),
            pltpu.SemaphoreType.DMA((4,)),
            pltpu.SemaphoreType.DMA(()),
            pltpu.SemaphoreType.DMA((2,)),
            pltpu.SemaphoreType.DMA(()),
            pltpu.SemaphoreType.DMA((2,)),
            pltpu.SemaphoreType.DMA((2,)),
            pltpu.SemaphoreType.REGULAR,
        ],
        compiler_params=pltpu.CompilerParams(
            vmem_limit_bytes=B_LIMIT << 20, collective_id=0, has_side_effects=True
        ),
        name="field_step",
    )(z_hi, z_lo, r_hi, r_lo, r_rows, r_mats, c_rows, c_mats)


def local(tiles, pupils, intensity, offsets):
    return field_step(*tile_step(tiles, pupils, intensity, offsets[0, 0]))


def solution(mesh):
    placed = (
        P(None, "row", "col"),
        P(None, "row", "col"),
        P(None, "row", "col"),
        P("row", "col", None, None),
    )
    return jax.shard_map(
        local, mesh=mesh, in_specs=placed, out_specs=P(None, "row", "col"), check_vma=False
    )
```

```python
import math

import numpy as np
import ml_dtypes
import jax
import jax.numpy as jnp
from jax import lax
from jax.experimental import pallas as pl
from jax.experimental.pallas import tpu as pltpu
from jax.sharding import PartitionSpec as P

TILE = 576
PAD = 640
OVL = 64
WIN = 128
LEDS = 16
STRIDE = 512
ROWS = 4096
COLS = 8192
FRESNEL = 2048
STEP_SIZE = 0.05
RADIX = 6
SUB = TILE // RADIX
BF = jnp.bfloat16
F32 = jnp.float32
GROUP = 8
A_LIMIT = 38
B_LIMIT = 24


def split_np(table):
    table = np.asarray(table, np.float64)
    high = table.astype(np.float32).astype(ml_dtypes.bfloat16)
    low = (table - high.astype(np.float64)).astype(np.float32).astype(ml_dtypes.bfloat16)
    return high, low


def unit(turns):
    turns = np.asarray(turns, np.float64)
    return np.exp(2j * np.pi * (turns - np.floor(turns)))


def right_block(table):
    return np.block([[table.real, table.imag], [-table.imag, table.real]])


def left_block(table):
    return np.block([[table.real, -table.imag], [table.imag, table.real]])


def dft_np(length, sign):
    index = np.arange(length)
    return unit(sign * (index[:, None] * index[None, :] % length) / length)


def axis_filter(length):
    freq = np.arange(length)
    signed = np.where(freq < length // 2, freq, freq - length).astype(np.float64)
    turns = signed * signed * (FRESNEL / (length * length))
    return np.exp(-2.0 * signed * signed / (length * length)) * unit(-turns) / length


def split(value):
    high = value.astype(BF)
    low = (value - high.astype(F32)).astype(BF)
    return high, low


def mm(left, right):
    return jnp.dot(left, right, preferred_element_type=F32)


def mm3(left, right):
    return mm(left[0], right[0]) + (mm(left[1], right[0]) + mm(left[0], right[1]))


def mm_nt(left, right):
    return lax.dot_general(left, right, (((1,), (1,)), ((), ())), preferred_element_type=F32)


def cmul(ar, ai, br, bi):
    return ar * br - ai * bi, ar * bi + ai * br


def cscale(value, factor):
    re, im = value
    fr, fi = float(factor.real), float(factor.imag)
    near = 1e-12
    if abs(fi) < near:
        if abs(fr - 1) < near:
            return re, im
        if abs(fr + 1) < near:
            return -re, -im
    if abs(fr) < near:
        if abs(fi - 1) < near:
            return -im, re
        if abs(fi + 1) < near:
            return im, -re
    if abs(abs(fr) - abs(fi)) < near:
        size = abs(fr)
        sr, si = math.copysign(1, fr), math.copysign(1, fi)
        left = re if sr > 0 else -re
        low = im if sr > 0 else -im
        new_re = left - im if si > 0 else left + im
        new_im = low + re if si > 0 else low - re
        return new_re * size, new_im * size
    return re * fr - im * fi, re * fi + im * fr


def fft_list(items, sign):
    count = len(items)
    if count == 1:
        return items
    if count == 3:
        (ar, ai), (br, bi), (cr, ci) = items
        sr, si, dr, di = br + cr, bi + ci, br - cr, bi - ci
        mr, mi = ar - 0.5 * sr, ai - 0.5 * si
        root = sign * math.sqrt(0.75)
        tr, ti = -root * di, root * dr
        return [(ar + sr, ai + si), (mr + tr, mi + ti), (mr - tr, mi - ti)]
    even = fft_list(items[0::2], sign)
    odd = fft_list(items[1::2], sign)
    half = count // 2
    first, second = [], []
    for index in range(half):
        turned = cscale(odd[index], unit(sign * index / count))
        er, ei = even[index]
        first.append((er + turned[0], ei + turned[1]))
        second.append((er - turned[0], ei - turned[1]))
    return first + second


def tile_tables():
    index = np.arange(TILE)
    low = unit(-(np.arange(24)[:, None] * index[None, :] % TILE) / TILE) / math.sqrt(TILE)
    high = unit(-(24 * np.arange(24)[:, None] * index[None, :] % TILE) / TILE)
    seeds = np.zeros((4, 24, PAD), np.float32)
    seeds[0, :, :TILE], seeds[1, :, :TILE] = low.real, low.imag
    seeds[2, :, :TILE], seeds[3, :, :TILE] = high.real, high.imag
    small = np.arange(SUB)
    forward, inverse = [], []
    for part in range(RADIX):
        turned = unit(-(part * small[:, None] + RADIX * small[:, None] * small[None, :]) / TILE)
        turned = turned / math.sqrt(TILE)
        forward.append(left_block(turned))
        inverse.append(left_block(np.conj(turned.T)))
    forward = np.stack(split_np(np.stack(forward)))
    inverse = np.stack(split_np(np.stack(inverse)))
    window = dft_np(WIN, -1) / math.sqrt(WIN)
    lanes = np.stack(split_np(right_block(np.conj(window))))
    sides = np.stack(
        [*split_np(left_block(np.conj(window))), *split_np(left_block(window))]
    )
    return seeds, forward, inverse, lanes, sides


def cut(ref, part, row, first, back):
    base = pl.multiple_of((row // 8) * 8, 8)
    down = row - base
    wide = ref[part, pl.ds(base, WIN + 8), pl.ds(first, 256)]
    wide = pltpu.roll(wide, back, 1)[:, :WIN].reshape(WIN // 8 + 1, 8, WIN)
    wide = pltpu.roll(wide, lax.rem(8 - down, 8), 1)
    lane = lax.broadcasted_iota(jnp.int32, (WIN // 8, 8, WIN), 1)
    return jnp.where(lane < 8 - down, wide[:-1], wide[1:]).reshape(WIN, WIN)


def add(ref, part, row, first, shift, value):
    base = pl.multiple_of((row // 8) * 8, 8)
    down = row - base
    turned = pltpu.roll(value.reshape(WIN // 8, 8, WIN), down, 1)
    zero = jnp.zeros((1, 8, WIN), F32)
    lane = lax.broadcasted_iota(jnp.int32, (WIN // 8 + 1, 8, WIN), 1)
    upper = jnp.concatenate([zero, turned], axis=0)
    lower = jnp.concatenate([turned, zero], axis=0)
    tall = jnp.where(lane < down, upper, lower).reshape(WIN + 8, WIN)
    wide = jnp.concatenate([tall, jnp.zeros((WIN + 8, 128), F32)], axis=1)
    here = (part, pl.ds(base, WIN + 8), pl.ds(first, 256))
    ref[here] = ref[here] + pltpu.roll(wide, shift, 1)


def tile_body(
    offs, tiles_in, pupils_in, intensity_in, seeds_in, fwd_in, inv_in, lanes_in, sides_in,
    z_hi, z_lo, r_hi, r_lo,
    base, y, sub, spec, wins_a, wins_b, turned,
    tiles, raw, pupils, intensity, seeds, fwd, inv, lanes, sides, sems,
):
    pairs = [(seeds_in, seeds), (tiles_in, raw), (fwd_in, fwd)]
    pairs += [(pupils_in, pupils), (intensity_in, intensity)]
    pairs += [(lanes_in, lanes), (sides_in, sides), (inv_in, inv)]
    loads = [
        pltpu.make_async_copy(source, target, sems.at[index])
        for index, (source, target) in enumerate(pairs)
    ]
    for load in loads:
        load.start()
    loads[0].wait()

    low_r, low_i = seeds[0], seeds[1]

    @pl.loop(0, 24)
    def _(a):
        hr = seeds[2, pl.ds(a, 1), :]
        hi = seeds[3, pl.ds(a, 1), :]
        tr, ti = cmul(low_r, low_i, hr, hi)
        start = pl.multiple_of(a * 24, 8)
        base[0, pl.ds(start, 24), :] = tr
        base[1, pl.ds(start, 24), :] = ti

    for ref in (r_hi, r_lo):
        zero_tail = jnp.zeros((PAD - TILE, 2 * TILE), BF)
        ref[TILE:PAD, :] = zero_tail
        ref[PAD + TILE :, :] = zero_tail

    @pl.loop(0, TILE // 96)
    def _(a):
        start = pl.multiple_of(a * 96, 16)
        re, im = base[0, pl.ds(start, 96), :], base[1, pl.ds(start, 96), :]
        for offset, left, right in ((0, re, -im), (PAD, im, re)):
            at = pl.ds(start + offset, 96)
            ends = left[:, STRIDE:] + pltpu.roll(right[:, STRIDE:], 64, 1)
            for where, value in (
                (slice(0, STRIDE), left[:, :STRIDE]),
                (slice(STRIDE, 2 * STRIDE), right[:, :STRIDE]),
                (slice(2 * STRIDE, 2 * TILE), ends),
            ):
                high, low = split(value)
                r_hi[at, where] = high
                r_lo[at, where] = low

    def forward():
        @pl.loop(0, RADIX)
        def _(b):
            rows = pl.ds(b, SUB, stride=RADIX)
            parts = [
                jnp.concatenate([tiles[part, n, rows, :] for n in range(5)], axis=1)
                for part in range(2)
            ]
            sub[b] = mm3((fwd[0, b], fwd[1, b]), split(jnp.concatenate(parts, axis=0)))

        @pl.loop(0, PAD // 128)
        def _(n):
            at = pl.ds(pl.multiple_of(n * 128, 128), 128)
            for row in range(0, SUB, 8):
                items = [
                    (sub[b, row : row + 8, at], sub[b, SUB + row : SUB + row + 8, at])
                    for b in range(RADIX)
                ]
                done = fft_list(items, -1)
                for k in range(RADIX):
                    here = slice(k * SUB + row, k * SUB + row + 8)
                    spec[0, here, at] = done[k][0]
                    spec[1, here, at] = done[k][1]

    loads[1].wait()
    for part in range(2):
        for n in range(5):
            width = min(128, TILE - 128 * n)
            tiles[part, n, :, :width] = raw[part, :, 128 * n : 128 * n + width]
    loads[2].wait()
    forward()

    def flip(part, at, count, to):
        for i in range(4):
            block = jnp.transpose(spec[part, 128 * i : 128 * i + 128, at])
            tiles[part, i, to, :] = block[:count]
        half = jnp.concatenate([spec[part, STRIDE:TILE, at], jnp.zeros((64, 128), F32)], axis=0)
        tiles[part, 4, to, :] = jnp.transpose(half)[:count]

    for part in range(2):
        @pl.loop(0, 4)
        def _(j):
            at = pl.ds(pl.multiple_of(j * 128, 128), 128)
            flip(part, at, 128, at)

        flip(part, slice(STRIDE, PAD), 64, slice(STRIDE, TILE))

    forward()

    for part in range(2):
        spec[part, TILE:, :] = jnp.zeros((8, PAD), F32)
    for load in loads[3:]:
        load.wait()
    for part in range(2):
        turned[part] = jnp.transpose(pupils[part])
    inv_lanes = (lanes[0], lanes[1])
    inv_sides = (sides[0], sides[1])
    fwd_sides = (sides[2], sides[3])

    def sides_nt(table, value):
        high, low = split(value)
        return mm_nt(table[0], high) + (mm_nt(table[1], high) + mm_nt(table[0], low))

    def restack(win_b, value):
        for j in range(GROUP):
            win_b[j * WIN : (j + 1) * WIN, :WIN] = value[:WIN, j * WIN : (j + 1) * WIN]
            win_b[j * WIN : (j + 1) * WIN, WIN:] = value[WIN:, j * WIN : (j + 1) * WIN]

    pr, pi = turned[0], turned[1]
    for step in range(LEDS // GROUP):
        win_b = wins_b.at[step]
        for j in range(GROUP):
            led = step * GROUP + j
            row, col = offs[1, led], offs[0, led]
            first = pl.multiple_of((col // 128) * 128, 128)
            back = lax.rem(first + 256 - col, 256)
            cr = cut(spec, 0, row, first, back)
            ci = cut(spec, 1, row, first, back)
            wr, wi = cmul(pr, pi, cr, ci)
            win_b[j * WIN : (j + 1) * WIN, :WIN] = wr
            win_b[j * WIN : (j + 1) * WIN, WIN:] = wi

    for step in range(LEDS // GROUP):
        win_a, win_b = wins_a.at[step], wins_b.at[step]
        pr, pi = turned[0], turned[1]
        restack(win_b, sides_nt(inv_sides, win_b[...]))
        wave = mm3(split(win_b[...]), inv_lanes)
        for j in range(GROUP):
            wr = wave[j * WIN : (j + 1) * WIN, :WIN]
            wi = wave[j * WIN : (j + 1) * WIN, WIN:]
            excess = wr * wr + wi * wi - intensity[step * GROUP + j]
            win_a[:WIN, j * WIN : (j + 1) * WIN] = wr * excess
            win_a[WIN:, j * WIN : (j + 1) * WIN] = wi * excess
        restack(win_b, mm3(fwd_sides, split(win_a[...])))
        win_a[...] = sides_nt(fwd_sides, win_b[...])
        for j in range(GROUP):
            led = step * GROUP + j
            row, col = offs[1, led], offs[0, led]
            first = pl.multiple_of((col // 128) * 128, 128)
            shift = col - first
            gr = win_a[:WIN, j * WIN : (j + 1) * WIN] * -STEP_SIZE
            gi = win_a[WIN:, j * WIN : (j + 1) * WIN] * -STEP_SIZE
            ur, ui = cmul(pr, -pi, gr, gi)
            add(spec, 0, row, first, shift, ur)
            add(spec, 1, row, first, shift, ui)

    @pl.loop(0, PAD // 128)
    def _(n):
        at = pl.ds(pl.multiple_of(n * 128, 128), 128)
        for row in range(0, SUB, 8):
            items = []
            for k in range(RADIX):
                here = slice(k * SUB + row, k * SUB + row + 8)
                items.append((spec[0, here, at], spec[1, here, at]))
            done = fft_list(items, 1)
            for b in range(RADIX):
                sub[b, row : row + 8, at] = done[b][0]
                sub[b, SUB + row : SUB + row + 8, at] = done[b][1]

    @pl.loop(0, RADIX)
    def _(b):
        mixed = mm3((inv[0, b], inv[1, b]), split(sub[b]))
        rows = pl.ds(b, SUB, stride=RADIX)
        for n in range(5):
            y[n, rows, :] = mixed[:SUB, 128 * n : 128 * n + 128]
            y[5 + n, rows, :] = mixed[SUB:, 128 * n : 128 * n + 128]

    for n in range(10):
        at = slice(128 * n, 128 * n + 128)
        high, low = split(y[n])
        z_hi[:, at] = high
        z_lo[:, at] = low


def vmem():
    return pl.BlockSpec(memory_space=pltpu.VMEM)


def tile_step(tiles, pupils, intensity, offsets):
    seeds, fwd, inv, lanes, sides = tile_tables()
    held = (pupils, intensity, seeds, fwd, inv, lanes, sides)
    return pl.pallas_call(
        tile_body,
        out_shape=[
            jax.ShapeDtypeStruct((TILE, 2 * PAD), BF),
            jax.ShapeDtypeStruct((TILE, 2 * PAD), BF),
            jax.ShapeDtypeStruct((2 * PAD, 2 * TILE), BF),
            jax.ShapeDtypeStruct((2 * PAD, 2 * TILE), BF),
        ],
        in_specs=[pl.BlockSpec(memory_space=pltpu.SMEM)]
        + [pl.BlockSpec(memory_space=pltpu.HBM)] * 8,
        out_specs=[vmem()] * 4,
        scratch_shapes=[
            pltpu.VMEM((2, TILE, PAD), F32),
            pltpu.VMEM((2 * PAD // 128, TILE, 128), F32),
            pltpu.VMEM((RADIX, 2 * SUB, PAD), F32),
            pltpu.VMEM((2, TILE + 8, PAD), F32),
            pltpu.VMEM((LEDS // GROUP, 2 * WIN, GROUP * WIN), F32),
            pltpu.VMEM((LEDS // GROUP, GROUP * WIN, 2 * WIN), F32),
            pltpu.VMEM((2, WIN, WIN), F32),
            pltpu.VMEM((2, PAD // 128, TILE, 128), F32),
            pltpu.VMEM((2, TILE, TILE), F32),
            *[pltpu.VMEM(value.shape, value.dtype) for value in held],
            pltpu.SemaphoreType.DMA((8,)),
        ],
        compiler_params=pltpu.CompilerParams(vmem_limit_bytes=A_LIMIT << 20),
        name="tile_step",
    )(
        *[
            pltpu.with_memory_space_constraint(jnp.asarray(value), pltpu.HBM)
            for value in (offsets, tiles, *held)
        ]
    )


def row_tables():
    lane = np.arange(128)
    k1 = np.arange(32)
    turn = unit(-(k1[:, None] * lane[None, :]) / ROWS)
    keep = axis_filter(ROWS)[k1[:, None] + 32 * lane[None, :]]
    rows = np.stack([turn.real, turn.imag, keep.real, keep.imag]).astype(np.float32)
    full = dft_np(128, -1)
    mats = np.stack([*split_np(right_block(full)), *split_np(right_block(np.conj(full)))])
    return rows, mats


def col_tables():
    lane = np.arange(64)
    kc = np.arange(16)
    kr = np.arange(8)
    low = kc[None, :] + 16 * kr[:, None]
    turn = unit(-(low[:, :, None] * lane) / COLS)
    keep = axis_filter(COLS)[low[:, :, None] + 128 * lane]
    rows = np.stack([turn.real, turn.imag, keep.real, keep.imag]).reshape(4, 128, 64)
    rows = np.concatenate([rows, rows], axis=2).astype(np.float32)
    inner = unit(-(np.arange(8)[:, None] * kc[None, :]) / 128)
    full = np.kron(np.eye(2), dft_np(64, -1))
    mats = np.stack([*split_np(right_block(full)), *split_np(right_block(np.conj(full)))])
    return rows, mats, inner


MESH = pl.DeviceIdType.MESH
FAR_ROWS = ((1, 2), (1, 1), (1, 3), (0, 2), (1, 0), (0, 1), (0, 3))
FAR_COLS = sorted(
    ((y, x, k) for y in range(4) for x in range(2) for k in range(2) if y or x or k),
    key=lambda step: -(min(step[0], 4 - step[0]) + step[1]),
)
QUARTER = 8


def settle(ref, sem):
    pltpu.make_async_copy(ref, ref, sem).wait()


def field_body(
    z_hi, z_lo, r_hi, r_lo, r_rows, r_mats, c_rows, c_mats, out,
    refined, halo, front, got, work, mid, give, have, send,
    halo_sem, send_sem, recv_row, own_row, recv_all, own_all, recv_col, own_sem, ready,
):
    row, col = lax.axis_index("row"), lax.axis_index("col")
    xh, z = row // 4, lax.rem(row, 4)
    y, xl, core = col // 4, lax.rem(col // 2, 2), lax.rem(col, 2)
    rows_at = [lax.rem(row + step, 8) for step in range(8)]
    cols_at = [lax.rem(col + step, 16) for step in range(16)]

    barrier = pltpu.get_barrier_semaphore()
    for i in range(1, 8):
        pl.semaphore_signal(barrier, inc=1, device_id=(rows_at[i], col), device_id_type=MESH)
    for j in range(1, 16):
        pl.semaphore_signal(barrier, inc=1, device_id=(row, cols_at[j]), device_id_type=MESH)

    chunks = [lax.rem(xh + i, 2) * 4 + lax.rem(z + j, 4) for i, j in FAR_ROWS]

    def columns_of(blocks):
        places = [pl.ds(pl.multiple_of(block * 64, 64), 64) for block in blocks]

        def fill(at):
            high = jnp.concatenate([z_hi[place, :] for place in places], axis=0)
            low = jnp.concatenate([z_lo[place, :] for place in places], axis=0)
            value = mm3((high, low), (r_hi[:, at], r_lo[:, at]))
            for index, place in enumerate(places):
                refined[place, at] = value[64 * index : 64 * index + 64]

        @pl.loop(0, 4)
        def _(n):
            fill(pl.ds(pl.multiple_of(n * 256, 256), 256))

        fill(slice(1024, 1152))

    columns_of([8, *chunks[:2]])
    pl.semaphore_wait(barrier, 22)
    for j in range(1, 16):
        pl.semaphore_signal(ready, inc=1, device_id=(row, cols_at[j]), device_id_type=MESH)

    edge = pltpu.make_async_remote_copy(
        refined.at[STRIDE:], halo, halo_sem.at[0], halo_sem.at[1],
        device_id=(row, cols_at[1]), device_id_type=MESH,
    )
    edge.start()

    def give_row(target, quarter, source):
        pltpu.make_async_remote_copy(
            source, got.at[row, quarter * QUARTER : (quarter + 1) * QUARTER],
            send_sem.at[0], recv_row.at[quarter], device_id=(target, col), device_id_type=MESH,
        ).start()

    def plain(target, quarter):
        start = pl.multiple_of(target * 64 + quarter * QUARTER, QUARTER)
        return refined.at[pl.ds(start, QUARTER)]

    def blended(quarter):
        return front.at[quarter * QUARTER : (quarter + 1) * QUARTER]

    def give_plain(targets, quarter=0):
        for target in targets:
            @pl.when(target != 0)
            def _():
                give_row(target, quarter, plain(target, quarter))

    def give_blended(quarter):
        for target in chunks:
            @pl.when(target == 0)
            def _():
                give_row(target, quarter, blended(quarter))

    give_plain(chunks[:2])
    columns_of(chunks[2:5])
    give_plain(chunks[2:5])
    columns_of([*chunks[5:], row])
    give_plain(chunks[5:])
    for quarter in range(1, 4):
        give_plain(chunks, quarter)

    edge.wait()
    place = lax.broadcasted_iota(jnp.int32, (OVL, 2 * TILE), 0).astype(F32)
    ramp = (place + 0.5) / OVL
    front[...] = ramp * refined[:OVL] + (1.0 - ramp) * halo[...]

    for quarter in range(4):
        give_blended(quarter)
    for quarter in range(4, 8):
        give_plain(chunks, quarter)
        give_blended(quarter)

    @pl.when(row == 0)
    def _():
        pltpu.make_async_copy(front, got.at[0], own_row).start()

    @pl.when(row != 0)
    def _():
        start = pl.multiple_of(row * 64, 64)
        pltpu.make_async_copy(refined.at[pl.ds(start, 64)], got.at[row], own_row).start()

    settle(front, own_row)

    lane = lax.broadcasted_iota(jnp.int32, (8, 128), 1)
    slope = jnp.where(lane < OVL, (lane.astype(F32) + 0.5) / OVL, 1.0)
    rest = jnp.where(lane < OVL, 1.0 - slope, 0.0)

    @pl.loop(0, 8)
    def _(quarter):
        columns = pl.ds(pl.multiple_of(quarter * QUARTER, QUARTER), QUARTER)
        settle(got.at[:7, columns], recv_row.at[quarter])

        at = pl.ds(pl.multiple_of(quarter * QUARTER, 8), 8)
        for a in range(4):
            items = []
            for p in range(8):
                re = got[p, at, 128 * a : 128 * a + 128]
                im = got[p, at, STRIDE + 128 * a : STRIDE + 128 * a + 128]
                if a == 0:
                    tail = got[(p - 1) % 8, at, 2 * STRIDE :]
                    re = slope * re + rest * tail
                    im = slope * im + rest * pltpu.roll(tail, 64, 1)
                items.append((re, im))
            done = fft_list(items, -1)
            for k in range(8):
                re, im = cscale(done[k], unit(-a * k / 32))
                mid[4 * k + a, 0, at, :] = re
                mid[4 * k + a, 1, at, :] = im

        @pl.loop(0, 8)
        def _(k):
            items = [(mid[4 * k + a, 0, at, :], mid[4 * k + a, 1, at, :]) for a in range(4)]
            done = fft_list(items, -1)
            for q in range(4):
                index = k + 8 * q
                tr = r_rows[0, pl.ds(index, 1), :]
                ti = r_rows[1, pl.ds(index, 1), :]
                re, im = cmul(*done[q], tr, ti)
                start = pl.ds(pl.multiple_of(index * QUARTER, 8), 8)
                work[start, :128] = re
                work[start, 128:] = im

        full = mm3(split(work[:256]), (r_mats[0], r_mats[1]))
        full = full.reshape(32, QUARTER, 256)
        kr, ki = r_rows[2][:, None, :], r_rows[3][:, None, :]
        re, im = cmul(full[:, :, :128], full[:, :, 128:], kr, ki)
        both = jnp.concatenate([re, im], axis=2).reshape(256, 256)
        work[:256] = mm3(split(both), (r_mats[2], r_mats[3]))

        at = pl.ds(pl.multiple_of(quarter * QUARTER, 8), 8)

        @pl.loop(0, 8)
        def _(k):
            items = []
            for q in range(4):
                index = k + 8 * q
                tr = r_rows[0, pl.ds(index, 1), :]
                ti = r_rows[1, pl.ds(index, 1), :]
                start = pl.ds(pl.multiple_of(index * QUARTER, 8), 8)
                items.append(cmul(work[start, :128], work[start, 128:], tr, -ti))
            done = fft_list(items, 1)
            for a in range(4):
                mid[4 * k + a, 0, at, :] = done[a][0]
                mid[4 * k + a, 1, at, :] = done[a][1]

        for a in range(4):
            items = [
                cscale((mid[4 * k + a, 0, at, :], mid[4 * k + a, 1, at, :]), unit(a * k / 32))
                for k in range(8)
            ]
            done = fft_list(items, 1)
            for p in range(8):
                mid[4 * p + a, 0, at, :] = done[p][0]
                mid[4 * p + a, 1, at, :] = done[p][1]

    me = row * 16 + col

    def peers(step):
        tr = lax.rem(xh + 1 + step // 16, 2) * 4 + lax.rem(z + 2 + (step // 4) % 4, 4)
        ty = lax.rem(y + 2 + step % 4, 4)
        ends = []
        for i in range(2):
            for j in range(2):
                ends.append((tr, ty * 4 + lax.rem(xl + i, 2) * 2 + lax.rem(core + j, 2)))
        return tr * 4 + ty, ends

    own_step = 26

    def give_all(step, ends, part):
        lines = slice(part * 16, part * 16 + 16)
        for index, (tr, tc) in enumerate(ends):
            def go(tr=tr, tc=tc):
                pltpu.make_async_remote_copy(
                    give.at[tr * 16 + tc, lines], have.at[me, lines],
                    send_sem.at[1], recv_all.at[part], device_id=(tr, tc), device_id_type=MESH,
                ).start()

            if index:
                go()
            else:
                pl.when(step != own_step)(go)

    pl.semaphore_wait(ready, 15)

    @pl.loop(0, 32)
    def _(step):
        block, ends = peers(step)
        flat = jnp.transpose(mid[block].reshape(128, 128))
        for i in range(4):
            give[block * 4 + i] = flat[32 * i : 32 * i + 32]
        give_all(step, ends, 0)

    own = pltpu.make_async_copy(give.at[me], have.at[me], own_all)
    own.start()

    @pl.loop(0, 32)
    def _(step):
        give_all(step, peers(step)[1], 1)

    own.wait()

    left = lane < 64
    inner = col_tables()[2]

    @pl.loop(0, 2)
    def _(part):
        lines = pl.ds(pl.multiple_of(part * 16, 16), 16)
        top = pl.ds(pl.multiple_of(part * 16, 8), 8)
        low = pl.ds(pl.multiple_of(part * 16 + 8, 8), 8)
        settle(have.at[:127, lines], recv_all.at[part])

        for r in range(8):
            items = []
            for c in range(16):
                a = have[16 * r + c, top, :]
                b = have[16 * r + c, low, :]
                re = jnp.where(left, a, pltpu.roll(b, 64, 1))
                im = jnp.where(left, pltpu.roll(a, 64, 1), b)
                items.append((re, im))
            done = fft_list(items, -1)
            for k in range(16):
                flat = 8 * (16 * r + k)
                re, im = cscale(done[k], inner[r, k])
                work[flat : flat + 8, :128] = re
                work[flat : flat + 8, 128:] = im

        @pl.loop(0, 16)
        def _(k):
            places = [pl.ds(pl.multiple_of(8 * (16 * r + k), 8), 8) for r in range(8)]
            items = [(work[at, :128], work[at, 128:]) for at in places]
            done = fft_list(items, -1)
            for q in range(8):
                tr = c_rows[0, pl.ds(16 * q + k, 1), :]
                ti = c_rows[1, pl.ds(16 * q + k, 1), :]
                re, im = cmul(*done[q], tr, ti)
                work[places[q], :128] = re
                work[places[q], 128:] = im

        @pl.loop(0, 2)
        def _(n):
            at = pl.ds(pl.multiple_of(n * 512, 512), 512)
            keep = pl.ds(pl.multiple_of(n * 64, 64), 64)
            full = mm3(split(work[at, :]), (c_mats[0], c_mats[1]))
            full = full.reshape(64, 8, 256)
            kr, ki = c_rows[2, keep, :][:, None, :], c_rows[3, keep, :][:, None, :]
            re, im = cmul(full[:, :, :128], full[:, :, 128:], kr, ki)
            both = jnp.concatenate([re, im], axis=2).reshape(512, 256)
            work[at, :] = mm3(split(both), (c_mats[2], c_mats[3]))

        @pl.loop(0, 16)
        def _(k):
            places = [pl.ds(pl.multiple_of(8 * (16 * r + k), 8), 8) for r in range(8)]
            items = []
            for q in range(8):
                tr = c_rows[0, pl.ds(16 * q + k, 1), :]
                ti = c_rows[1, pl.ds(16 * q + k, 1), :]
                items.append(cmul(work[places[q], :128], work[places[q], 128:], tr, -ti))
            done = fft_list(items, 1)
            for r in range(8):
                work[places[r], :128] = done[r][0]
                work[places[r], 128:] = done[r][1]

        for r in range(8):
            items = []
            for k in range(16):
                flat = 8 * (16 * r + k)
                value = (work[flat : flat + 8, :128], work[flat : flat + 8, 128:])
                items.append(cscale(value, np.conj(inner[r, k])))
            done = fft_list(items, 1)
            for c in range(16):
                flat = 8 * (16 * r + c)
                work[flat : flat + 8, :128] = done[c][0]
                work[flat : flat + 8, 128:] = done[c][1]

        @pl.loop(0, 16)
        def _(c):
            for piece in range(2):
                lanes = slice(128 * piece, 128 * piece + 128)
                for pair in range(4):
                    first = pl.ds(pl.multiple_of(8 * (32 * pair + c), 8), 8)
                    second = pl.ds(pl.multiple_of(8 * (32 * pair + 16 + c), 8), 8)
                    a = work[first, lanes]
                    b = work[second, lanes]
                    to = slice(128 * pair, 128 * pair + 128)
                    send[c, piece, top, to] = jnp.where(left, a, pltpu.roll(b, 64, 1))
                    send[c, piece, low, to] = jnp.where(left, pltpu.roll(a, 64, 1), b)

        mine = pl.ds(pl.multiple_of(col * 32 + part * 16, 16), 16)
        for i, j, k in FAR_COLS:
            tc = lax.rem(y + i, 4) * 4 + lax.rem(xl + j, 2) * 2 + lax.rem(core + k, 2)
            pltpu.make_async_remote_copy(
                send.at[tc, :, lines], out.at[:, mine],
                send_sem.at[2], recv_col.at[part], device_id=(row, tc), device_id_type=MESH,
            ).start()
        pltpu.make_async_copy(send.at[col, :, lines], out.at[:, mine], own_sem.at[part]).start()

    for part in range(2):
        settle(send.at[:15, :, :16], recv_col.at[part])
        settle(send.at[0, :, :16], own_sem.at[part])
    settle(got.at[:7], send_sem.at[0])
    settle(have.at[:127], send_sem.at[1])
    settle(send.at[:15], send_sem.at[2])


def field_step(z_hi, z_lo, r_hi, r_lo):
    r_rows, r_mats = row_tables()
    c_rows, c_mats, _ = col_tables()
    return pl.pallas_call(
        field_body,
        out_shape=jax.ShapeDtypeStruct((2, STRIDE, STRIDE), F32),
        in_specs=[vmem()] * 8,
        out_specs=vmem(),
        scratch_shapes=[
            pltpu.VMEM((TILE, 2 * TILE), F32),
            pltpu.VMEM((OVL, 2 * TILE), F32),
            pltpu.VMEM((OVL, 2 * TILE), F32),
            pltpu.VMEM((8, 64, 2 * TILE), F32),
            pltpu.VMEM((1024, 256), F32),
            pltpu.VMEM((32, 2, 64, 128), F32),
            pltpu.VMEM((128, 32, 128), F32),
            pltpu.VMEM((128, 32, 128), F32),
            pltpu.VMEM((16, 2, 32, STRIDE), F32),
            pltpu.SemaphoreType.DMA((2,)),
            pltpu.SemaphoreType.DMA((3,)),
            pltpu.SemaphoreType.DMA((8,)),
            pltpu.SemaphoreType.DMA(()),
            pltpu.SemaphoreType.DMA((2,)),
            pltpu.SemaphoreType.DMA(()),
            pltpu.SemaphoreType.DMA((2,)),
            pltpu.SemaphoreType.DMA((2,)),
            pltpu.SemaphoreType.REGULAR,
        ],
        compiler_params=pltpu.CompilerParams(
            vmem_limit_bytes=B_LIMIT << 20, collective_id=0, has_side_effects=True
        ),
        name="field_step",
    )(z_hi, z_lo, r_hi, r_lo, r_rows, r_mats, c_rows, c_mats)


def local(tiles, pupils, intensity, offsets):
    return field_step(*tile_step(tiles, pupils, intensity, offsets[0, 0]))


def solution(mesh):
    placed = (
        P(None, "row", "col"),
        P(None, "row", "col"),
        P(None, "row", "col"),
        P("row", "col", None, None),
    )
    return jax.shard_map(
        local, mesh=mesh, in_specs=placed, out_specs=P(None, "row", "col"), check_vma=False
    )
```

```python
import math

import numpy as np
import ml_dtypes
import jax
import jax.numpy as jnp
from jax import lax
from jax.experimental import pallas as pl
from jax.experimental.pallas import tpu as pltpu
from jax.sharding import PartitionSpec as P

TILE = 576
PAD = 640
OVL = 64
WIN = 128
LEDS = 16
STRIDE = 512
ROWS = 4096
COLS = 8192
FRESNEL = 2048
STEP_SIZE = 0.05
RADIX = 6
SUB = TILE // RADIX
BF = jnp.bfloat16
F32 = jnp.float32
GROUP = 8
A_LIMIT = 38
B_LIMIT = 24


def split_np(table):
    table = np.asarray(table, np.float64)
    high = table.astype(np.float32).astype(ml_dtypes.bfloat16)
    low = (table - high.astype(np.float64)).astype(np.float32).astype(ml_dtypes.bfloat16)
    return high, low


def unit(turns):
    turns = np.asarray(turns, np.float64)
    return np.exp(2j * np.pi * (turns - np.floor(turns)))


def right_block(table):
    return np.block([[table.real, table.imag], [-table.imag, table.real]])


def left_block(table):
    return np.block([[table.real, -table.imag], [table.imag, table.real]])


def dft_np(length, sign):
    index = np.arange(length)
    return unit(sign * (index[:, None] * index[None, :] % length) / length)


def axis_filter(length):
    freq = np.arange(length)
    signed = np.where(freq < length // 2, freq, freq - length).astype(np.float64)
    turns = signed * signed * (FRESNEL / (length * length))
    return np.exp(-2.0 * signed * signed / (length * length)) * unit(-turns) / length


def split(value):
    high = value.astype(BF)
    low = (value - high.astype(F32)).astype(BF)
    return high, low


def mm(left, right):
    return jnp.dot(left, right, preferred_element_type=F32)


def mm3(left, right):
    return mm(left[0], right[0]) + (mm(left[1], right[0]) + mm(left[0], right[1]))


def mm_nt(left, right):
    return lax.dot_general(left, right, (((1,), (1,)), ((), ())), preferred_element_type=F32)


def cmul(ar, ai, br, bi):
    return ar * br - ai * bi, ar * bi + ai * br


def cscale(value, factor):
    re, im = value
    fr, fi = float(factor.real), float(factor.imag)
    near = 1e-12
    if abs(fi) < near:
        if abs(fr - 1) < near:
            return re, im
        if abs(fr + 1) < near:
            return -re, -im
    if abs(fr) < near:
        if abs(fi - 1) < near:
            return -im, re
        if abs(fi + 1) < near:
            return im, -re
    if abs(abs(fr) - abs(fi)) < near:
        size = abs(fr)
        sr, si = math.copysign(1, fr), math.copysign(1, fi)
        left = re if sr > 0 else -re
        low = im if sr > 0 else -im
        new_re = left - im if si > 0 else left + im
        new_im = low + re if si > 0 else low - re
        return new_re * size, new_im * size
    return re * fr - im * fi, re * fi + im * fr


def fft_list(items, sign):
    count = len(items)
    if count == 1:
        return items
    if count == 3:
        (ar, ai), (br, bi), (cr, ci) = items
        sr, si, dr, di = br + cr, bi + ci, br - cr, bi - ci
        mr, mi = ar - 0.5 * sr, ai - 0.5 * si
        root = sign * math.sqrt(0.75)
        tr, ti = -root * di, root * dr
        return [(ar + sr, ai + si), (mr + tr, mi + ti), (mr - tr, mi - ti)]
    even = fft_list(items[0::2], sign)
    odd = fft_list(items[1::2], sign)
    half = count // 2
    first, second = [], []
    for index in range(half):
        turned = cscale(odd[index], unit(sign * index / count))
        er, ei = even[index]
        first.append((er + turned[0], ei + turned[1]))
        second.append((er - turned[0], ei - turned[1]))
    return first + second


def tile_tables():
    index = np.arange(TILE)
    low = unit(-(np.arange(24)[:, None] * index[None, :] % TILE) / TILE) / math.sqrt(TILE)
    high = unit(-(24 * np.arange(24)[:, None] * index[None, :] % TILE) / TILE)
    seeds = np.zeros((4, 24, PAD), np.float32)
    seeds[0, :, :TILE], seeds[1, :, :TILE] = low.real, low.imag
    seeds[2, :, :TILE], seeds[3, :, :TILE] = high.real, high.imag
    small = np.arange(SUB)
    forward, inverse = [], []
    for part in range(RADIX):
        turned = unit(-(part * small[:, None] + RADIX * small[:, None] * small[None, :]) / TILE)
        turned = turned / math.sqrt(TILE)
        forward.append(left_block(turned))
        inverse.append(left_block(np.conj(turned.T)))
    forward = np.stack(split_np(np.stack(forward)))
    inverse = np.stack(split_np(np.stack(inverse)))
    window = dft_np(WIN, -1) / math.sqrt(WIN)
    lanes = np.stack(split_np(right_block(np.conj(window))))
    sides = np.stack(
        [*split_np(left_block(np.conj(window))), *split_np(left_block(window))]
    )
    return seeds, forward, inverse, lanes, sides


def cut(ref, part, row, first, back):
    base = pl.multiple_of((row // 8) * 8, 8)
    down = row - base
    wide = ref[part, pl.ds(base, WIN + 8), pl.ds(first, 256)]
    wide = pltpu.roll(wide, back, 1)[:, :WIN].reshape(WIN // 8 + 1, 8, WIN)
    wide = pltpu.roll(wide, lax.rem(8 - down, 8), 1)
    lane = lax.broadcasted_iota(jnp.int32, (WIN // 8, 8, WIN), 1)
    return jnp.where(lane < 8 - down, wide[:-1], wide[1:]).reshape(WIN, WIN)


def add(ref, part, row, first, shift, value):
    base = pl.multiple_of((row // 8) * 8, 8)
    down = row - base
    turned = pltpu.roll(value.reshape(WIN // 8, 8, WIN), down, 1)
    zero = jnp.zeros((1, 8, WIN), F32)
    lane = lax.broadcasted_iota(jnp.int32, (WIN // 8 + 1, 8, WIN), 1)
    upper = jnp.concatenate([zero, turned], axis=0)
    lower = jnp.concatenate([turned, zero], axis=0)
    tall = jnp.where(lane < down, upper, lower).reshape(WIN + 8, WIN)
    wide = jnp.concatenate([tall, jnp.zeros((WIN + 8, 128), F32)], axis=1)
    here = (part, pl.ds(base, WIN + 8), pl.ds(first, 256))
    ref[here] = ref[here] + pltpu.roll(wide, shift, 1)


def tile_body(
    offs, tiles_in, pupils_in, intensity_in, seeds_in, fwd_in, inv_in, lanes_in, sides_in,
    z_hi, z_lo, r_hi, r_lo,
    base, y, sub, spec, wins_a, wins_b, turned,
    tiles, raw, pupils, intensity, seeds, fwd, inv, lanes, sides, sems,
):
    pairs = [(seeds_in, seeds), (tiles_in, raw), (fwd_in, fwd)]
    pairs += [(pupils_in, pupils), (intensity_in, intensity)]
    pairs += [(lanes_in, lanes), (sides_in, sides), (inv_in, inv)]
    loads = [
        pltpu.make_async_copy(source, target, sems.at[index])
        for index, (source, target) in enumerate(pairs)
    ]
    for load in loads:
        load.start()
    loads[0].wait()

    low_r, low_i = seeds[0], seeds[1]

    @pl.loop(0, 24)
    def _(a):
        hr = seeds[2, pl.ds(a, 1), :]
        hi = seeds[3, pl.ds(a, 1), :]
        tr, ti = cmul(low_r, low_i, hr, hi)
        start = pl.multiple_of(a * 24, 8)
        base[0, pl.ds(start, 24), :] = tr
        base[1, pl.ds(start, 24), :] = ti

    for ref in (r_hi, r_lo):
        zero_tail = jnp.zeros((PAD - TILE, 2 * TILE), BF)
        ref[TILE:PAD, :] = zero_tail
        ref[PAD + TILE :, :] = zero_tail

    @pl.loop(0, TILE // 96)
    def _(a):
        start = pl.multiple_of(a * 96, 16)
        re, im = base[0, pl.ds(start, 96), :], base[1, pl.ds(start, 96), :]
        for offset, left, right in ((0, re, -im), (PAD, im, re)):
            at = pl.ds(start + offset, 96)
            ends = left[:, STRIDE:] + pltpu.roll(right[:, STRIDE:], 64, 1)
            for where, value in (
                (slice(0, STRIDE), left[:, :STRIDE]),
                (slice(STRIDE, 2 * STRIDE), right[:, :STRIDE]),
                (slice(2 * STRIDE, 2 * TILE), ends),
            ):
                high, low = split(value)
                r_hi[at, where] = high
                r_lo[at, where] = low

    def forward():
        @pl.loop(0, RADIX)
        def _(b):
            rows = pl.ds(b, SUB, stride=RADIX)
            parts = [
                jnp.concatenate([tiles[part, n, rows, :] for n in range(5)], axis=1)
                for part in range(2)
            ]
            sub[b] = mm3((fwd[0, b], fwd[1, b]), split(jnp.concatenate(parts, axis=0)))

        @pl.loop(0, PAD // 128)
        def _(n):
            at = pl.ds(pl.multiple_of(n * 128, 128), 128)
            for row in range(0, SUB, 8):
                items = [
                    (sub[b, row : row + 8, at], sub[b, SUB + row : SUB + row + 8, at])
                    for b in range(RADIX)
                ]
                done = fft_list(items, -1)
                for k in range(RADIX):
                    here = slice(k * SUB + row, k * SUB + row + 8)
                    spec[0, here, at] = done[k][0]
                    spec[1, here, at] = done[k][1]

    loads[1].wait()
    for part in range(2):
        for n in range(5):
            width = min(128, TILE - 128 * n)
            tiles[part, n, :, :width] = raw[part, :, 128 * n : 128 * n + width]
    loads[2].wait()
    forward()

    def flip(part, at, count, to):
        for i in range(4):
            block = jnp.transpose(spec[part, 128 * i : 128 * i + 128, at])
            tiles[part, i, to, :] = block[:count]
        half = jnp.concatenate([spec[part, STRIDE:TILE, at], jnp.zeros((64, 128), F32)], axis=0)
        tiles[part, 4, to, :] = jnp.transpose(half)[:count]

    for part in range(2):
        @pl.loop(0, 4)
        def _(j):
            at = pl.ds(pl.multiple_of(j * 128, 128), 128)
            flip(part, at, 128, at)

        flip(part, slice(STRIDE, PAD), 64, slice(STRIDE, TILE))

    forward()

    for part in range(2):
        spec[part, TILE:, :] = jnp.zeros((8, PAD), F32)
    for load in loads[3:]:
        load.wait()
    for part in range(2):
        turned[part] = jnp.transpose(pupils[part])
    inv_lanes = (lanes[0], lanes[1])
    inv_sides = (sides[0], sides[1])
    fwd_sides = (sides[2], sides[3])

    def sides_nt(table, value):
        high, low = split(value)
        return mm_nt(table[0], high) + (mm_nt(table[1], high) + mm_nt(table[0], low))

    def restack(win_b, value):
        for j in range(GROUP):
            win_b[j * WIN : (j + 1) * WIN, :WIN] = value[:WIN, j * WIN : (j + 1) * WIN]
            win_b[j * WIN : (j + 1) * WIN, WIN:] = value[WIN:, j * WIN : (j + 1) * WIN]

    pr, pi = turned[0], turned[1]
    for step in range(LEDS // GROUP):
        win_b = wins_b.at[step]
        for j in range(GROUP):
            led = step * GROUP + j
            row, col = offs[1, led], offs[0, led]
            first = pl.multiple_of((col // 128) * 128, 128)
            back = lax.rem(first + 256 - col, 256)
            cr = cut(spec, 0, row, first, back)
            ci = cut(spec, 1, row, first, back)
            wr, wi = cmul(pr, pi, cr, ci)
            win_b[j * WIN : (j + 1) * WIN, :WIN] = wr
            win_b[j * WIN : (j + 1) * WIN, WIN:] = wi

    for step in range(LEDS // GROUP):
        win_a, win_b = wins_a.at[step], wins_b.at[step]
        pr, pi = turned[0], turned[1]
        restack(win_b, sides_nt(inv_sides, win_b[...]))
        wave = mm3(split(win_b[...]), inv_lanes)
        for j in range(GROUP):
            wr = wave[j * WIN : (j + 1) * WIN, :WIN]
            wi = wave[j * WIN : (j + 1) * WIN, WIN:]
            excess = wr * wr + wi * wi - intensity[step * GROUP + j]
            win_a[:WIN, j * WIN : (j + 1) * WIN] = wr * excess
            win_a[WIN:, j * WIN : (j + 1) * WIN] = wi * excess
        restack(win_b, mm3(fwd_sides, split(win_a[...])))
        win_a[...] = sides_nt(fwd_sides, win_b[...])
        for j in range(GROUP):
            led = step * GROUP + j
            row, col = offs[1, led], offs[0, led]
            first = pl.multiple_of((col // 128) * 128, 128)
            shift = col - first
            gr = win_a[:WIN, j * WIN : (j + 1) * WIN] * -STEP_SIZE
            gi = win_a[WIN:, j * WIN : (j + 1) * WIN] * -STEP_SIZE
            ur, ui = cmul(pr, -pi, gr, gi)
            add(spec, 0, row, first, shift, ur)
            add(spec, 1, row, first, shift, ui)

    @pl.loop(0, PAD // 128)
    def _(n):
        at = pl.ds(pl.multiple_of(n * 128, 128), 128)
        for row in range(0, SUB, 8):
            items = []
            for k in range(RADIX):
                here = slice(k * SUB + row, k * SUB + row + 8)
                items.append((spec[0, here, at], spec[1, here, at]))
            done = fft_list(items, 1)
            for b in range(RADIX):
                sub[b, row : row + 8, at] = done[b][0]
                sub[b, SUB + row : SUB + row + 8, at] = done[b][1]

    @pl.loop(0, RADIX)
    def _(b):
        mixed = mm3((inv[0, b], inv[1, b]), split(sub[b]))
        rows = pl.ds(b, SUB, stride=RADIX)
        for n in range(5):
            y[n, rows, :] = mixed[:SUB, 128 * n : 128 * n + 128]
            y[5 + n, rows, :] = mixed[SUB:, 128 * n : 128 * n + 128]

    for n in range(10):
        at = slice(128 * n, 128 * n + 128)
        high, low = split(y[n])
        z_hi[:, at] = high
        z_lo[:, at] = low


def vmem():
    return pl.BlockSpec(memory_space=pltpu.VMEM)


def tile_step(tiles, pupils, intensity, offsets):
    seeds, fwd, inv, lanes, sides = tile_tables()
    held = (pupils, intensity, seeds, fwd, inv, lanes, sides)
    return pl.pallas_call(
        tile_body,
        out_shape=[
            jax.ShapeDtypeStruct((TILE, 2 * PAD), BF),
            jax.ShapeDtypeStruct((TILE, 2 * PAD), BF),
            jax.ShapeDtypeStruct((2 * PAD, 2 * TILE), BF),
            jax.ShapeDtypeStruct((2 * PAD, 2 * TILE), BF),
        ],
        in_specs=[pl.BlockSpec(memory_space=pltpu.SMEM)]
        + [pl.BlockSpec(memory_space=pltpu.HBM)] * 8,
        out_specs=[vmem()] * 4,
        scratch_shapes=[
            pltpu.VMEM((2, TILE, PAD), F32),
            pltpu.VMEM((2 * PAD // 128, TILE, 128), F32),
            pltpu.VMEM((RADIX, 2 * SUB, PAD), F32),
            pltpu.VMEM((2, TILE + 8, PAD), F32),
            pltpu.VMEM((LEDS // GROUP, 2 * WIN, GROUP * WIN), F32),
            pltpu.VMEM((LEDS // GROUP, GROUP * WIN, 2 * WIN), F32),
            pltpu.VMEM((2, WIN, WIN), F32),
            pltpu.VMEM((2, PAD // 128, TILE, 128), F32),
            pltpu.VMEM((2, TILE, TILE), F32),
            *[pltpu.VMEM(value.shape, value.dtype) for value in held],
            pltpu.SemaphoreType.DMA((8,)),
        ],
        compiler_params=pltpu.CompilerParams(vmem_limit_bytes=A_LIMIT << 20),
        name="tile_step",
    )(
        *[
            pltpu.with_memory_space_constraint(jnp.asarray(value), pltpu.HBM)
            for value in (offsets, tiles, *held)
        ]
    )


def row_tables():
    lane = np.arange(128)
    k1 = np.arange(32)
    turn = unit(-(k1[:, None] * lane[None, :]) / ROWS)
    keep = axis_filter(ROWS)[k1[:, None] + 32 * lane[None, :]]
    rows = np.stack([turn.real, turn.imag, keep.real, keep.imag]).astype(np.float32)
    full = dft_np(128, -1)
    mats = np.stack([*split_np(right_block(full)), *split_np(right_block(np.conj(full)))])
    return rows, mats


def col_tables():
    lane = np.arange(64)
    kc = np.arange(16)
    kr = np.arange(8)
    low = kc[None, :] + 16 * kr[:, None]
    turn = unit(-(low[:, :, None] * lane) / COLS)
    keep = axis_filter(COLS)[low[:, :, None] + 128 * lane]
    rows = np.stack([turn.real, turn.imag, keep.real, keep.imag]).reshape(4, 128, 64)
    rows = np.concatenate([rows, rows], axis=2).astype(np.float32)
    inner = unit(-(np.arange(8)[:, None] * kc[None, :]) / 128)
    full = np.kron(np.eye(2), dft_np(64, -1))
    mats = np.stack([*split_np(right_block(full)), *split_np(right_block(np.conj(full)))])
    return rows, mats, inner


MESH = pl.DeviceIdType.MESH
FAR_ROWS = ((1, 2), (1, 1), (1, 3), (0, 2), (1, 0), (0, 1), (0, 3))
FAR_COLS = sorted(
    ((y, x, k) for y in range(4) for x in range(2) for k in range(2) if y or x or k),
    key=lambda step: -(min(step[0], 4 - step[0]) + step[1]),
)
QUARTER = 8


def settle(ref, sem):
    pltpu.make_async_copy(ref, ref, sem).wait()


def field_body(
    z_hi, z_lo, r_hi, r_lo, r_rows, r_mats, c_rows, c_mats, out,
    refined, halo, front, got, work, mid, give, have, send,
    halo_sem, send_sem, recv_row, own_row, recv_all, own_all, recv_col, own_sem, ready,
):
    row, col = lax.axis_index("row"), lax.axis_index("col")
    xh, z = row // 4, lax.rem(row, 4)
    y, xl, core = col // 4, lax.rem(col // 2, 2), lax.rem(col, 2)
    rows_at = [lax.rem(row + step, 8) for step in range(8)]
    cols_at = [lax.rem(col + step, 16) for step in range(16)]

    barrier = pltpu.get_barrier_semaphore()
    for i in range(1, 8):
        pl.semaphore_signal(barrier, inc=1, device_id=(rows_at[i], col), device_id_type=MESH)
    for j in range(1, 16):
        pl.semaphore_signal(barrier, inc=1, device_id=(row, cols_at[j]), device_id_type=MESH)

    chunks = [lax.rem(xh + i, 2) * 4 + lax.rem(z + j, 4) for i, j in FAR_ROWS]

    def columns_of(blocks):
        places = [pl.ds(pl.multiple_of(block * 64, 64), 64) for block in blocks]

        def fill(at):
            high = jnp.concatenate([z_hi[place, :] for place in places], axis=0)
            low = jnp.concatenate([z_lo[place, :] for place in places], axis=0)
            value = mm3((high, low), (r_hi[:, at], r_lo[:, at]))
            for index, place in enumerate(places):
                refined[place, at] = value[64 * index : 64 * index + 64]

        @pl.loop(0, 4)
        def _(n):
            fill(pl.ds(pl.multiple_of(n * 256, 256), 256))

        fill(slice(1024, 1152))

    columns_of([8, *chunks[:2]])
    pl.semaphore_wait(barrier, 22)
    for j in range(1, 16):
        pl.semaphore_signal(ready, inc=1, device_id=(row, cols_at[j]), device_id_type=MESH)

    edge = pltpu.make_async_remote_copy(
        refined.at[STRIDE:], halo, halo_sem.at[0], halo_sem.at[1],
        device_id=(row, cols_at[1]), device_id_type=MESH,
    )
    edge.start()

    def give_row(target, quarter, source):
        pltpu.make_async_remote_copy(
            source, got.at[row, quarter * QUARTER : (quarter + 1) * QUARTER],
            send_sem.at[0], recv_row.at[quarter], device_id=(target, col), device_id_type=MESH,
        ).start()

    def plain(target, quarter):
        start = pl.multiple_of(target * 64 + quarter * QUARTER, QUARTER)
        return refined.at[pl.ds(start, QUARTER)]

    def blended(quarter):
        return front.at[quarter * QUARTER : (quarter + 1) * QUARTER]

    def give_plain(targets, quarter=0):
        for target in targets:
            @pl.when(target != 0)
            def _():
                give_row(target, quarter, plain(target, quarter))

    def give_blended(quarter):
        for target in chunks:
            @pl.when(target == 0)
            def _():
                give_row(target, quarter, blended(quarter))

    give_plain(chunks[:2])
    columns_of(chunks[2:5])
    give_plain(chunks[2:5])
    columns_of([*chunks[5:], row])
    give_plain(chunks[5:])
    for quarter in range(1, 4):
        give_plain(chunks, quarter)

    edge.wait()
    place = lax.broadcasted_iota(jnp.int32, (OVL, 2 * TILE), 0).astype(F32)
    ramp = (place + 0.5) / OVL
    front[...] = ramp * refined[:OVL] + (1.0 - ramp) * halo[...]

    for quarter in range(4):
        give_blended(quarter)
    for quarter in range(4, 8):
        give_plain(chunks, quarter)
        give_blended(quarter)

    @pl.when(row == 0)
    def _():
        pltpu.make_async_copy(front, got.at[0], own_row).start()

    @pl.when(row != 0)
    def _():
        start = pl.multiple_of(row * 64, 64)
        pltpu.make_async_copy(refined.at[pl.ds(start, 64)], got.at[row], own_row).start()

    settle(front, own_row)

    lane = lax.broadcasted_iota(jnp.int32, (8, 128), 1)
    slope = jnp.where(lane < OVL, (lane.astype(F32) + 0.5) / OVL, 1.0)
    rest = jnp.where(lane < OVL, 1.0 - slope, 0.0)

    @pl.loop(0, 8)
    def _(quarter):
        columns = pl.ds(pl.multiple_of(quarter * QUARTER, QUARTER), QUARTER)
        settle(got.at[:7, columns], recv_row.at[quarter])

        at = pl.ds(pl.multiple_of(quarter * QUARTER, 8), 8)
        for a in range(4):
            items = []
            for p in range(8):
                re = got[p, at, 128 * a : 128 * a + 128]
                im = got[p, at, STRIDE + 128 * a : STRIDE + 128 * a + 128]
                if a == 0:
                    tail = got[(p - 1) % 8, at, 2 * STRIDE :]
                    re = slope * re + rest * tail
                    im = slope * im + rest * pltpu.roll(tail, 64, 1)
                items.append((re, im))
            done = fft_list(items, -1)
            for k in range(8):
                re, im = cscale(done[k], unit(-a * k / 32))
                mid[4 * k + a, 0, at, :] = re
                mid[4 * k + a, 1, at, :] = im

        @pl.loop(0, 8)
        def _(k):
            items = [(mid[4 * k + a, 0, at, :], mid[4 * k + a, 1, at, :]) for a in range(4)]
            done = fft_list(items, -1)
            for q in range(4):
                index = k + 8 * q
                tr = r_rows[0, pl.ds(index, 1), :]
                ti = r_rows[1, pl.ds(index, 1), :]
                re, im = cmul(*done[q], tr, ti)
                start = pl.ds(pl.multiple_of(index * QUARTER, 8), 8)
                work[start, :128] = re
                work[start, 128:] = im

        full = mm3(split(work[:256]), (r_mats[0], r_mats[1]))
        full = full.reshape(32, QUARTER, 256)
        kr, ki = r_rows[2][:, None, :], r_rows[3][:, None, :]
        re, im = cmul(full[:, :, :128], full[:, :, 128:], kr, ki)
        both = jnp.concatenate([re, im], axis=2).reshape(256, 256)
        work[:256] = mm3(split(both), (r_mats[2], r_mats[3]))

        at = pl.ds(pl.multiple_of(quarter * QUARTER, 8), 8)

        @pl.loop(0, 8)
        def _(k):
            items = []
            for q in range(4):
                index = k + 8 * q
                tr = r_rows[0, pl.ds(index, 1), :]
                ti = r_rows[1, pl.ds(index, 1), :]
                start = pl.ds(pl.multiple_of(index * QUARTER, 8), 8)
                items.append(cmul(work[start, :128], work[start, 128:], tr, -ti))
            done = fft_list(items, 1)
            for a in range(4):
                mid[4 * k + a, 0, at, :] = done[a][0]
                mid[4 * k + a, 1, at, :] = done[a][1]

        for a in range(4):
            items = [
                cscale((mid[4 * k + a, 0, at, :], mid[4 * k + a, 1, at, :]), unit(a * k / 32))
                for k in range(8)
            ]
            done = fft_list(items, 1)
            for p in range(8):
                mid[4 * p + a, 0, at, :] = done[p][0]
                mid[4 * p + a, 1, at, :] = done[p][1]

    me = row * 16 + col

    def peers(step):
        tr = lax.rem(xh + 1 + step // 16, 2) * 4 + lax.rem(z + 2 + (step // 4) % 4, 4)
        ty = lax.rem(y + 2 + step % 4, 4)
        ends = []
        for i in range(2):
            for j in range(2):
                ends.append((tr, ty * 4 + lax.rem(xl + i, 2) * 2 + lax.rem(core + j, 2)))
        return tr * 4 + ty, ends

    own_step = 26

    def give_all(step, ends, part):
        lines = slice(part * 16, part * 16 + 16)
        for index, (tr, tc) in enumerate(ends):
            def go(tr=tr, tc=tc):
                pltpu.make_async_remote_copy(
                    give.at[tr * 16 + tc, lines], have.at[me, lines],
                    send_sem.at[1], recv_all.at[part], device_id=(tr, tc), device_id_type=MESH,
                ).start()

            if index:
                go()
            else:
                pl.when(step != own_step)(go)

    pl.semaphore_wait(ready, 15)

    @pl.loop(0, 32)
    def _(step):
        block, ends = peers(step)
        flat = jnp.transpose(mid[block].reshape(128, 128))
        for i in range(4):
            give[block * 4 + i] = flat[32 * i : 32 * i + 32]
        give_all(step, ends, 0)

    own = pltpu.make_async_copy(give.at[me], have.at[me], own_all)
    own.start()

    @pl.loop(0, 32)
    def _(step):
        give_all(step, peers(step)[1], 1)

    own.wait()

    left = lane < 64
    inner = col_tables()[2]

    @pl.loop(0, 2)
    def _(part):
        lines = pl.ds(pl.multiple_of(part * 16, 16), 16)
        top = pl.ds(pl.multiple_of(part * 16, 8), 8)
        low = pl.ds(pl.multiple_of(part * 16 + 8, 8), 8)
        settle(have.at[:127, lines], recv_all.at[part])

        for r in range(8):
            items = []
            for c in range(16):
                a = have[16 * r + c, top, :]
                b = have[16 * r + c, low, :]
                re = jnp.where(left, a, pltpu.roll(b, 64, 1))
                im = jnp.where(left, pltpu.roll(a, 64, 1), b)
                items.append((re, im))
            done = fft_list(items, -1)
            for k in range(16):
                flat = 8 * (16 * r + k)
                re, im = cscale(done[k], inner[r, k])
                work[flat : flat + 8, :128] = re
                work[flat : flat + 8, 128:] = im

        for k in range(16):
            places = [slice(8 * (16 * r + k), 8 * (16 * r + k) + 8) for r in range(8)]
            items = [(work[at, :128], work[at, 128:]) for at in places]
            done = fft_list(items, -1)
            for q in range(8):
                tr = c_rows[0, 16 * q + k : 16 * q + k + 1, :]
                ti = c_rows[1, 16 * q + k : 16 * q + k + 1, :]
                re, im = cmul(*done[q], tr, ti)
                work[places[q], :128] = re
                work[places[q], 128:] = im

        @pl.loop(0, 2)
        def _(n):
            at = pl.ds(pl.multiple_of(n * 512, 512), 512)
            keep = pl.ds(pl.multiple_of(n * 64, 64), 64)
            full = mm3(split(work[at, :]), (c_mats[0], c_mats[1]))
            full = full.reshape(64, 8, 256)
            kr, ki = c_rows[2, keep, :][:, None, :], c_rows[3, keep, :][:, None, :]
            re, im = cmul(full[:, :, :128], full[:, :, 128:], kr, ki)
            both = jnp.concatenate([re, im], axis=2).reshape(512, 256)
            work[at, :] = mm3(split(both), (c_mats[2], c_mats[3]))

        for k in range(16):
            places = [slice(8 * (16 * r + k), 8 * (16 * r + k) + 8) for r in range(8)]
            items = []
            for q in range(8):
                tr = c_rows[0, 16 * q + k : 16 * q + k + 1, :]
                ti = c_rows[1, 16 * q + k : 16 * q + k + 1, :]
                items.append(cmul(work[places[q], :128], work[places[q], 128:], tr, -ti))
            done = fft_list(items, 1)
            for r in range(8):
                work[places[r], :128] = done[r][0]
                work[places[r], 128:] = done[r][1]

        for r in range(8):
            items = []
            for k in range(16):
                flat = 8 * (16 * r + k)
                value = (work[flat : flat + 8, :128], work[flat : flat + 8, 128:])
                items.append(cscale(value, np.conj(inner[r, k])))
            done = fft_list(items, 1)
            for c in range(16):
                flat = 8 * (16 * r + c)
                work[flat : flat + 8, :128] = done[c][0]
                work[flat : flat + 8, 128:] = done[c][1]

        def pack(c):
            for piece in range(2):
                lanes = slice(128 * piece, 128 * piece + 128)
                for pair in range(4):
                    first = pl.ds(pl.multiple_of(8 * (32 * pair + c), 8), 8)
                    second = pl.ds(pl.multiple_of(8 * (32 * pair + 16 + c), 8), 8)
                    a = work[first, lanes]
                    b = work[second, lanes]
                    to = slice(128 * pair, 128 * pair + 128)
                    send[c, piece, top, to] = jnp.where(left, a, pltpu.roll(b, 64, 1))
                    send[c, piece, low, to] = jnp.where(left, pltpu.roll(a, 64, 1), b)

        mine = pl.ds(pl.multiple_of(col * 32 + part * 16, 16), 16)
        for i, j, k in FAR_COLS:
            tc = lax.rem(y + i, 4) * 4 + lax.rem(xl + j, 2) * 2 + lax.rem(core + k, 2)
            pack(tc)
            pltpu.make_async_remote_copy(
                send.at[tc, :, lines], out.at[:, mine],
                send_sem.at[2], recv_col.at[part], device_id=(row, tc), device_id_type=MESH,
            ).start()
        pack(col)
        pltpu.make_async_copy(send.at[col, :, lines], out.at[:, mine], own_sem.at[part]).start()

    for part in range(2):
        settle(send.at[:15, :, :16], recv_col.at[part])
        settle(send.at[0, :, :16], own_sem.at[part])
    settle(got.at[:7], send_sem.at[0])
    settle(have.at[:127], send_sem.at[1])
    settle(send.at[:15], send_sem.at[2])


def field_step(z_hi, z_lo, r_hi, r_lo):
    r_rows, r_mats = row_tables()
    c_rows, c_mats, _ = col_tables()
    return pl.pallas_call(
        field_body,
        out_shape=jax.ShapeDtypeStruct((2, STRIDE, STRIDE), F32),
        in_specs=[vmem()] * 8,
        out_specs=vmem(),
        scratch_shapes=[
            pltpu.VMEM((TILE, 2 * TILE), F32),
            pltpu.VMEM((OVL, 2 * TILE), F32),
            pltpu.VMEM((OVL, 2 * TILE), F32),
            pltpu.VMEM((8, 64, 2 * TILE), F32),
            pltpu.VMEM((1024, 256), F32),
            pltpu.VMEM((32, 2, 64, 128), F32),
            pltpu.VMEM((128, 32, 128), F32),
            pltpu.VMEM((128, 32, 128), F32),
            pltpu.VMEM((16, 2, 32, STRIDE), F32),
            pltpu.SemaphoreType.DMA((2,)),
            pltpu.SemaphoreType.DMA((3,)),
            pltpu.SemaphoreType.DMA((8,)),
            pltpu.SemaphoreType.DMA(()),
            pltpu.SemaphoreType.DMA((2,)),
            pltpu.SemaphoreType.DMA(()),
            pltpu.SemaphoreType.DMA((2,)),
            pltpu.SemaphoreType.DMA((2,)),
            pltpu.SemaphoreType.REGULAR,
        ],
        compiler_params=pltpu.CompilerParams(
            vmem_limit_bytes=B_LIMIT << 20, collective_id=0, has_side_effects=True
        ),
        name="field_step",
    )(z_hi, z_lo, r_hi, r_lo, r_rows, r_mats, c_rows, c_mats)


def local(tiles, pupils, intensity, offsets):
    return field_step(*tile_step(tiles, pupils, intensity, offsets[0, 0]))


def solution(mesh):
    placed = (
        P(None, "row", "col"),
        P(None, "row", "col"),
        P(None, "row", "col"),
        P("row", "col", None, None),
    )
    return jax.shard_map(
        local, mesh=mesh, in_specs=placed, out_specs=P(None, "row", "col"), check_vma=False
    )
```

```python
import math

import numpy as np
import ml_dtypes
import jax
import jax.numpy as jnp
from jax import lax
from jax.experimental import pallas as pl
from jax.experimental.pallas import tpu as pltpu
from jax.sharding import PartitionSpec as P

TILE = 576
PAD = 640
OVL = 64
WIN = 128
LEDS = 16
STRIDE = 512
ROWS = 4096
COLS = 8192
FRESNEL = 2048
STEP_SIZE = 0.05
RADIX = 6
SUB = TILE // RADIX
BF = jnp.bfloat16
F32 = jnp.float32
GROUP = 8
A_LIMIT = 38
B_LIMIT = 24


def split_np(table):
    table = np.asarray(table, np.float64)
    high = table.astype(np.float32).astype(ml_dtypes.bfloat16)
    low = (table - high.astype(np.float64)).astype(np.float32).astype(ml_dtypes.bfloat16)
    return high, low


def unit(turns):
    turns = np.asarray(turns, np.float64)
    return np.exp(2j * np.pi * (turns - np.floor(turns)))


def right_block(table):
    return np.block([[table.real, table.imag], [-table.imag, table.real]])


def left_block(table):
    return np.block([[table.real, -table.imag], [table.imag, table.real]])


def dft_np(length, sign):
    index = np.arange(length)
    return unit(sign * (index[:, None] * index[None, :] % length) / length)


def axis_filter(length):
    freq = np.arange(length)
    signed = np.where(freq < length // 2, freq, freq - length).astype(np.float64)
    turns = signed * signed * (FRESNEL / (length * length))
    return np.exp(-2.0 * signed * signed / (length * length)) * unit(-turns) / length


def split(value):
    high = value.astype(BF)
    low = (value - high.astype(F32)).astype(BF)
    return high, low


def mm(left, right):
    return jnp.dot(left, right, preferred_element_type=F32)


def mm3(left, right):
    return mm(left[0], right[0]) + (mm(left[1], right[0]) + mm(left[0], right[1]))


def mm_nt(left, right):
    return lax.dot_general(left, right, (((1,), (1,)), ((), ())), preferred_element_type=F32)


def cmul(ar, ai, br, bi):
    return ar * br - ai * bi, ar * bi + ai * br


def cscale(value, factor):
    re, im = value
    fr, fi = float(factor.real), float(factor.imag)
    near = 1e-12
    if abs(fi) < near:
        if abs(fr - 1) < near:
            return re, im
        if abs(fr + 1) < near:
            return -re, -im
    if abs(fr) < near:
        if abs(fi - 1) < near:
            return -im, re
        if abs(fi + 1) < near:
            return im, -re
    if abs(abs(fr) - abs(fi)) < near:
        size = abs(fr)
        sr, si = math.copysign(1, fr), math.copysign(1, fi)
        left = re if sr > 0 else -re
        low = im if sr > 0 else -im
        new_re = left - im if si > 0 else left + im
        new_im = low + re if si > 0 else low - re
        return new_re * size, new_im * size
    return re * fr - im * fi, re * fi + im * fr


def fft_list(items, sign):
    count = len(items)
    if count == 1:
        return items
    if count == 3:
        (ar, ai), (br, bi), (cr, ci) = items
        sr, si, dr, di = br + cr, bi + ci, br - cr, bi - ci
        mr, mi = ar - 0.5 * sr, ai - 0.5 * si
        root = sign * math.sqrt(0.75)
        tr, ti = -root * di, root * dr
        return [(ar + sr, ai + si), (mr + tr, mi + ti), (mr - tr, mi - ti)]
    even = fft_list(items[0::2], sign)
    odd = fft_list(items[1::2], sign)
    half = count // 2
    first, second = [], []
    for index in range(half):
        turned = cscale(odd[index], unit(sign * index / count))
        er, ei = even[index]
        first.append((er + turned[0], ei + turned[1]))
        second.append((er - turned[0], ei - turned[1]))
    return first + second


def tile_tables():
    index = np.arange(TILE)
    low = unit(-(np.arange(24)[:, None] * index[None, :] % TILE) / TILE) / math.sqrt(TILE)
    high = unit(-(24 * np.arange(24)[:, None] * index[None, :] % TILE) / TILE)
    seeds = np.zeros((4, 24, PAD), np.float32)
    seeds[0, :, :TILE], seeds[1, :, :TILE] = low.real, low.imag
    seeds[2, :, :TILE], seeds[3, :, :TILE] = high.real, high.imag
    small = np.arange(SUB)
    forward, inverse = [], []
    for part in range(RADIX):
        turned = unit(-(part * small[:, None] + RADIX * small[:, None] * small[None, :]) / TILE)
        turned = turned / math.sqrt(TILE)
        forward.append(left_block(turned))
        inverse.append(left_block(np.conj(turned.T)))
    forward = np.stack(split_np(np.stack(forward)))
    inverse = np.stack(split_np(np.stack(inverse)))
    window = dft_np(WIN, -1) / math.sqrt(WIN)
    lanes = np.stack(split_np(right_block(np.conj(window))))
    sides = np.stack(
        [*split_np(left_block(np.conj(window))), *split_np(left_block(window))]
    )
    return seeds, forward, inverse, lanes, sides


def cut(ref, part, row, first, back):
    base = pl.multiple_of((row // 8) * 8, 8)
    down = row - base
    wide = ref[part, pl.ds(base, WIN + 8), pl.ds(first, 256)]
    wide = pltpu.roll(wide, back, 1)[:, :WIN].reshape(WIN // 8 + 1, 8, WIN)
    wide = pltpu.roll(wide, lax.rem(8 - down, 8), 1)
    lane = lax.broadcasted_iota(jnp.int32, (WIN // 8, 8, WIN), 1)
    return jnp.where(lane < 8 - down, wide[:-1], wide[1:]).reshape(WIN, WIN)


def add(ref, part, row, first, shift, value):
    base = pl.multiple_of((row // 8) * 8, 8)
    down = row - base
    turned = pltpu.roll(value.reshape(WIN // 8, 8, WIN), down, 1)
    zero = jnp.zeros((1, 8, WIN), F32)
    lane = lax.broadcasted_iota(jnp.int32, (WIN // 8 + 1, 8, WIN), 1)
    upper = jnp.concatenate([zero, turned], axis=0)
    lower = jnp.concatenate([turned, zero], axis=0)
    tall = jnp.where(lane < down, upper, lower).reshape(WIN + 8, WIN)
    wide = jnp.concatenate([tall, jnp.zeros((WIN + 8, 128), F32)], axis=1)
    here = (part, pl.ds(base, WIN + 8), pl.ds(first, 256))
    ref[here] = ref[here] + pltpu.roll(wide, shift, 1)


def tile_body(
    offs, tiles_in, pupils_in, intensity_in, seeds_in, fwd_in, inv_in, lanes_in, sides_in,
    z_hi, z_lo, r_hi, r_lo,
    base, y, sub, spec, wins_a, wins_b, turned,
    tiles, raw, pupils, intensity, seeds, fwd, inv, lanes, sides, sems,
):
    pairs = [(seeds_in, seeds), (tiles_in, raw), (fwd_in, fwd)]
    pairs += [(pupils_in, pupils), (intensity_in, intensity)]
    pairs += [(lanes_in, lanes), (sides_in, sides), (inv_in, inv)]
    loads = [
        pltpu.make_async_copy(source, target, sems.at[index])
        for index, (source, target) in enumerate(pairs)
    ]
    for load in loads:
        load.start()
    loads[0].wait()

    low_r, low_i = seeds[0], seeds[1]

    @pl.loop(0, 24)
    def _(a):
        hr = seeds[2, pl.ds(a, 1), :]
        hi = seeds[3, pl.ds(a, 1), :]
        tr, ti = cmul(low_r, low_i, hr, hi)
        start = pl.multiple_of(a * 24, 8)
        base[0, pl.ds(start, 24), :] = tr
        base[1, pl.ds(start, 24), :] = ti

    for ref in (r_hi, r_lo):
        zero_tail = jnp.zeros((PAD - TILE, 2 * TILE), BF)
        ref[TILE:PAD, :] = zero_tail
        ref[PAD + TILE :, :] = zero_tail

    @pl.loop(0, TILE // 96)
    def _(a):
        start = pl.multiple_of(a * 96, 16)
        re, im = base[0, pl.ds(start, 96), :], base[1, pl.ds(start, 96), :]
        for offset, left, right in ((0, re, -im), (PAD, im, re)):
            at = pl.ds(start + offset, 96)
            ends = left[:, STRIDE:] + pltpu.roll(right[:, STRIDE:], 64, 1)
            for where, value in (
                (slice(0, STRIDE), left[:, :STRIDE]),
                (slice(STRIDE, 2 * STRIDE), right[:, :STRIDE]),
                (slice(2 * STRIDE, 2 * TILE), ends),
            ):
                high, low = split(value)
                r_hi[at, where] = high
                r_lo[at, where] = low

    def forward():
        @pl.loop(0, RADIX)
        def _(b):
            rows = pl.ds(b, SUB, stride=RADIX)
            parts = [
                jnp.concatenate([tiles[part, n, rows, :] for n in range(5)], axis=1)
                for part in range(2)
            ]
            sub[b] = mm3((fwd[0, b], fwd[1, b]), split(jnp.concatenate(parts, axis=0)))

        @pl.loop(0, PAD // 128)
        def _(n):
            at = pl.ds(pl.multiple_of(n * 128, 128), 128)
            for row in range(0, SUB, 8):
                items = [
                    (sub[b, row : row + 8, at], sub[b, SUB + row : SUB + row + 8, at])
                    for b in range(RADIX)
                ]
                done = fft_list(items, -1)
                for k in range(RADIX):
                    here = slice(k * SUB + row, k * SUB + row + 8)
                    spec[0, here, at] = done[k][0]
                    spec[1, here, at] = done[k][1]

    loads[1].wait()
    for part in range(2):
        for n in range(5):
            width = min(128, TILE - 128 * n)
            tiles[part, n, :, :width] = raw[part, :, 128 * n : 128 * n + width]
    loads[2].wait()
    forward()

    def flip(part, at, count, to):
        for i in range(4):
            block = jnp.transpose(spec[part, 128 * i : 128 * i + 128, at])
            tiles[part, i, to, :] = block[:count]
        half = jnp.concatenate([spec[part, STRIDE:TILE, at], jnp.zeros((64, 128), F32)], axis=0)
        tiles[part, 4, to, :] = jnp.transpose(half)[:count]

    for part in range(2):
        @pl.loop(0, 4)
        def _(j):
            at = pl.ds(pl.multiple_of(j * 128, 128), 128)
            flip(part, at, 128, at)

        flip(part, slice(STRIDE, PAD), 64, slice(STRIDE, TILE))

    forward()

    for part in range(2):
        spec[part, TILE:, :] = jnp.zeros((8, PAD), F32)
    for load in loads[3:]:
        load.wait()
    for part in range(2):
        turned[part] = jnp.transpose(pupils[part])
    inv_lanes = (lanes[0], lanes[1])
    inv_sides = (sides[0], sides[1])
    fwd_sides = (sides[2], sides[3])

    def sides_nt(table, value):
        high, low = split(value)
        return mm_nt(table[0], high) + (mm_nt(table[1], high) + mm_nt(table[0], low))

    def restack(win_b, value):
        for j in range(GROUP):
            win_b[j * WIN : (j + 1) * WIN, :WIN] = value[:WIN, j * WIN : (j + 1) * WIN]
            win_b[j * WIN : (j + 1) * WIN, WIN:] = value[WIN:, j * WIN : (j + 1) * WIN]

    pr, pi = turned[0], turned[1]
    for step in range(LEDS // GROUP):
        win_b = wins_b.at[step]
        for j in range(GROUP):
            led = step * GROUP + j
            row, col = offs[1, led], offs[0, led]
            first = pl.multiple_of((col // 128) * 128, 128)
            back = lax.rem(first + 256 - col, 256)
            cr = cut(spec, 0, row, first, back)
            ci = cut(spec, 1, row, first, back)
            wr, wi = cmul(pr, pi, cr, ci)
            win_b[j * WIN : (j + 1) * WIN, :WIN] = wr
            win_b[j * WIN : (j + 1) * WIN, WIN:] = wi

    for step in range(LEDS // GROUP):
        win_a, win_b = wins_a.at[step], wins_b.at[step]
        pr, pi = turned[0], turned[1]
        restack(win_b, sides_nt(inv_sides, win_b[...]))
        wave = mm3(split(win_b[...]), inv_lanes)
        for j in range(GROUP):
            wr = wave[j * WIN : (j + 1) * WIN, :WIN]
            wi = wave[j * WIN : (j + 1) * WIN, WIN:]
            excess = wr * wr + wi * wi - intensity[step * GROUP + j]
            win_a[:WIN, j * WIN : (j + 1) * WIN] = wr * excess
            win_a[WIN:, j * WIN : (j + 1) * WIN] = wi * excess
        restack(win_b, mm3(fwd_sides, split(win_a[...])))
        win_a[...] = sides_nt(fwd_sides, win_b[...])
        for j in range(GROUP):
            led = step * GROUP + j
            row, col = offs[1, led], offs[0, led]
            first = pl.multiple_of((col // 128) * 128, 128)
            shift = col - first
            gr = win_a[:WIN, j * WIN : (j + 1) * WIN] * -STEP_SIZE
            gi = win_a[WIN:, j * WIN : (j + 1) * WIN] * -STEP_SIZE
            ur, ui = cmul(pr, -pi, gr, gi)
            add(spec, 0, row, first, shift, ur)
            add(spec, 1, row, first, shift, ui)

    @pl.loop(0, PAD // 128)
    def _(n):
        at = pl.ds(pl.multiple_of(n * 128, 128), 128)
        for row in range(0, SUB, 8):
            items = []
            for k in range(RADIX):
                here = slice(k * SUB + row, k * SUB + row + 8)
                items.append((spec[0, here, at], spec[1, here, at]))
            done = fft_list(items, 1)
            for b in range(RADIX):
                sub[b, row : row + 8, at] = done[b][0]
                sub[b, SUB + row : SUB + row + 8, at] = done[b][1]

    @pl.loop(0, RADIX)
    def _(b):
        mixed = mm3((inv[0, b], inv[1, b]), split(sub[b]))
        rows = pl.ds(b, SUB, stride=RADIX)
        for n in range(5):
            y[n, rows, :] = mixed[:SUB, 128 * n : 128 * n + 128]
            y[5 + n, rows, :] = mixed[SUB:, 128 * n : 128 * n + 128]

    for n in range(10):
        at = slice(128 * n, 128 * n + 128)
        high, low = split(y[n])
        z_hi[:, at] = high
        z_lo[:, at] = low


def vmem():
    return pl.BlockSpec(memory_space=pltpu.VMEM)


def tile_step(tiles, pupils, intensity, offsets):
    seeds, fwd, inv, lanes, sides = tile_tables()
    held = (pupils, intensity, seeds, fwd, inv, lanes, sides)
    return pl.pallas_call(
        tile_body,
        out_shape=[
            jax.ShapeDtypeStruct((TILE, 2 * PAD), BF),
            jax.ShapeDtypeStruct((TILE, 2 * PAD), BF),
            jax.ShapeDtypeStruct((2 * PAD, 2 * TILE), BF),
            jax.ShapeDtypeStruct((2 * PAD, 2 * TILE), BF),
        ],
        in_specs=[pl.BlockSpec(memory_space=pltpu.SMEM)]
        + [pl.BlockSpec(memory_space=pltpu.HBM)] * 8,
        out_specs=[vmem()] * 4,
        scratch_shapes=[
            pltpu.VMEM((2, TILE, PAD), F32),
            pltpu.VMEM((2 * PAD // 128, TILE, 128), F32),
            pltpu.VMEM((RADIX, 2 * SUB, PAD), F32),
            pltpu.VMEM((2, TILE + 8, PAD), F32),
            pltpu.VMEM((LEDS // GROUP, 2 * WIN, GROUP * WIN), F32),
            pltpu.VMEM((LEDS // GROUP, GROUP * WIN, 2 * WIN), F32),
            pltpu.VMEM((2, WIN, WIN), F32),
            pltpu.VMEM((2, PAD // 128, TILE, 128), F32),
            pltpu.VMEM((2, TILE, TILE), F32),
            *[pltpu.VMEM(value.shape, value.dtype) for value in held],
            pltpu.SemaphoreType.DMA((8,)),
        ],
        compiler_params=pltpu.CompilerParams(vmem_limit_bytes=A_LIMIT << 20),
        name="tile_step",
    )(
        *[
            pltpu.with_memory_space_constraint(jnp.asarray(value), pltpu.HBM)
            for value in (offsets, tiles, *held)
        ]
    )


def row_tables():
    lane = np.arange(128)
    k1 = np.arange(32)
    turn = unit(-(k1[:, None] * lane[None, :]) / ROWS)
    keep = axis_filter(ROWS)[k1[:, None] + 32 * lane[None, :]]
    rows = np.stack([turn.real, turn.imag, keep.real, keep.imag]).astype(np.float32)
    full = dft_np(128, -1)
    mats = np.stack([*split_np(right_block(full)), *split_np(right_block(np.conj(full)))])
    return rows, mats


def col_tables():
    lane = np.arange(64)
    kc = np.arange(16)
    kr = np.arange(8)
    low = kc[None, :] + 16 * kr[:, None]
    turn = unit(-(low[:, :, None] * lane) / COLS)
    keep = axis_filter(COLS)[low[:, :, None] + 128 * lane]
    rows = np.stack([turn.real, turn.imag, keep.real, keep.imag]).reshape(4, 128, 64)
    rows = np.concatenate([rows, rows], axis=2).astype(np.float32)
    inner = unit(-(np.arange(8)[:, None] * kc[None, :]) / 128)
    full = np.kron(np.eye(2), dft_np(64, -1))
    mats = np.stack([*split_np(right_block(full)), *split_np(right_block(np.conj(full)))])
    return rows, mats, inner


MESH = pl.DeviceIdType.MESH
FAR_ROWS = ((1, 2), (1, 1), (1, 3), (0, 2), (1, 0), (0, 1), (0, 3))
FAR_COLS = sorted(
    ((y, x, k) for y in range(4) for x in range(2) for k in range(2) if y or x or k),
    key=lambda step: -(min(step[0], 4 - step[0]) + step[1]),
)
QUARTER = 8


def settle(ref, sem):
    pltpu.make_async_copy(ref, ref, sem).wait()


def field_body(
    z_hi, z_lo, r_hi, r_lo, r_rows, r_mats, c_rows, c_mats, out,
    refined, halo, front, got, work, mid, give, have, send,
    halo_sem, send_sem, recv_row, own_row, recv_all, own_all, recv_col, own_sem, ready,
):
    row, col = lax.axis_index("row"), lax.axis_index("col")
    xh, z = row // 4, lax.rem(row, 4)
    y, xl, core = col // 4, lax.rem(col // 2, 2), lax.rem(col, 2)
    rows_at = [lax.rem(row + step, 8) for step in range(8)]
    cols_at = [lax.rem(col + step, 16) for step in range(16)]

    barrier = pltpu.get_barrier_semaphore()
    for i in range(1, 8):
        pl.semaphore_signal(barrier, inc=1, device_id=(rows_at[i], col), device_id_type=MESH)
    for j in range(1, 16):
        pl.semaphore_signal(barrier, inc=1, device_id=(row, cols_at[j]), device_id_type=MESH)

    chunks = [lax.rem(xh + i, 2) * 4 + lax.rem(z + j, 4) for i, j in FAR_ROWS]

    def columns_of(blocks):
        places = [pl.ds(pl.multiple_of(block * 64, 64), 64) for block in blocks]

        def fill(at):
            high = jnp.concatenate([z_hi[place, :] for place in places], axis=0)
            low = jnp.concatenate([z_lo[place, :] for place in places], axis=0)
            value = mm3((high, low), (r_hi[:, at], r_lo[:, at]))
            for index, place in enumerate(places):
                refined[place, at] = value[64 * index : 64 * index + 64]

        @pl.loop(0, 4)
        def _(n):
            fill(pl.ds(pl.multiple_of(n * 256, 256), 256))

        fill(slice(1024, 1152))

    columns_of([8, *chunks[:2]])
    pl.semaphore_wait(barrier, 22)
    for j in range(1, 16):
        pl.semaphore_signal(ready, inc=1, device_id=(row, cols_at[j]), device_id_type=MESH)

    edge = pltpu.make_async_remote_copy(
        refined.at[STRIDE:], halo, halo_sem.at[0], halo_sem.at[1],
        device_id=(row, cols_at[1]), device_id_type=MESH,
    )
    edge.start()

    def give_row(target, quarter, source):
        pltpu.make_async_remote_copy(
            source, got.at[row, quarter * QUARTER : (quarter + 1) * QUARTER],
            send_sem.at[0], recv_row.at[quarter], device_id=(target, col), device_id_type=MESH,
        ).start()

    def plain(target, quarter):
        start = pl.multiple_of(target * 64 + quarter * QUARTER, QUARTER)
        return refined.at[pl.ds(start, QUARTER)]

    def blended(quarter):
        return front.at[quarter * QUARTER : (quarter + 1) * QUARTER]

    def give_plain(targets, quarter=0):
        for target in targets:
            @pl.when(target != 0)
            def _():
                give_row(target, quarter, plain(target, quarter))

    def give_blended(quarter):
        for target in chunks:
            @pl.when(target == 0)
            def _():
                give_row(target, quarter, blended(quarter))

    give_plain(chunks[:2])
    columns_of(chunks[2:5])
    give_plain(chunks[2:5])
    columns_of([*chunks[5:], row])
    give_plain(chunks[5:])
    for quarter in range(1, 4):
        give_plain(chunks, quarter)

    edge.wait()
    place = lax.broadcasted_iota(jnp.int32, (OVL, 2 * TILE), 0).astype(F32)
    ramp = (place + 0.5) / OVL
    front[...] = ramp * refined[:OVL] + (1.0 - ramp) * halo[...]

    for quarter in range(4):
        give_blended(quarter)
    for quarter in range(4, 8):
        give_plain(chunks, quarter)
        give_blended(quarter)

    @pl.when(row == 0)
    def _():
        pltpu.make_async_copy(front, got.at[0], own_row).start()

    @pl.when(row != 0)
    def _():
        start = pl.multiple_of(row * 64, 64)
        pltpu.make_async_copy(refined.at[pl.ds(start, 64)], got.at[row], own_row).start()

    settle(front, own_row)

    lane = lax.broadcasted_iota(jnp.int32, (8, 128), 1)
    slope = jnp.where(lane < OVL, (lane.astype(F32) + 0.5) / OVL, 1.0)
    rest = jnp.where(lane < OVL, 1.0 - slope, 0.0)

    @pl.loop(0, 8)
    def _(quarter):
        columns = pl.ds(pl.multiple_of(quarter * QUARTER, QUARTER), QUARTER)
        settle(got.at[:7, columns], recv_row.at[quarter])

        at = pl.ds(pl.multiple_of(quarter * QUARTER, 8), 8)
        for a in range(4):
            items = []
            for p in range(8):
                re = got[p, at, 128 * a : 128 * a + 128]
                im = got[p, at, STRIDE + 128 * a : STRIDE + 128 * a + 128]
                if a == 0:
                    tail = got[(p - 1) % 8, at, 2 * STRIDE :]
                    re = slope * re + rest * tail
                    im = slope * im + rest * pltpu.roll(tail, 64, 1)
                items.append((re, im))
            done = fft_list(items, -1)
            for k in range(8):
                re, im = cscale(done[k], unit(-a * k / 32))
                mid[4 * k + a, 0, at, :] = re
                mid[4 * k + a, 1, at, :] = im

        for k in range(8):
            items = [(mid[4 * k + a, 0, at, :], mid[4 * k + a, 1, at, :]) for a in range(4)]
            done = fft_list(items, -1)
            for q in range(4):
                index = k + 8 * q
                tr = r_rows[0, index : index + 1, :]
                ti = r_rows[1, index : index + 1, :]
                re, im = cmul(*done[q], tr, ti)
                start = slice(index * QUARTER, index * QUARTER + 8)
                work[start, :128] = re
                work[start, 128:] = im

        full = mm3(split(work[:256]), (r_mats[0], r_mats[1]))
        full = full.reshape(32, QUARTER, 256)
        kr, ki = r_rows[2][:, None, :], r_rows[3][:, None, :]
        re, im = cmul(full[:, :, :128], full[:, :, 128:], kr, ki)
        both = jnp.concatenate([re, im], axis=2).reshape(256, 256)
        work[:256] = mm3(split(both), (r_mats[2], r_mats[3]))

        at = pl.ds(pl.multiple_of(quarter * QUARTER, 8), 8)

        for k in range(8):
            items = []
            for q in range(4):
                index = k + 8 * q
                tr = r_rows[0, index : index + 1, :]
                ti = r_rows[1, index : index + 1, :]
                start = slice(index * QUARTER, index * QUARTER + 8)
                items.append(cmul(work[start, :128], work[start, 128:], tr, -ti))
            done = fft_list(items, 1)
            for a in range(4):
                mid[4 * k + a, 0, at, :] = done[a][0]
                mid[4 * k + a, 1, at, :] = done[a][1]

        for a in range(4):
            items = [
                cscale((mid[4 * k + a, 0, at, :], mid[4 * k + a, 1, at, :]), unit(a * k / 32))
                for k in range(8)
            ]
            done = fft_list(items, 1)
            for p in range(8):
                mid[4 * p + a, 0, at, :] = done[p][0]
                mid[4 * p + a, 1, at, :] = done[p][1]

    me = row * 16 + col

    def peers(step):
        tr = lax.rem(xh + 1 + step // 16, 2) * 4 + lax.rem(z + 2 + (step // 4) % 4, 4)
        ty = lax.rem(y + 2 + step % 4, 4)
        ends = []
        for i in range(2):
            for j in range(2):
                ends.append((tr, ty * 4 + lax.rem(xl + i, 2) * 2 + lax.rem(core + j, 2)))
        return tr * 4 + ty, ends

    own_step = 26

    def give_all(step, ends, part):
        lines = slice(part * 16, part * 16 + 16)
        for index, (tr, tc) in enumerate(ends):
            def go(tr=tr, tc=tc):
                pltpu.make_async_remote_copy(
                    give.at[tr * 16 + tc, lines], have.at[me, lines],
                    send_sem.at[1], recv_all.at[part], device_id=(tr, tc), device_id_type=MESH,
                ).start()

            if index:
                go()
            else:
                pl.when(step != own_step)(go)

    pl.semaphore_wait(ready, 15)

    @pl.loop(0, 32)
    def _(step):
        block, ends = peers(step)
        flat = jnp.transpose(mid[block].reshape(128, 128))
        for i in range(4):
            give[block * 4 + i] = flat[32 * i : 32 * i + 32]
        give_all(step, ends, 0)

    own = pltpu.make_async_copy(give.at[me], have.at[me], own_all)
    own.start()

    @pl.loop(0, 32)
    def _(step):
        give_all(step, peers(step)[1], 1)

    own.wait()

    left = lane < 64
    inner = col_tables()[2]

    @pl.loop(0, 2)
    def _(part):
        lines = pl.ds(pl.multiple_of(part * 16, 16), 16)
        top = pl.ds(pl.multiple_of(part * 16, 8), 8)
        low = pl.ds(pl.multiple_of(part * 16 + 8, 8), 8)
        settle(have.at[:127, lines], recv_all.at[part])

        for r in range(8):
            items = []
            for c in range(16):
                a = have[16 * r + c, top, :]
                b = have[16 * r + c, low, :]
                re = jnp.where(left, a, pltpu.roll(b, 64, 1))
                im = jnp.where(left, pltpu.roll(a, 64, 1), b)
                items.append((re, im))
            done = fft_list(items, -1)
            for k in range(16):
                flat = 8 * (16 * r + k)
                re, im = cscale(done[k], inner[r, k])
                work[flat : flat + 8, :128] = re
                work[flat : flat + 8, 128:] = im

        for k in range(16):
            places = [slice(8 * (16 * r + k), 8 * (16 * r + k) + 8) for r in range(8)]
            items = [(work[at, :128], work[at, 128:]) for at in places]
            done = fft_list(items, -1)
            for q in range(8):
                tr = c_rows[0, 16 * q + k : 16 * q + k + 1, :]
                ti = c_rows[1, 16 * q + k : 16 * q + k + 1, :]
                re, im = cmul(*done[q], tr, ti)
                work[places[q], :128] = re
                work[places[q], 128:] = im

        @pl.loop(0, 2)
        def _(n):
            at = pl.ds(pl.multiple_of(n * 512, 512), 512)
            keep = pl.ds(pl.multiple_of(n * 64, 64), 64)
            full = mm3(split(work[at, :]), (c_mats[0], c_mats[1]))
            full = full.reshape(64, 8, 256)
            kr, ki = c_rows[2, keep, :][:, None, :], c_rows[3, keep, :][:, None, :]
            re, im = cmul(full[:, :, :128], full[:, :, 128:], kr, ki)
            both = jnp.concatenate([re, im], axis=2).reshape(512, 256)
            work[at, :] = mm3(split(both), (c_mats[2], c_mats[3]))

        for k in range(16):
            places = [slice(8 * (16 * r + k), 8 * (16 * r + k) + 8) for r in range(8)]
            items = []
            for q in range(8):
                tr = c_rows[0, 16 * q + k : 16 * q + k + 1, :]
                ti = c_rows[1, 16 * q + k : 16 * q + k + 1, :]
                items.append(cmul(work[places[q], :128], work[places[q], 128:], tr, -ti))
            done = fft_list(items, 1)
            for r in range(8):
                work[places[r], :128] = done[r][0]
                work[places[r], 128:] = done[r][1]

        for r in range(8):
            items = []
            for k in range(16):
                flat = 8 * (16 * r + k)
                value = (work[flat : flat + 8, :128], work[flat : flat + 8, 128:])
                items.append(cscale(value, np.conj(inner[r, k])))
            done = fft_list(items, 1)
            for c in range(16):
                flat = 8 * (16 * r + c)
                work[flat : flat + 8, :128] = done[c][0]
                work[flat : flat + 8, 128:] = done[c][1]

        def pack(c):
            for piece in range(2):
                lanes = slice(128 * piece, 128 * piece + 128)
                for pair in range(4):
                    first = pl.ds(pl.multiple_of(8 * (32 * pair + c), 8), 8)
                    second = pl.ds(pl.multiple_of(8 * (32 * pair + 16 + c), 8), 8)
                    a = work[first, lanes]
                    b = work[second, lanes]
                    to = slice(128 * pair, 128 * pair + 128)
                    send[c, piece, top, to] = jnp.where(left, a, pltpu.roll(b, 64, 1))
                    send[c, piece, low, to] = jnp.where(left, pltpu.roll(a, 64, 1), b)

        mine = pl.ds(pl.multiple_of(col * 32 + part * 16, 16), 16)
        for i, j, k in FAR_COLS:
            tc = lax.rem(y + i, 4) * 4 + lax.rem(xl + j, 2) * 2 + lax.rem(core + k, 2)
            pack(tc)
            pltpu.make_async_remote_copy(
                send.at[tc, :, lines], out.at[:, mine],
                send_sem.at[2], recv_col.at[part], device_id=(row, tc), device_id_type=MESH,
            ).start()
        pack(col)
        pltpu.make_async_copy(send.at[col, :, lines], out.at[:, mine], own_sem.at[part]).start()

    for part in range(2):
        settle(send.at[:15, :, :16], recv_col.at[part])
        settle(send.at[0, :, :16], own_sem.at[part])
    settle(got.at[:7], send_sem.at[0])
    settle(have.at[:127], send_sem.at[1])
    settle(send.at[:15], send_sem.at[2])


def field_step(z_hi, z_lo, r_hi, r_lo):
    r_rows, r_mats = row_tables()
    c_rows, c_mats, _ = col_tables()
    return pl.pallas_call(
        field_body,
        out_shape=jax.ShapeDtypeStruct((2, STRIDE, STRIDE), F32),
        in_specs=[vmem()] * 8,
        out_specs=vmem(),
        scratch_shapes=[
            pltpu.VMEM((TILE, 2 * TILE), F32),
            pltpu.VMEM((OVL, 2 * TILE), F32),
            pltpu.VMEM((OVL, 2 * TILE), F32),
            pltpu.VMEM((8, 64, 2 * TILE), F32),
            pltpu.VMEM((1024, 256), F32),
            pltpu.VMEM((32, 2, 64, 128), F32),
            pltpu.VMEM((128, 32, 128), F32),
            pltpu.VMEM((128, 32, 128), F32),
            pltpu.VMEM((16, 2, 32, STRIDE), F32),
            pltpu.SemaphoreType.DMA((2,)),
            pltpu.SemaphoreType.DMA((3,)),
            pltpu.SemaphoreType.DMA((8,)),
            pltpu.SemaphoreType.DMA(()),
            pltpu.SemaphoreType.DMA((2,)),
            pltpu.SemaphoreType.DMA(()),
            pltpu.SemaphoreType.DMA((2,)),
            pltpu.SemaphoreType.DMA((2,)),
            pltpu.SemaphoreType.REGULAR,
        ],
        compiler_params=pltpu.CompilerParams(
            vmem_limit_bytes=B_LIMIT << 20, collective_id=0, has_side_effects=True
        ),
        name="field_step",
    )(z_hi, z_lo, r_hi, r_lo, r_rows, r_mats, c_rows, c_mats)


def local(tiles, pupils, intensity, offsets):
    return field_step(*tile_step(tiles, pupils, intensity, offsets[0, 0]))


def solution(mesh):
    placed = (
        P(None, "row", "col"),
        P(None, "row", "col"),
        P(None, "row", "col"),
        P("row", "col", None, None),
    )
    return jax.shard_map(
        local, mesh=mesh, in_specs=placed, out_specs=P(None, "row", "col"), check_vma=False
    )
```
